32 devices in a mesh: dp: 8 (over z, x), mp: 4 (over y, core).
Axes of the slice: x: 2, y: 2, z: 4, core: 2. Of those that a mesh axis runs over, the one named last changes fastest.
Arguments:
- hidden: bfloat16 [16, 448, 768], P('dp'), may hold values from -6 to 6
- encoder: bfloat16 [16, 1500, 768], P('dp'), may hold values from -6 to 6
- lengths: int32 [16], P('dp'), may hold values from 1 to 448, as said below
- tasks: int32 [16], P('dp'), may hold values from 0 to 2, as said below
- frames: int32 [16], P('dp'), may hold values from 750 to 1500, as said below
- out_grad: bfloat16 [16, 448, 768], P('dp'), may hold values from -6 to 6
- gain_self: bfloat16 [768], replicated, may hold values from 0.099609375 to 1.8984375
- shift_self: bfloat16 [768], replicated, may hold values from -1.75 to 1.75
- query_self: bfloat16 [768, 768], P(None, 'mp'), may hold values from -0.21875 to 0.21875
- qbias_self: bfloat16 [768], P('mp'), may hold values from -3 to 3
- key_self: bfloat16 [768, 768], P(None, 'mp'), may hold values from -0.21875 to 0.21875
- value_self: bfloat16 [768, 768], P(None, 'mp'), may hold values from -0.21875 to 0.21875
- vbias_self: bfloat16 [768], P('mp'), may hold values from -1.75 to 1.75
- output_self: bfloat16 [768, 768], P('mp'), may hold values from -0.875 to 0.875
- obias_self: bfloat16 [768], replicated, may hold values from -1.75 to 1.75
- gain_cross: bfloat16 [768], replicated, may hold values from 0.099609375 to 1.8984375
- shift_cross: bfloat16 [768], replicated, may hold values from -1.75 to 1.75
- query_cross: bfloat16 [768, 768], P(None, 'mp'), may hold values from -0.21875 to 0.21875
- qbias_cross: bfloat16 [768], P('mp'), may hold values from -3 to 3
- key_cross: bfloat16 [768, 768], P(None, 'mp'), may hold values from -0.21875 to 0.21875
- value_cross: bfloat16 [768, 768], P(None, 'mp'), may hold values from -0.21875 to 0.21875
- vbias_cross: bfloat16 [768], P('mp'), may hold values from -1.75 to 1.75
- output_cross: bfloat16 [768, 768], P('mp'), may hold values from -0.875 to 0.875
- obias_cross: bfloat16 [768], replicated, may hold values from -1.75 to 1.75
- gain_feed: bfloat16 [768], replicated, may hold values from 0.099609375 to 1.8984375
- shift_feed: bfloat16 [768], replicated, may hold values from -1.75 to 1.75
- expand_weight: bfloat16 [768, 3072], P(None, 'mp'), may hold values from -0.21875 to 0.21875
- expand_bias: bfloat16 [3072], P('mp'), may hold values from -1.75 to 1.75
- contract_weight: bfloat16 [3072, 768], P('mp'), may hold values from -0.15625 to 0.15625
- contract_bias: bfloat16 [768], replicated, may hold values from -1.75 to 1.75
Outputs:
- block_out: bfloat16 [16, 448, 768], P('dp')
- hidden_grad: float32 [16, 448, 768], P('dp')
- encoder_grad: float32 [16, 1500, 768], P('dp', None, 'mp')
- gain_self_grad: float32 [768], replicated
- shift_self_grad: float32 [768], replicated
- query_self_grad: float32 [768, 768], P(None, 'mp')
- qbias_self_grad: float32 [768], P('mp')
- key_self_grad: float32 [768, 768], P(None, 'mp')
- value_self_grad: float32 [768, 768], P(None, 'mp')
- vbias_self_grad: float32 [768], P('mp')
- output_self_grad: float32 [768, 768], P('mp')
- obias_self_grad: float32 [768], replicated
- gain_cross_grad: float32 [768], replicated
- shift_cross_grad: float32 [768], replicated
- query_cross_grad: float32 [768, 768], P(None, 'mp')
- qbias_cross_grad: float32 [768], P('mp')
- key_cross_grad: float32 [768, 768], P(None, 'mp')
- value_cross_grad: float32 [768, 768], P(None, 'mp')
- vbias_cross_grad: float32 [768], P('mp')
- output_cross_grad: float32 [768, 768], P('mp')
- obias_cross_grad: float32 [768], replicated
- gain_feed_grad: float32 [768], replicated
- shift_feed_grad: float32 [768], replicated
- expand_weight_grad: float32 [768, 3072], P(None, 'mp')
- expand_bias_grad: float32 [3072], P('mp')
- contract_weight_grad: float32 [3072, 768], P('mp')
- contract_bias_grad: float32 [768], replicated
The draws below stay inside these ranges and needn't reach their ends.
Inputs may be any that keep to these rules, and one draw needn't show every extreme that they name: `tasks`: 0 transcription, 1 translation, 2 language identification. `lengths`: an item of task 2 has at most min(8, 112) tokens, any other item 448 // 2 or more; some item has 448. `frames`: some item has 1500.
All inputs are finite; a program needn't handle non-finite values.
Results may differ from the reference program's by a relative error of at most 0.035.
Values may be sent and summed in bfloat16 or wider, within the bound.
No kernel may reach another device: no remote copies, remote signals or barrier semaphores. Data moves between devices by JAX's collectives and lax.ppermute only.
A program may use at most 192 MiB of HBM per device.

```python
import jax
import jax.numpy as jnp
from jax import lax

D = 768
HEAD = 64
FF = 3072
L = 448
ENC = 1500
ITEMS = 16
N_MP = 4


def draw_plan(key):
    base = jax.random.fold_in(key, 17)
    rolled = jax.random.randint(jax.random.fold_in(base, 1), (ITEMS,), 0, 10)
    task_ids = jnp.where(rolled < 5, 0, jnp.where(rolled < 8, 1, 2)).astype(jnp.int32)
    task_ids = task_ids.at[0].set(0)
    long_len = jax.random.randint(jax.random.fold_in(base, 2), (ITEMS,), L // 2, L + 1)
    short_len = jax.random.randint(jax.random.fold_in(base, 3), (ITEMS,), 1, min(8, L // 4) + 1)
    counts = jnp.where(task_ids == 2, short_len, long_len).astype(jnp.int32)
    counts = counts.at[0].set(L)
    return (task_ids, counts)


def draw_tasks(key, part):
    return draw_plan(key)[0]


def draw_lengths(key, part):
    return draw_plan(key)[1]


def draw_frames(key, part):
    counts = jax.random.randint(jax.random.fold_in(key, 29), (ITEMS,), ENC // 2, ENC + 1).astype(jnp.int32)
    return counts.at[0].set(ENC)


def shard_levels(rng, shape, shards, smallest, top_value):
    factor_of, own = 1.0, jax.random.fold_in(rng, 6)
    for axis_at, blocks in shards:
        steps = jnp.exp(jax.random.uniform(jax.random.fold_in(own, axis_at), (blocks,), jnp.float32, smallest / len(shards), top_value / len(shards)))
        factor_of = factor_of * jnp.repeat(steps, shape[axis_at] // blocks).reshape([-1 if axis == axis_at else 1 for axis in range(len(shape))])
    return factor_of


def noise(rng, dims, scale, reach, split=(), dtype=jnp.bfloat16):
    values = scale * jax.random.normal(rng, dims, jnp.float32)
    if split:
        values = values * shard_levels(rng, dims, split, -0.22, 0.18)
    return jnp.clip(values, -reach, reach).astype(dtype)


def setup_inputs(seed: int = 0) -> dict:
    arg_keys = jax.random.split(jax.random.key(seed), 31)
    hidden = noise(arg_keys[0], (ITEMS, L, D), 1.0, 6.0, ((0, 8),))
    encoder = noise(arg_keys[1], (ITEMS, ENC, D), 1.0, 6.0, ((0, 8),))
    lengths = draw_lengths(jax.random.fold_in(arg_keys[30], 71), 0)
    tasks = draw_tasks(jax.random.fold_in(arg_keys[30], 71), 0)
    frames = draw_frames(jax.random.fold_in(arg_keys[30], 71), 0)
    out_grad = noise(arg_keys[5], (ITEMS, L, D), 1.0, 6.0, ((0, 8),))
    gain_self = jnp.clip(1.0 + 0.18 * jax.random.normal(arg_keys[6], (D,), jnp.float32), 0.099609375, 1.8984375).astype(jnp.bfloat16)
    shift_self = noise(arg_keys[7], (D,), 0.3, 1.75)
    query_self = noise(arg_keys[8], (D, D), D ** -0.5, 0.21875, ((1, 4),))
    qbias_self = noise(arg_keys[9], (D,), 0.5, 3.0, ((0, 4),))
    key_self = noise(arg_keys[10], (D, D), D ** -0.5, 0.21875, ((1, 4),))
    value_self = noise(arg_keys[11], (D, D), D ** -0.5, 0.21875, ((1, 4),))
    vbias_self = noise(arg_keys[12], (D,), 0.3, 1.75, ((0, 4),))
    output_self = noise(arg_keys[13], (D, D), (D // 16) ** -0.5, 0.875, ((0, 4),))
    obias_self = noise(arg_keys[14], (D,), 0.3, 1.75)
    gain_cross = jnp.clip(1.0 + 0.18 * jax.random.normal(arg_keys[15], (D,), jnp.float32), 0.099609375, 1.8984375).astype(jnp.bfloat16)
    shift_cross = noise(arg_keys[16], (D,), 0.3, 1.75)
    query_cross = noise(arg_keys[17], (D, D), D ** -0.5, 0.21875, ((1, 4),))
    qbias_cross = noise(arg_keys[18], (D,), 0.5, 3.0, ((0, 4),))
    key_cross = noise(arg_keys[19], (D, D), D ** -0.5, 0.21875, ((1, 4),))
    value_cross = noise(arg_keys[20], (D, D), D ** -0.5, 0.21875, ((1, 4),))
    vbias_cross = noise(arg_keys[21], (D,), 0.3, 1.75, ((0, 4),))
    output_cross = noise(arg_keys[22], (D, D), (D // 16) ** -0.5, 0.875, ((0, 4),))
    obias_cross = noise(arg_keys[23], (D,), 0.3, 1.75)
    gain_feed = jnp.clip(1.0 + 0.18 * jax.random.normal(arg_keys[24], (D,), jnp.float32), 0.099609375, 1.8984375).astype(jnp.bfloat16)
    shift_feed = noise(arg_keys[25], (D,), 0.3, 1.75)
    expand_weight = noise(arg_keys[26], (D, FF), D ** -0.5, 0.21875, ((1, 4),))
    expand_bias = noise(arg_keys[27], (FF,), 0.3, 1.75, ((0, 4),))
    contract_weight = noise(arg_keys[28], (FF, D), (FF // 2) ** -0.5, 0.15625, ((0, 4),))
    contract_bias = noise(arg_keys[29], (D,), 0.3, 1.75)
    return dict(hidden=hidden, encoder=encoder, lengths=lengths, tasks=tasks, frames=frames, out_grad=out_grad, gain_self=gain_self, shift_self=shift_self, query_self=query_self, qbias_self=qbias_self, key_self=key_self, value_self=value_self, vbias_self=vbias_self, output_self=output_self, obias_self=obias_self, gain_cross=gain_cross, shift_cross=shift_cross, query_cross=query_cross, qbias_cross=qbias_cross, key_cross=key_cross, value_cross=value_cross, vbias_cross=vbias_cross, output_cross=output_cross, obias_cross=obias_cross, gain_feed=gain_feed, shift_feed=shift_feed, expand_weight=expand_weight, expand_bias=expand_bias, contract_weight=contract_weight, contract_bias=contract_bias)


@jax.custom_vjp
def low(v):
    return lax.optimization_barrier(v.astype(jnp.bfloat16)).astype(jnp.float32)

@jax.custom_vjp
def low_back(v):
    return v

def low_keep(v):
    return (low(v), None)

def low_pass(kept, grad):
    return (grad,)

def back_keep(v):
    return (v, None)

def back_low(kept, grad):
    return (low(grad),)
low.defvjp(low_keep, low_pass)
low_back.defvjp(back_keep, back_low)
highest = lax.Precision.HIGHEST
epsilon = 1e-05

def matmul(operand, weight):
    return jnp.dot(operand, weight, precision=highest, preferred_element_type=jnp.float32)

def layer_norm(values, norm_gain, norm_shift):
    centred = values - lax.optimization_barrier(jnp.mean(values, axis=-1, keepdims=True))
    spread = lax.optimization_barrier(jnp.mean(centred * centred, axis=-1, keepdims=True))
    return centred * lax.rsqrt(spread + epsilon) * norm_gain + norm_shift

def grouped(operand, weight, groups):
    stride = operand.shape[-1] // groups
    summed = jnp.zeros((operand.shape[0], weight.shape[1]), jnp.float32)
    for member in range(groups):
        portion = matmul(operand[:, member * stride:(member + 1) * stride], weight[member * stride:(member + 1) * stride])
        summed = summed + low(portion)
    return summed

def attend(queries, key_rows, value_rows, allowed):
    split_q = queries.reshape(queries.shape[0], -1, HEAD)
    split_k = key_rows.reshape(key_rows.shape[0], -1, HEAD)
    split_v = value_rows.reshape(value_rows.shape[0], -1, HEAD)
    scores = low_back(jnp.einsum('qhe,khe->hqk', split_q, split_k, precision=highest) * HEAD ** (-0.5))
    scores = jnp.where(allowed[None], scores, -1e+30)
    largest = lax.optimization_barrier(jnp.max(scores, axis=-1, keepdims=True))
    powers = jnp.exp(scores - largest)
    shares = low(powers / lax.optimization_barrier(jnp.sum(powers, axis=-1, keepdims=True)))
    mixture = jnp.einsum('hqk,khe->qhe', shares, split_v, precision=highest)
    return mixture.reshape(queries.shape[0], -1)

def item_forward(params, row_block, mem_block, length, count):
    gain_self, shift_self, query_self, qbias_self, key_self, value_self, vbias_self, output_self, obias_self, gain_cross, shift_cross, query_cross, qbias_cross, key_cross, value_cross, vbias_cross, output_cross, obias_cross, gain_feed, shift_feed, expand_weight, expand_bias, contract_weight, contract_bias = params
    places = jnp.arange(L)
    causal = (places[None, :] <= places[:, None]) & (places[None, :] < length)
    heard = (jnp.arange(ENC) < count)[None, :]
    normed = low(layer_norm(row_block, gain_self, shift_self))
    queries = low_back(low(matmul(normed, query_self) + qbias_self))
    key_rows = low_back(low(matmul(normed, key_self)))
    value_rows = low_back(low(matmul(normed, value_self) + vbias_self))
    mixture = low_back(low(attend(queries, key_rows, value_rows, causal)))
    after_self = row_block + low_back(grouped(mixture, output_self, N_MP)) + obias_self
    normed_two = low(layer_norm(after_self, gain_cross, shift_cross))
    cross_q = low_back(low(matmul(normed_two, query_cross) + qbias_cross))
    cross_k = low_back(low(matmul(mem_block, key_cross)))
    cross_v = low_back(low(matmul(mem_block, value_cross) + vbias_cross))
    cross_mix = low_back(low(attend(cross_q, cross_k, cross_v, heard)))
    after_cross = after_self + low_back(grouped(cross_mix, output_cross, N_MP)) + obias_cross
    normed_three = low(layer_norm(after_cross, gain_feed, shift_feed))
    before_act = low_back(matmul(normed_three, expand_weight) + expand_bias)
    activated = low(jax.nn.gelu(before_act, approximate=False))
    return after_cross + low_back(grouped(activated, contract_weight, N_MP)) + contract_bias

def reference(hidden, encoder, lengths, tasks, frames, out_grad, gain_self, shift_self, query_self, qbias_self, key_self, value_self, vbias_self, output_self, obias_self, gain_cross, shift_cross, query_cross, qbias_cross, key_cross, value_cross, vbias_cross, output_cross, obias_cross, gain_feed, shift_feed, expand_weight, expand_bias, contract_weight, contract_bias):
    params = tuple((weight.astype(jnp.float32) for weight in (gain_self, shift_self, query_self, qbias_self, key_self, value_self, vbias_self, output_self, obias_self, gain_cross, shift_cross, query_cross, qbias_cross, key_cross, value_cross, vbias_cross, output_cross, obias_cross, gain_feed, shift_feed, expand_weight, expand_bias, contract_weight, contract_bias)))
    inputs = hidden.astype(jnp.float32)
    memory = encoder.astype(jnp.float32)

    def whole(weights, row_all, mem_all):

        def one_item(packed):
            return jax.checkpoint(item_forward)(weights, packed[0], packed[1], packed[2], packed[3])
        return lax.map(one_item, (row_all, mem_all, lengths, frames))
    outputs, pullback = jax.vjp(whole, params, inputs, memory)
    task_weight = jnp.where(tasks == 0, 1.0, jnp.where(tasks == 1, 0.6, 2.0)).astype(jnp.float32)
    valid = jnp.arange(L)[None, :] < lengths[:, None]
    upstream = out_grad.astype(jnp.float32) * jnp.where(valid, task_weight[:, None], 0.0).astype(jnp.float32)[:, :, None]
    param_grads, hidden_grad, encoder_grad = pullback(upstream)
    return (outputs.astype(jnp.bfloat16), hidden_grad, encoder_grad, param_grads[0], param_grads[1], param_grads[2], param_grads[3], param_grads[4], param_grads[5], param_grads[6], param_grads[7], param_grads[8], param_grads[9], param_grads[10], param_grads[11], param_grads[12], param_grads[13], param_grads[14], param_grads[15], param_grads[16], param_grads[17], param_grads[18], param_grads[19], param_grads[20], param_grads[21], param_grads[22], param_grads[23])
```

```python
import functools
import math

import jax
import jax.numpy as jnp
from jax import lax
from jax.experimental import pallas as pl
from jax.experimental.pallas import tpu as pltpu
from jax.sharding import PartitionSpec as P

HEAD = 64
AUG = 80
EPS = 1e-05
NEG = -1e30
F32 = jnp.float32
BF16 = jnp.bfloat16
ROOT_HALF = math.sqrt(0.5)
INV_ROOT_TAU = 1.0 / math.sqrt(2.0 * math.pi)
VMEM_BYTES = 28 * 1024 * 1024


def dot(left, right, left_dim, right_dim):
    return lax.dot_general(
        left, right, (((left_dim,), (right_dim,)), ((), ())), preferred_element_type=F32
    )


def nn(left, right):
    return dot(left, right, 1, 0)


def nt(left, right):
    return dot(left, right, 1, 1)


def tn(left, right):
    return dot(left, right, 0, 0)


def iota(shape, axis):
    return lax.broadcasted_iota(jnp.int32, shape, axis)


def norm_parts(values):
    centred = values - jnp.mean(values, axis=-1, keepdims=True)
    spread = jnp.mean(centred * centred, axis=-1, keepdims=True)
    scale = lax.rsqrt(spread + EPS)
    return centred * scale, scale


def norm_back(values, gain, upstream):
    unit, scale = norm_parts(values)
    inner = upstream * gain
    first = jnp.mean(inner, axis=-1, keepdims=True)
    second = jnp.mean(inner * unit, axis=-1, keepdims=True)
    grad = scale * (inner - first - unit * second)
    return (
        grad,
        jnp.sum(upstream * unit, axis=0, keepdims=True),
        jnp.sum(upstream, axis=0, keepdims=True),
    )


def line(ref):
    return ref[...].astype(F32).reshape(1, ref.shape[0])


def column_bias(ref, count):
    first = jnp.where(iota((16, ref.shape[0]), 0) == 0, line(ref), 0.0).astype(BF16)
    return tn(first, jnp.ones((16, count), BF16))


def mp_side():
    return lax.axis_index("mp") % 2


def key_extra(count, limit):
    rows = iota((16, count), 0)
    hidden_keys = jnp.where(iota((16, count), 1) < limit, 0.0, NEG)
    ones = jnp.where(rows < 4, 1.0, 0.0)
    return jnp.where(rows == 0, hidden_keys, ones).astype(BF16)


def value_extra(count):
    return jnp.where(iota((16, count), 0) < 3, 1.0, 0.0).astype(BF16)


def three_parts(row):
    high = row.astype(BF16)
    rest = row - high.astype(F32)
    middle = rest.astype(BF16)
    last = (rest - middle.astype(F32)).astype(BF16)
    return high.astype(F32), middle.astype(F32), last.astype(F32)


def split_rows(rows, row, first, with_one):
    high, middle, last = three_parts(row)
    base = jnp.where(rows == 0, 1.0, 0.0) if with_one else jnp.zeros(rows.shape, F32)
    out = jnp.where(rows == first, high, base)
    out = jnp.where(rows == first + 1, middle, out)
    return jnp.where(rows == first + 2, last, out).astype(BF16)


def store_halves(part, side, keep_ref, send_ref):
    half = part.shape[0] // 2
    low = part.astype(BF16)

    @pl.when(side == 0)
    def _():
        keep_ref[...] = low[:half]
        send_ref[...] = low[half:]

    @pl.when(side == 1)
    def _():
        keep_ref[...] = low[half:]
        send_ref[...] = low[:half]


def join_halves(pieces, side, scratch):
    own, own_far, other, other_far = pieces
    half = own.shape[0]
    here = pl.multiple_of(side * half, 16)
    there = pl.multiple_of((1 - side) * half, 16)
    scratch[pl.ds(here, half), :] = own[...].astype(F32) + own_far[...].astype(F32)
    scratch[pl.ds(there, half), :] = other[...].astype(F32) + other_far[...].astype(F32)
    return scratch[...]


def attend_block(keys, queries, keep):
    scores = tn(keys, queries)
    if keep is not None:
        scores = jnp.where(keep, scores, NEG)
    return scores


def causal_mask(count):
    return iota((count, count), 0) <= iota((count, count), 1)


def attention_forward(q_ref, ka_ref, va_ref, qa, o_ref, lse_ref, chunk, causal):
    heads, _, keys = ka_ref.shape
    count = q_ref.shape[1]
    rows = iota((16, count), 0)
    qa[HEAD:AUG, :] = jnp.where(rows == 0, 1.0, 0.0).astype(BF16)
    keep = causal_mask(count) if causal else None
    lse_rows = iota((8, count), 0)
    lse = jnp.zeros((8, count), F32)
    for head in range(heads):
        spot = slice(head * HEAD, (head + 1) * HEAD)
        qa[0:HEAD, :] = q_ref[spot, :]
        queries = qa[...]
        largest = None
        for start in range(0, keys, chunk):
            part = slice(start, start + chunk)
            scores = attend_block(ka_ref[head, :, part], queries, keep)
            top = jnp.max(scores, axis=0, keepdims=True)
            if largest is None:
                powers = jnp.exp(scores - top).astype(BF16)
                mixed = nn(va_ref[head, :, part], powers)
                largest = top
            else:
                newer = jnp.maximum(largest, top)
                powers = jnp.exp(scores - newer).astype(BF16)
                mixed = mixed * jnp.exp(largest - newer) + nn(va_ref[head, :, part], powers)
                largest = newer
        total = mixed[HEAD : HEAD + 1]
        o_ref[spot, :] = (mixed[0:HEAD] / total).astype(BF16)
        lse = jnp.where(lse_rows == head, largest + jnp.log(total), lse)
    lse_ref[...] = lse


def attention_backward(
    q_ref, ka_ref, va_ref, o_ref, lse_ref, do_ref, qa, doa, dq_ref, dk_ref, dv_ref, chunk, causal
):
    heads, _, keys = ka_ref.shape
    count = q_ref.shape[1]
    rows = iota((16, count), 0)
    keep = causal_mask(count) if causal else None
    for head in range(heads):
        spot = slice(head * HEAD, (head + 1) * HEAD)
        queries = q_ref[spot, :]
        mix_grad = do_ref[spot, :]
        qa[0:HEAD, :] = queries
        doa[0:HEAD, :] = mix_grad
        qa[HEAD:AUG, :] = split_rows(rows, -lse_ref[head : head + 1, :], 1, True)
        centre = jnp.sum(
            mix_grad.astype(F32) * o_ref[spot, :].astype(F32), axis=0, keepdims=True
        )
        doa[HEAD:AUG, :] = split_rows(rows, -centre, 0, False)
        query_side = qa[...]
        grad_side = doa[...]
        query_grad = jnp.zeros((HEAD, count), F32)
        for start in range(0, keys, chunk):
            part = slice(start, start + chunk)
            shares = jnp.exp(attend_block(ka_ref[head, :, part], query_side, keep))
            pushed = tn(va_ref[head, :, part], grad_side)
            score_grad = (shares * pushed).astype(BF16)
            dv_ref[spot, part] = nt(mix_grad, shares.astype(BF16)).astype(BF16)
            dk_ref[spot, part] = nt(queries, score_grad).astype(BF16)
            query_grad = query_grad + nn(ka_ref[head, 0:HEAD, part], score_grad)
        dq_ref[spot, :] = (query_grad * 0.125).astype(BF16)


def row_of_sums(matrix):
    ones = jnp.ones((16, matrix.shape[1]), BF16)
    return nt(ones, matrix)[0:1]


def self_forward(item, lengths, x_ref, gain, shift, wq, qbias, wk, wv, vbias, wo, q_o, ka_o, va_o, o_o, lse_o, keep_o, send_o, qa):
    count = x_ref.shape[1]
    unit, _ = norm_parts(x_ref[item].astype(F32))
    normed = (unit * line(gain) + line(shift)).astype(BF16)
    queries = (nt(wq[...], normed) + column_bias(qbias, count)).astype(BF16)
    q_o[...] = queries * jnp.asarray(0.125, BF16)
    key_rows = nt(wk[...], normed).astype(BF16)
    value_rows = (nt(wv[...], normed) + column_bias(vbias, count)).astype(BF16)
    extra = key_extra(count, lengths[item])
    other = value_extra(count)
    for head in range(ka_o.shape[0]):
        spot = slice(head * HEAD, (head + 1) * HEAD)
        ka_o[head, 0:HEAD, :] = key_rows[spot]
        ka_o[head, HEAD:AUG, :] = extra
        va_o[head, 0:HEAD, :] = value_rows[spot]
        va_o[head, HEAD:AUG, :] = other
    attention_forward(q_o, ka_o, va_o, qa, o_o, lse_o, count, True)
    store_halves(tn(o_o[...], wo[...]), mp_side(), keep_o, send_o)


def cross_keys(item, frames, enc, wk, wv, vbias, ka_o, va_o):
    count = enc.shape[0]
    wide = ka_o.shape[2]
    memory = enc[...]
    key_rows = nt(wk[...], memory).astype(BF16)
    value_rows = (nt(wv[...], memory) + column_bias(vbias, count)).astype(BF16)
    extra = key_extra(wide, frames[item])
    other = value_extra(wide)
    for head in range(ka_o.shape[0]):
        spot = slice(head * HEAD, (head + 1) * HEAD)
        if wide > count:
            ka_o[head, 0:HEAD, wide - 128 :] = jnp.zeros((HEAD, 128), BF16)
            va_o[head, 0:HEAD, wide - 128 :] = jnp.zeros((HEAD, 128), BF16)
        ka_o[head, 0:HEAD, 0:count] = key_rows[spot]
        ka_o[head, HEAD:AUG, :] = extra
        va_o[head, 0:HEAD, 0:count] = value_rows[spot]
        va_o[head, HEAD:AUG, :] = other


def cross_forward(item, chunk, x_ref, s0, s1, s2, s3, obias, gain, shift, wq, qbias, wo, ka, va, x1_o, h2_o, q_o, o_o, lse_o, keep_o, send_o, whole, qa):
    count = x_ref.shape[1]
    side = mp_side()
    after = x_ref[item].astype(F32) + join_halves((s0, s1, s2, s3), side, whole) + line(obias)
    x1_o[...] = after
    unit, _ = norm_parts(after)
    normed = (unit * line(gain) + line(shift)).astype(BF16)
    h2_o[...] = normed
    queries = (nt(wq[...], normed) + column_bias(qbias, count)).astype(BF16)
    q_o[...] = queries * jnp.asarray(0.125, BF16)
    attention_forward(q_o, ka, va, qa, o_o, lse_o, chunk, False)
    store_halves(tn(o_o[...], wo[...]), side, keep_o, send_o)


def upstream_rows(item, lengths, tasks, og):
    task = tasks[item]
    weight = jnp.where(task == 0, 1.0, jnp.where(task == 1, 0.6, 2.0)).astype(F32)
    valid = iota((og.shape[1], 1), 0) < lengths[item]
    return og[item].astype(F32) * jnp.where(valid, weight, 0.0)


def feed(item, lengths, tasks, x1, s0, s1, s2, s3, og, obias, gain, shift, we, ebias, wc, x2_o, h3_o, a_o, dz_o, gy_o, vec_o, keep_o, send_o, bkeep_o, bsend_o, whole):
    side = mp_side()
    after = x1[...] + join_halves((s0, s1, s2, s3), side, whole) + line(obias)
    x2_o[...] = after
    unit, _ = norm_parts(after)
    normed = (unit * line(gain) + line(shift)).astype(BF16)
    h3_o[...] = normed
    before = nn(normed, we[...]) + line(ebias)
    share = 0.5 + 0.5 * lax.erf(before * ROOT_HALF)
    active = (before * share).astype(BF16)
    a_o[...] = active
    slope = share + before * (jnp.exp(before * before * -0.5) * INV_ROOT_TAU)
    grad = upstream_rows(item, lengths, tasks, og)
    low = grad.astype(BF16)
    gy_o[...] = low
    inner = (nt(low, wc[...]) * slope).astype(BF16)
    dz_o[...] = inner
    store_halves(nt(inner, we[...]), side, bkeep_o, bsend_o)
    store_halves(nn(active, wc[...]), side, keep_o, send_o)
    pick = iota((8, vec_o.shape[1]), 0)
    out = jnp.where(pick == 0, jnp.sum(grad, axis=0, keepdims=True), 0.0)
    vec_o[...] = jnp.where(pick == 1, jnp.sum(inner.astype(F32), axis=0, keepdims=True), out)


def sum_of(refs):
    out = refs[0]
    for other in refs[1:]:
        out = out + other
    return out


def feed_weights(items, *refs):
    h3, dz, a, gy, vecs = (refs[k * items : (k + 1) * items] for k in range(5))
    pack = refs[5 * items]
    width = h3[0].shape[1]
    unit = dz[0].shape[1]
    pack[0:width, :] = sum_of([tn(h3[k][...], dz[k][...]) for k in range(items)]).astype(BF16)
    pack[width : width + unit, :] = sum_of([tn(a[k][...], gy[k][...]) for k in range(items)]).astype(BF16)
    tail = pack.shape[0] - width - unit
    pack[width + unit :, :] = jnp.zeros((tail, width), BF16)
    low = sum_of([v[...] for v in vecs]).astype(BF16)
    pack[width + unit : width + unit + 8, :] = low


def cross_backward(item, chunk, lengths, tasks, x2, s0, s1, s2, s3, og, gain, wo, wq, ka, va, q, o, lse, dx2_o, g2_o, dq_o, dk_o, dv_o, vec_o, keep_o, send_o, whole, qa, doa, do):
    side = mp_side()
    grad_in = join_halves((s0, s1, s2, s3), side, whole)
    grad, gain_row, shift_row = norm_back(x2[...], line(gain), grad_in)
    total = upstream_rows(item, lengths, tasks, og) + grad
    dx2_o[...] = total
    low = total.astype(BF16)
    g2_o[...] = low
    do[...] = nt(wo[...], low).astype(BF16)
    attention_backward(q, ka, va, o, lse, do, qa, doa, dq_o, dk_o, dv_o, chunk, False)
    store_halves(tn(dq_o[...], wq[...]), side, keep_o, send_o)
    pick = iota((8, vec_o.shape[1]), 0)
    out = jnp.where(pick == 0, gain_row, 0.0)
    out = jnp.where(pick == 1, shift_row, out)
    vec_o[...] = jnp.where(pick == 2, jnp.sum(total, axis=0, keepdims=True), out)
    vec_o[3:4, 0 : dq_o.shape[0]] = row_of_sums(dq_o[...])
    vec_o[4:5, 0 : dq_o.shape[0]] = row_of_sums(dv_o[...])


def memory_grad(wk, wv, dk, dv, keep_o, send_o):
    count = keep_o.shape[2]
    position = lax.axis_index("mp")
    rows = keep_o.shape[1]
    whole = (tn(wk[...], dk[...]) + tn(wv[...], dv[...])).astype(BF16)
    for block in range(4):
        piece = whole[block * rows : (block + 1) * rows, 0:count]
        relative = lax.bitwise_xor(position, block)
        slot = relative // 2

        @pl.when(relative % 2 == 0)
        def _():
            keep_o[slot] = piece

        @pl.when(relative % 2 == 1)
        def _():
            send_o[slot] = piece


def place_of(block):
    return (block % 2) * 4 + (block // 2 % 2) * 2 + block // 4 % 2


def scatter_blocks(whole, keep_o, send_o):
    position = lax.axis_index("dp") % 8
    rows = keep_o.shape[1]
    for block in range(8):
        place = place_of(lax.bitwise_xor(position, block))
        piece = whole[block * rows : (block + 1) * rows, :].astype(BF16)

        @pl.when(place < 4)
        def _():
            keep_o[place] = piece

        @pl.when(place >= 4)
        def _():
            send_o[place - 4] = piece


def gather_blocks(near, far, whole):
    position = lax.axis_index("dp") % 8
    rows = near.shape[1]
    for block in range(8):
        place = place_of(lax.bitwise_xor(position, block))
        spot = slice(block * rows, (block + 1) * rows)

        @pl.when(place < 4)
        def _():
            whole[spot, :] = near[place].astype(F32)

        @pl.when(place >= 4)
        def _():
            whole[spot, :] = far[place - 4].astype(F32)


def cross_weights(items, enc, *refs):
    dq, h2, o, g2, dk, dv, vecs = (refs[k * items : (k + 1) * items] for k in range(7))
    keep_o, send_o, whole = refs[7 * items :]
    rows = dq[0].shape[0]
    count = enc.shape[1]
    span = range(items)
    whole[0:rows, :] = sum_of([nn(dq[k][...], h2[k][...]) for k in span])
    whole[rows : 2 * rows, :] = sum_of([nn(dk[k][:, 0:count], enc[k]) for k in span])
    whole[2 * rows : 3 * rows, :] = sum_of([nn(dv[k][:, 0:count], enc[k]) for k in span])
    whole[3 * rows : 4 * rows, :] = sum_of([nn(o[k][...], g2[k][...]) for k in span])
    whole[4 * rows :, :] = jnp.zeros((whole.shape[0] - 4 * rows, whole.shape[1]), F32)
    whole[4 * rows : 4 * rows + 8, :] = sum_of([v[...] for v in vecs])
    scatter_blocks(whole, keep_o, send_o)


def self_backward(item, x1, s0, s1, s2, s3, dx2, x_ref, gain, wo, wq, wk, wv, ka, va, q, o, lse, dx1_o, g1_o, dqkv_o, vec_o, keep_o, send_o, whole, qa, doa, do):
    side = mp_side()
    grad_in = join_halves((s0, s1, s2, s3), side, whole)
    grad, gain_row, shift_row = norm_back(x1[...], line(gain), grad_in)
    total = dx2[...] + grad
    dx1_o[...] = total
    low = total.astype(BF16)
    g1_o[...] = low
    do[...] = nt(wo[...], low).astype(BF16)
    rows = do.shape[0]
    dq_o = dqkv_o.at[0:rows]
    dk_o = dqkv_o.at[rows : 2 * rows]
    dv_o = dqkv_o.at[2 * rows : 3 * rows]
    attention_backward(q, ka, va, o, lse, do, qa, doa, dq_o, dk_o, dv_o, q.shape[1], True)
    part = tn(dq_o[...], wq[...]) + tn(dk_o[...], wk[...]) + tn(dv_o[...], wv[...])
    store_halves(part, side, keep_o, send_o)
    unit, _ = norm_parts(x_ref[item].astype(F32))
    pick = iota((8, vec_o.shape[1]), 0)
    out = jnp.where(pick == 0, gain_row, 0.0)
    out = jnp.where(pick == 1, shift_row, out)
    out = jnp.where(pick == 2, jnp.sum(total, axis=0, keepdims=True), out)
    out = jnp.where(pick == 5, jnp.sum(part * unit, axis=0, keepdims=True), out)
    vec_o[...] = jnp.where(pick == 6, jnp.sum(part, axis=0, keepdims=True), out)
    vec_o[3:4, 0:rows] = row_of_sums(dq_o[...])
    vec_o[4:5, 0:rows] = row_of_sums(dv_o[...])


def self_weights(items, x_ref, gain, shift, *refs):
    dqkv, o, g1, vecs = (refs[k * items : (k + 1) * items] for k in range(4))
    keep_o, send_o, whole = refs[4 * items :]
    rows = o[0].shape[0]
    span = range(items)
    normed = []
    for k in span:
        unit, _ = norm_parts(x_ref[k].astype(F32))
        normed.append((unit * line(gain) + line(shift)).astype(BF16))
    whole[0 : 3 * rows, :] = sum_of([nn(dqkv[k][...], normed[k]) for k in span])
    whole[3 * rows : 4 * rows, :] = sum_of([nn(o[k][...], g1[k][...]) for k in span])
    whole[4 * rows :, :] = jnp.zeros((whole.shape[0] - 4 * rows, whole.shape[1]), F32)
    whole[4 * rows : 4 * rows + 8, :] = sum_of([v[...] for v in vecs])
    scatter_blocks(whole, keep_o, send_o)


def unpack(near, far, first, second, third, fourth, vec_o, whole):
    gather_blocks(near, far, whole)
    rows = first.shape[0]
    for k, out in enumerate((first, second, third, fourth)):
        out[...] = whole[k * rows : (k + 1) * rows, :]
    vec_o[...] = whole[4 * rows : 4 * rows + 8, :]


def finish_out(item, x2, s0, s1, s2, s3, bias, *rest):
    out, whole = rest[-2:]
    total = x2[...] + join_halves((s0, s1, s2, s3), mp_side(), whole) + line(bias)
    out[...] = total.astype(BF16)


def finish_grad(item, dx1, s0, s1, s2, s3, x_ref, gain, *rest):
    out, whole = rest[-2:]
    grad_in = join_halves((s0, s1, s2, s3), mp_side(), whole)
    grad, _, _ = norm_back(x_ref[item].astype(F32), line(gain), grad_in)
    out[...] = dx1[...] + grad


SCALARS = pl.BlockSpec(memory_space=pltpu.SMEM)
LEFT = pl.BlockSpec(memory_space=pl.ANY)
NEAR = pl.BlockSpec(memory_space=pltpu.VMEM)


def chosen(array, item):
    rest = (0,) * (len(array.shape) - 1)
    return pl.BlockSpec((None,) + tuple(array.shape[1:]), lambda *_: (item,) + rest)


def shape(dims, dtype):
    return jax.ShapeDtypeStruct(dims, dtype)


def run(body, name, cost, operands, outs, scratch=(), specs=None, out_specs=None, aliases=None):
    specs = specs or {}
    placed, in_specs = [], []
    for k, array in enumerate(operands):
        spec = specs.get(k, SCALARS if array.dtype == jnp.int32 else NEAR)
        if spec is NEAR:
            array = pltpu.with_memory_space_constraint(array, pltpu.VMEM)
        placed.append(array)
        in_specs.append(spec)
    return pl.pallas_call(
        body,
        name=name,
        grid=(1,),
        in_specs=in_specs,
        out_specs=out_specs or [NEAR] * len(outs),
        out_shape=list(outs),
        scratch_shapes=list(scratch),
        input_output_aliases=aliases or {},
        cost_estimate=pl.CostEstimate(flops=int(cost * 1.1e9), transcendentals=0, bytes_accessed=0),
        compiler_params=pltpu.CompilerParams(vmem_limit_bytes=VMEM_BYTES),
    )(*placed)


def swap(value, axis, size, bit):
    return lax.ppermute(value, axis, [(k, k ^ bit) for k in range(size)])


def after(value, *earlier):
    return lax.optimization_barrier((value, earlier))[0]


def add_low(left, right):
    return (left.astype(F32) + right.astype(F32)).astype(BF16)


def mp_near(send, size):
    return swap(send, "mp", size, 1)


def mp_pieces(keep, near, size):
    own = add_low(keep, near)
    far = swap(own, "mp", size, 2)
    other = swap(own, "mp", size, 1)
    other_far = swap(far, "mp", size, 1)
    return own, far, other, other_far


def dp_sum(keep, send, size):
    near = swap(send, "dp", size, 1)
    keep, send = add_low(keep[:2], near[:2]), add_low(keep[2:], near[2:])
    near = swap(send, "dp", size, 2)
    keep, send = add_low(keep[:1], near[:1]), add_low(keep[1:], near[1:])
    total = add_low(keep, swap(send, "dp", size, 4))
    bit = 8
    while bit < size:
        total = add_low(total, swap(total, "dp", size, bit))
        bit *= 2
    total = jnp.concatenate([total, swap(total, "dp", size, 4)])
    total = jnp.concatenate([total, swap(total, "dp", size, 2)])
    return total, swap(total, "dp", size, 1)


def shards(sizes, *arguments):
    (
        hidden, encoder, lengths, tasks, frames, out_grad,
        gain_self, shift_self, query_self, qbias_self, key_self, value_self, vbias_self, output_self, obias_self,
        gain_cross, shift_cross, query_cross, qbias_cross, key_cross, value_cross, vbias_cross, output_cross, obias_cross,
        gain_feed, shift_feed, expand_weight, expand_bias, contract_weight, contract_bias,
    ) = arguments
    n_mp, n_dp = sizes["mp"], sizes["dp"]
    items, length, width = hidden.shape
    memory_len = encoder.shape[1]
    rows = query_self.shape[1]
    heads = rows // HEAD
    units = expand_weight.shape[1]
    wide = -(-memory_len // 512) * 512
    chunk = 512
    half = length // 2
    wq1, wk1, wv1 = query_self.T, key_self.T, value_self.T
    wq2, wk2, wv2 = query_cross.T, key_cross.T, value_cross.T

    def near_shape(dims, dtype=BF16):
        return pltpu.VMEM(dims, dtype)

    low_rows = near_shape((rows, length))
    mem_rows = near_shape((rows, wide))
    half_out = near_shape((half, width))
    state = near_shape((length, width), F32)
    low_state = near_shape((length, width))
    unit_state = near_shape((length, units))
    vec_out = near_shape((8, width), F32)
    lse_out = near_shape((8, length), F32)
    aug_out = near_shape((heads, AUG, length))
    aug_mem = near_shape((heads, AUG, wide))
    whole = pltpu.VMEM((length, width), F32)
    aug = pltpu.VMEM((AUG, length), BF16)
    row_scratch = pltpu.VMEM((rows, length), BF16)
    pack_rows = 4 * rows + 64
    pack_scratch = pltpu.VMEM((pack_rows, width), F32)
    pack_half = shape((4, pack_rows // 8, width), BF16)
    span = range(items)
    last = items - 1
    bind = functools.partial

    self_out, near = [], []
    for i in span:
        out = run(
            bind(self_forward, i), "self_forward", 6,
            (lengths, hidden, gain_self, shift_self, wq1, qbias_self, wk1, wv1, vbias_self, output_self),
            (low_rows, aug_out, aug_out, low_rows, lse_out, half_out, half_out), (aug,),
        )
        self_out.append(out)
        near.append(mp_near(out[6], n_mp))

    def keys(i, start):
        return run(
            bind(cross_keys, i), "cross_keys", 5, (after(frames, start), encoder, wk2, wv2, vbias_cross),
            (aug_mem, aug_mem), (), {1: chosen(encoder, i)},
        )

    cross_kv, pieces = [None] * items, []
    token = self_out[last][4]
    for i in span:
        pieces.append(mp_pieces(self_out[i][5], after(near[i], token), n_mp))
        if i == 0:
            cross_kv[0] = keys(0, token)
            token = cross_kv[0][0]

    cross_out, cross_near = [], []
    for i in span:
        out = run(
            bind(cross_forward, i, chunk), "cross_forward", 9,
            (hidden, *pieces[i], obias_self, gain_cross, shift_cross, wq2, qbias_cross, output_cross, *cross_kv[i]),
            (state, low_state, low_rows, low_rows, lse_out, half_out, half_out), (whole, aug),
        )
        cross_out.append(out)
        cross_near.append(mp_near(out[6], n_mp))
        if i < last:
            cross_kv[i + 1] = keys(i + 1, out[4])
            cross_near[i] = after(cross_near[i], cross_kv[i + 1][0])

    feed_out, feed_near = [], []
    for i in span:
        done = mp_pieces(cross_out[i][5], cross_near[i], n_mp)
        out = run(
            bind(feed, i), "feed", 9,
            (lengths, tasks, cross_out[i][0], *done, out_grad, obias_cross, gain_feed, shift_feed, expand_weight, expand_bias, contract_weight),
            (state, low_state, unit_state, unit_state, low_state, vec_out, half_out, half_out, half_out, half_out), (whole,),
        )
        feed_out.append(out)
        feed_near.append(mp_near(out[9], n_mp))

    token = feed_out[last][5]
    back_pieces = [mp_pieces(feed_out[i][8], after(feed_near[i], token), n_mp) for i in span]
    feed_pack = run(
        bind(feed_weights, items), "feed_weights", 7,
        [feed_out[i][k] for k in (1, 3, 2, 4, 5) for i in span],
        (shape((width + units + 16, width), BF16),),
    )[0]
    feed_pack = lax.psum(feed_pack, "dp")
    block_near = [mp_near(feed_out[i][7], n_mp) for i in span]

    back_out, back_near = [], []
    for i in span:
        _, _, q2, o2, lse2 = cross_out[i][:5]
        out = run(
            bind(cross_backward, i, chunk), "cross_backward", 12,
            (lengths, tasks, feed_out[i][0], *back_pieces[i], out_grad, gain_feed, output_cross, wq2, *cross_kv[i], q2, o2, lse2),
            (state, low_state, low_rows, mem_rows, mem_rows, vec_out, half_out, half_out), (whole, aug, aug, row_scratch),
        )
        back_out.append(out)
        back_near.append(mp_near(out[7], n_mp))
    block_pieces = [mp_pieces(feed_out[i][6], after(block_near[i], back_out[0][5]), n_mp) for i in span]
    token = back_out[last][5]
    dq_pieces = [mp_pieces(back_out[i][6], after(back_near[i], token), n_mp) for i in span]

    memory_parts = []
    for i in span:
        memory_parts.append(
            run(
                memory_grad, "memory_grad", 5, (wk2, wv2, back_out[i][3], back_out[i][4]),
                (near_shape((2, rows, memory_len)), near_shape((2, rows, memory_len))),
            )
        )

    cross_pack = run(
        bind(cross_weights, items), "cross_weights", 8,
        [encoder] + [out[2] for out in back_out] + [out[1] for out in cross_out] + [out[3] for out in cross_out]
        + [out[1] for out in back_out] + [out[3] for out in back_out] + [out[4] for out in back_out]
        + [out[5] for out in back_out],
        (pack_half, pack_half), (pack_scratch,), {0: pl.BlockSpec(encoder.shape, lambda *_: (0, 0, 0))},
    )
    cross_sum = dp_sum(*cross_pack, n_dp)

    self_back, self_near = [], []
    for i in span:
        q1, ka1, va1, o1, lse1 = self_out[i][:5]
        out = run(
            bind(self_backward, i), "self_backward", 9,
            (cross_out[i][0], *dq_pieces[i], back_out[i][0], hidden, gain_cross, output_self, wq1, wk1, wv1, ka1, va1, q1, o1, lse1),
            (state, low_state, near_shape((3 * rows, length)), vec_out, half_out, half_out), (whole, aug, aug, row_scratch),
        )
        self_back.append(out)
        self_near.append(mp_near(out[5], n_mp))

    self_pack = run(
        bind(self_weights, items), "self_weights", 6,
        [hidden, gain_self, shift_self] + [out[2] for out in self_back] + [out[3] for out in self_out]
        + [out[1] for out in self_back] + [out[3] for out in self_back],
        (pack_half, pack_half), (pack_scratch,),
    )
    self_sum = dp_sum(*self_pack, n_dp)
    token = self_back[last][3]
    last_pieces = [mp_pieces(self_back[i][4], after(self_near[i], token), n_mp) for i in span]

    block_out, hidden_grad = None, None
    block_shape = shape(hidden.shape, BF16)
    grad_shape = shape(hidden.shape, F32)
    for i in span:
        extra = () if block_out is None else (block_out,)
        block_out = run(
            bind(finish_out, i), "finish_out", 3,
            (feed_out[i][0], *block_pieces[i], contract_bias, *extra), (block_shape,), (whole,),
            {6: LEFT}, [chosen(block_shape, i)], {6: 0} if extra else {},
        )[0]
    for i in span:
        extra = () if hidden_grad is None else (hidden_grad,)
        hidden_grad = run(
            bind(finish_grad, i), "finish_grad", 4,
            (self_back[i][0], *last_pieces[i], hidden, gain_self, *extra), (grad_shape,), (whole,),
            {7: LEFT}, [chosen(grad_shape, i)], {7: 0} if extra else {},
        )[0]

    memory_grads = []
    for keep, send in memory_parts:
        near_part = swap(send, "mp", n_mp, 1)
        kept, sent = add_low(keep[0], near_part[0]), add_low(keep[1], near_part[1])
        memory_grads.append(kept.astype(F32) + swap(sent, "mp", n_mp, 2).astype(F32))
    encoder_grad = jnp.stack(memory_grads).transpose(0, 2, 1)

    matrix = shape((rows, width), F32)
    outs = (matrix, matrix, matrix, matrix, shape((8, width), F32))
    cross_grads = run(unpack, "unpack", 3, cross_sum, outs, (pack_scratch,))
    self_grads = run(unpack, "unpack", 3, self_sum, outs, (pack_scratch,))
    feed_grads = feed_pack.astype(F32)
    norm_rows = self_grads[4]
    norm_rows = norm_rows + swap(norm_rows, "mp", n_mp, 1)
    norm_rows = norm_rows + swap(norm_rows, "mp", n_mp, 2)
    return (
        block_out,
        hidden_grad,
        encoder_grad,
        norm_rows[5],
        norm_rows[6],
        self_grads[0].T,
        self_grads[4][3, 0:rows],
        self_grads[1].T,
        self_grads[2].T,
        self_grads[4][4, 0:rows],
        self_grads[3],
        self_grads[4][2],
        self_grads[4][0],
        self_grads[4][1],
        cross_grads[0].T,
        cross_grads[4][3, 0:rows],
        cross_grads[1].T,
        cross_grads[2].T,
        cross_grads[4][4, 0:rows],
        cross_grads[3],
        cross_grads[4][2],
        cross_grads[4][0],
        cross_grads[4][1],
        feed_grads[0:width],
        feed_grads[width + units + 1],
        feed_grads[width : width + units],
        feed_grads[width + units],
    )


def solution(mesh):
    column, row, flat = P(None, "mp"), P("mp", None), P("mp")
    cube = P("dp", None, None)
    attention = (P(), P(), column, flat, column, column, flat, row, P())
    grads = (P(), P(), column, flat, column, column, flat, row, P())
    return jax.shard_map(
        functools.partial(shards, dict(mesh.shape)),
        mesh=mesh,
        in_specs=(cube, cube, P("dp"), P("dp"), P("dp"), cube)
        + attention
        + attention
        + (P(), P(), column, flat, row, P()),
        out_specs=(cube, cube, P("dp", None, "mp")) + grads + grads + (P(), P(), column, flat, row, P()),
        check_vma=False,
    )
```

```python
import functools
import math

import jax
import jax.numpy as jnp
from jax import lax
from jax.experimental import pallas as pl
from jax.experimental.pallas import tpu as pltpu
from jax.sharding import PartitionSpec as P

HEAD = 64
AUG = 80
EPS = 1e-05
NEG = -1e30
F32 = jnp.float32
BF16 = jnp.bfloat16
ROOT_HALF = math.sqrt(0.5)
INV_ROOT_TAU = 1.0 / math.sqrt(2.0 * math.pi)
VMEM_BYTES = 20 * 1024 * 1024
COST = 1


def dot(left, right, left_dim, right_dim):
    return lax.dot_general(
        left, right, (((left_dim,), (right_dim,)), ((), ())), preferred_element_type=F32
    )


def nn(left, right):
    return dot(left, right, 1, 0)


def nt(left, right):
    return dot(left, right, 1, 1)


def tn(left, right):
    return dot(left, right, 0, 0)


def iota(shape, axis):
    return lax.broadcasted_iota(jnp.int32, shape, axis)


def norm_parts(values):
    centred = values - jnp.mean(values, axis=-1, keepdims=True)
    spread = jnp.mean(centred * centred, axis=-1, keepdims=True)
    scale = lax.rsqrt(spread + EPS)
    return centred * scale, scale


def norm_back(values, gain, upstream):
    unit, scale = norm_parts(values)
    inner = upstream * gain
    first = jnp.mean(inner, axis=-1, keepdims=True)
    second = jnp.mean(inner * unit, axis=-1, keepdims=True)
    grad = scale * (inner - first - unit * second)
    return (
        grad,
        jnp.sum(upstream * unit, axis=0, keepdims=True),
        jnp.sum(upstream, axis=0, keepdims=True),
    )


def line(ref):
    return ref[...].astype(F32).reshape(1, ref.shape[0])


def column_bias(ref, count):
    first = jnp.where(iota((16, ref.shape[0]), 0) == 0, line(ref), 0.0).astype(BF16)
    return tn(first, jnp.ones((16, count), BF16))


def mp_side():
    return lax.axis_index("mp") % 2


def key_extra(count, limit):
    rows = iota((16, count), 0)
    hidden_keys = jnp.where(iota((16, count), 1) < limit, 0.0, NEG)
    ones = jnp.where(rows < 4, 1.0, 0.0)
    return jnp.where(rows == 0, hidden_keys, ones).astype(BF16)


def value_extra(count):
    return jnp.where(iota((16, count), 0) < 3, 1.0, 0.0).astype(BF16)


def three_parts(row):
    high = row.astype(BF16)
    rest = row - high.astype(F32)
    middle = rest.astype(BF16)
    last = (rest - middle.astype(F32)).astype(BF16)
    return high.astype(F32), middle.astype(F32), last.astype(F32)


def split_rows(rows, row, first, with_one):
    high, middle, last = three_parts(row)
    base = jnp.where(rows == 0, 1.0, 0.0) if with_one else jnp.zeros(rows.shape, F32)
    out = jnp.where(rows == first, high, base)
    out = jnp.where(rows == first + 1, middle, out)
    return jnp.where(rows == first + 2, last, out).astype(BF16)


def store_halves(part, side, keep_ref, send_ref, rest_ref):
    half = part.shape[0] // 2
    edge = send_ref.shape[0]
    low = part.astype(BF16)

    @pl.when(side == 0)
    def _():
        keep_ref[...] = low[:half]
        send_ref[...] = low[half : half + edge]
        rest_ref[...] = low[half + edge :]

    @pl.when(side == 1)
    def _():
        keep_ref[...] = low[half:]
        send_ref[...] = low[:edge]
        rest_ref[...] = low[edge:half]


def join_halves(pieces, side, scratch):
    own, own_far, other, other_far = pieces
    half = own.shape[0]
    here = pl.multiple_of(side * half, 16)
    there = pl.multiple_of((1 - side) * half, 16)
    scratch[pl.ds(here, half), :] = own[...].astype(F32) + own_far[...].astype(F32)
    scratch[pl.ds(there, half), :] = other[...].astype(F32) + other_far[...].astype(F32)
    return scratch[...]


def attend_block(keys, queries, keep):
    scores = tn(keys, queries)
    if keep is not None:
        scores = jnp.where(keep, scores, NEG)
    return scores


def causal_mask(count):
    return iota((count, count), 0) <= iota((count, count), 1)


def attention_forward(q_ref, ka_ref, va_ref, qa, o_ref, lse_ref, chunk, causal):
    heads, _, keys = ka_ref.shape
    count = q_ref.shape[1]
    rows = iota((16, count), 0)
    qa[HEAD:AUG, :] = jnp.where(rows == 0, 1.0, 0.0).astype(BF16)
    keep = causal_mask(count) if causal else None
    lse_rows = iota((8, count), 0)
    lse = jnp.zeros((8, count), F32)
    for head in range(heads):
        spot = slice(head * HEAD, (head + 1) * HEAD)
        qa[0:HEAD, :] = q_ref[spot, :]
        queries = qa[...]
        largest = None
        for start in range(0, keys, chunk):
            part = slice(start, start + chunk)
            scores = attend_block(ka_ref[head, :, part], queries, keep)
            top = jnp.max(scores, axis=0, keepdims=True)
            if largest is None:
                powers = jnp.exp(scores - top).astype(BF16)
                mixed = nn(va_ref[head, :, part], powers)
                largest = top
            else:
                newer = jnp.maximum(largest, top)
                powers = jnp.exp(scores - newer).astype(BF16)
                mixed = mixed * jnp.exp(largest - newer) + nn(va_ref[head, :, part], powers)
                largest = newer
        total = mixed[HEAD : HEAD + 1]
        o_ref[spot, :] = (mixed[0:HEAD] / total).astype(BF16)
        lse = jnp.where(lse_rows == head, largest + jnp.log(total), lse)
    lse_ref[...] = lse


def attention_backward(
    q_ref, ka_ref, va_ref, o_ref, lse_ref, do_ref, qa, doa, dq_ref, dk_ref, dv_ref, chunk, causal
):
    heads, _, keys = ka_ref.shape
    count = q_ref.shape[1]
    rows = iota((16, count), 0)
    keep = causal_mask(count) if causal else None
    for head in range(heads):
        spot = slice(head * HEAD, (head + 1) * HEAD)
        queries = q_ref[spot, :]
        mix_grad = do_ref[spot, :]
        qa[0:HEAD, :] = queries
        doa[0:HEAD, :] = mix_grad
        qa[HEAD:AUG, :] = split_rows(rows, -lse_ref[head : head + 1, :], 1, True)
        centre = jnp.sum(
            mix_grad.astype(F32) * o_ref[spot, :].astype(F32), axis=0, keepdims=True
        )
        doa[HEAD:AUG, :] = split_rows(rows, -centre, 0, False)
        query_side = qa[...]
        grad_side = doa[...]
        query_grad = jnp.zeros((HEAD, count), F32)
        for start in range(0, keys, chunk):
            part = slice(start, start + chunk)
            shares = jnp.exp(attend_block(ka_ref[head, :, part], query_side, keep))
            pushed = tn(va_ref[head, :, part], grad_side)
            score_grad = (shares * pushed).astype(BF16)
            dv_ref[spot, part] = nt(mix_grad, shares.astype(BF16)).astype(BF16)
            dk_ref[spot, part] = nt(queries, score_grad).astype(BF16)
            query_grad = query_grad + nn(ka_ref[head, 0:HEAD, part], score_grad)
        dq_ref[spot, :] = (query_grad * 0.125).astype(BF16)


def row_of_sums(matrix):
    ones = jnp.ones((16, matrix.shape[1]), BF16)
    return nt(ones, matrix)[0:1]


def self_forward(item, lengths, x_ref, gain, shift, wq, qbias, wk, wv, vbias, wo, q_o, ka_o, va_o, o_o, lse_o, keep_o, send_o, rest_o, qa):
    count = x_ref.shape[1]
    unit, _ = norm_parts(x_ref[item].astype(F32))
    normed = (unit * line(gain) + line(shift)).astype(BF16)
    queries = (nt(wq[...], normed) + column_bias(qbias, count)).astype(BF16)
    q_o[...] = queries * jnp.asarray(0.125, BF16)
    key_rows = nt(wk[...], normed).astype(BF16)
    value_rows = (nt(wv[...], normed) + column_bias(vbias, count)).astype(BF16)
    extra = key_extra(count, lengths[item])
    other = value_extra(count)
    for head in range(ka_o.shape[0]):
        spot = slice(head * HEAD, (head + 1) * HEAD)
        ka_o[head, 0:HEAD, :] = key_rows[spot]
        ka_o[head, HEAD:AUG, :] = extra
        va_o[head, 0:HEAD, :] = value_rows[spot]
        va_o[head, HEAD:AUG, :] = other
    attention_forward(q_o, ka_o, va_o, qa, o_o, lse_o, count, True)
    store_halves(tn(o_o[...], wo[...]), mp_side(), keep_o, send_o, rest_o)


def first_forward(item, first, count, lengths, *refs):
    sources, targets = refs[:count], refs[count + 8 : 2 * count + 8]
    outs, qa, sems = refs[count : count + 8], refs[-2], refs[-1]
    copies = [pltpu.make_async_copy(s, t, sems.at[k]) for k, (s, t) in enumerate(zip(sources, targets))]
    for copy in copies:
        copy.start()
    for copy in copies[:first]:
        copy.wait()
    self_forward(item, lengths, *targets[:first], *outs, qa)
    for copy in copies[first:]:
        copy.wait()


def cross_keys(item, frames, enc, wk, wv, vbias, ka_o, va_o):
    count = enc.shape[0]
    wide = ka_o.shape[2]
    memory = enc[...]
    key_rows = nt(wk[...], memory).astype(BF16)
    value_rows = (nt(wv[...], memory) + column_bias(vbias, count)).astype(BF16)
    extra = key_extra(wide, frames[item])
    other = value_extra(wide)
    for head in range(ka_o.shape[0]):
        spot = slice(head * HEAD, (head + 1) * HEAD)
        if wide > count:
            ka_o[head, 0:HEAD, wide - 128 :] = jnp.zeros((HEAD, 128), BF16)
            va_o[head, 0:HEAD, wide - 128 :] = jnp.zeros((HEAD, 128), BF16)
        ka_o[head, 0:HEAD, 0:count] = key_rows[spot]
        ka_o[head, HEAD:AUG, :] = extra
        va_o[head, 0:HEAD, 0:count] = value_rows[spot]
        va_o[head, HEAD:AUG, :] = other


def cross_forward(item, chunk, x_ref, s0, s1, s2, s3, obias, gain, shift, wq, qbias, wo, ka, va, x1_o, h2_o, q_o, o_o, lse_o, keep_o, send_o, rest_o, whole, qa):
    count = x_ref.shape[1]
    side = mp_side()
    after = x_ref[item].astype(F32) + join_halves((s0, s1, s2, s3), side, whole) + line(obias)
    x1_o[...] = after
    unit, _ = norm_parts(after)
    normed = (unit * line(gain) + line(shift)).astype(BF16)
    h2_o[...] = normed
    queries = (nt(wq[...], normed) + column_bias(qbias, count)).astype(BF16)
    q_o[...] = queries * jnp.asarray(0.125, BF16)
    attention_forward(q_o, ka, va, qa, o_o, lse_o, chunk, False)
    store_halves(tn(o_o[...], wo[...]), side, keep_o, send_o, rest_o)


def upstream_rows(item, lengths, tasks, og):
    task = tasks[item]
    weight = jnp.where(task == 0, 1.0, jnp.where(task == 1, 0.6, 2.0)).astype(F32)
    valid = iota((og.shape[1], 1), 0) < lengths[item]
    return og[item].astype(F32) * jnp.where(valid, weight, 0.0)


def feed(item, lengths, tasks, x1, s0, s1, s2, s3, og, obias, gain, shift, we, ebias, wc, x2_o, h3_o, a_o, dz_o, gy_o, vec_o, bkeep_o, bsend_o, brest_o, whole):
    side = mp_side()
    after = x1[...] + join_halves((s0, s1, s2, s3), side, whole) + line(obias)
    x2_o[...] = after
    unit, _ = norm_parts(after)
    normed = (unit * line(gain) + line(shift)).astype(BF16)
    h3_o[...] = normed
    before = nn(normed, we[...]) + line(ebias)
    share = 0.5 + 0.5 * lax.erf(before * ROOT_HALF)
    active = (before * share).astype(BF16)
    a_o[...] = active
    slope = share + before * (jnp.exp(before * before * -0.5) * INV_ROOT_TAU)
    grad = upstream_rows(item, lengths, tasks, og)
    low = grad.astype(BF16)
    gy_o[...] = low
    inner = (nt(low, wc[...]) * slope).astype(BF16)
    dz_o[...] = inner
    store_halves(nt(inner, we[...]), side, bkeep_o, bsend_o, brest_o)
    pick = iota((8, vec_o.shape[1]), 0)
    out = jnp.where(pick == 0, jnp.sum(grad, axis=0, keepdims=True), 0.0)
    vec_o[...] = jnp.where(pick == 1, jnp.sum(inner.astype(F32), axis=0, keepdims=True), out)


def feed_out_part(active, wc, keep_o, send_o, rest_o):
    store_halves(nn(active[...], wc[...]), mp_side(), keep_o, send_o, rest_o)


def sum_of(refs):
    out = refs[0]
    for other in refs[1:]:
        out = out + other
    return out


def feed_weights(items, *refs):
    h3, dz, a, gy, vecs = (refs[k * items : (k + 1) * items] for k in range(5))
    keep_o, send_o, whole = refs[5 * items :]
    width = h3[0].shape[1]
    edge = width + dz[0].shape[1]
    whole[0:width, :] = sum_of([tn(h3[k][...], dz[k][...]) for k in range(items)])
    whole[width:edge, :] = sum_of([tn(a[k][...], gy[k][...]) for k in range(items)])
    whole[edge:, :] = jnp.zeros((whole.shape[0] - edge, width), F32)
    whole[edge : edge + 8, :] = sum_of([v[...] for v in vecs])
    scatter_blocks(whole, keep_o, send_o)


def cross_backward(item, chunk, lengths, tasks, x2, s0, s1, s2, s3, og, gain, wo, wq, ka, va, q, o, lse, dx2_o, g2_o, dq_o, dk_o, dv_o, vec_o, keep_o, send_o, rest_o, whole, qa, doa, do):
    side = mp_side()
    grad_in = join_halves((s0, s1, s2, s3), side, whole)
    grad, gain_row, shift_row = norm_back(x2[...], line(gain), grad_in)
    total = upstream_rows(item, lengths, tasks, og) + grad
    dx2_o[...] = total
    low = total.astype(BF16)
    g2_o[...] = low
    do[...] = nt(wo[...], low).astype(BF16)
    attention_backward(q, ka, va, o, lse, do, qa, doa, dq_o, dk_o, dv_o, chunk, False)
    store_halves(tn(dq_o[...], wq[...]), side, keep_o, send_o, rest_o)
    pick = iota((8, vec_o.shape[1]), 0)
    out = jnp.where(pick == 0, gain_row, 0.0)
    out = jnp.where(pick == 1, shift_row, out)
    vec_o[...] = jnp.where(pick == 2, jnp.sum(total, axis=0, keepdims=True), out)
    vec_o[3:4, 0 : dq_o.shape[0]] = row_of_sums(dq_o[...])
    vec_o[4:5, 0 : dq_o.shape[0]] = row_of_sums(dv_o[...])


def memory_grad(wk, wv, dk, dv, keep_o, send_o):
    count = keep_o.shape[2]
    position = lax.axis_index("mp")
    rows = keep_o.shape[1]
    whole = (tn(wk[...], dk[...]) + tn(wv[...], dv[...])).astype(BF16)
    for block in range(4):
        piece = whole[block * rows : (block + 1) * rows, 0:count]
        relative = lax.bitwise_xor(position, block)
        slot = relative // 2

        @pl.when(relative % 2 == 0)
        def _():
            keep_o[slot] = piece

        @pl.when(relative % 2 == 1)
        def _():
            send_o[slot] = piece


def place_of(block):
    return (block % 2) * 4 + (block // 2 % 2) * 2 + block // 4 % 2


def scatter_blocks(whole, keep_o, send_o):
    position = lax.axis_index("dp") % 8
    rows = keep_o.shape[1]
    for block in range(8):
        place = place_of(lax.bitwise_xor(position, block))
        piece = whole[block * rows : (block + 1) * rows, :].astype(BF16)

        @pl.when(place < 4)
        def _():
            keep_o[place] = piece

        @pl.when(place >= 4)
        def _():
            send_o[place - 4] = piece


def gather_blocks(near, far, whole):
    position = lax.axis_index("dp") % 8
    rows = near.shape[1]
    for block in range(8):
        place = place_of(lax.bitwise_xor(position, block))
        spot = slice(block * rows, (block + 1) * rows)

        @pl.when(place < 4)
        def _():
            whole[spot, :] = near[place].astype(F32)

        @pl.when(place >= 4)
        def _():
            whole[spot, :] = far[place - 4].astype(F32)


def cross_weights(items, enc, *refs):
    dq, h2, o, g2, dk, dv, vecs = (refs[k * items : (k + 1) * items] for k in range(7))
    keep_o, send_o, whole = refs[7 * items :]
    rows = dq[0].shape[0]
    count = enc.shape[1]
    span = range(items)
    whole[0:rows, :] = sum_of([nn(dq[k][...], h2[k][...]) for k in span])
    whole[rows : 2 * rows, :] = sum_of([nn(dk[k][:, 0:count], enc[k]) for k in span])
    whole[2 * rows : 3 * rows, :] = sum_of([nn(dv[k][:, 0:count], enc[k]) for k in span])
    whole[3 * rows : 4 * rows, :] = sum_of([nn(o[k][...], g2[k][...]) for k in span])
    whole[4 * rows :, :] = jnp.zeros((whole.shape[0] - 4 * rows, whole.shape[1]), F32)
    whole[4 * rows : 4 * rows + 8, :] = sum_of([v[...] for v in vecs])
    scatter_blocks(whole, keep_o, send_o)


def self_backward(item, x1, s0, s1, s2, s3, dx2, x_ref, gain, wo, wq, wk, wv, ka, va, q, o, lse, dx1_o, g1_o, dqkv_o, vec_o, keep_o, send_o, rest_o, whole, qa, doa, do):
    side = mp_side()
    grad_in = join_halves((s0, s1, s2, s3), side, whole)
    grad, gain_row, shift_row = norm_back(x1[...], line(gain), grad_in)
    total = dx2[...] + grad
    dx1_o[...] = total
    low = total.astype(BF16)
    g1_o[...] = low
    do[...] = nt(wo[...], low).astype(BF16)
    rows = do.shape[0]
    dq_o = dqkv_o.at[0:rows]
    dk_o = dqkv_o.at[rows : 2 * rows]
    dv_o = dqkv_o.at[2 * rows : 3 * rows]
    attention_backward(q, ka, va, o, lse, do, qa, doa, dq_o, dk_o, dv_o, q.shape[1], True)
    part = tn(dq_o[...], wq[...]) + tn(dk_o[...], wk[...]) + tn(dv_o[...], wv[...])
    store_halves(part, side, keep_o, send_o, rest_o)
    unit, _ = norm_parts(x_ref[item].astype(F32))
    pick = iota((8, vec_o.shape[1]), 0)
    out = jnp.where(pick == 0, gain_row, 0.0)
    out = jnp.where(pick == 1, shift_row, out)
    out = jnp.where(pick == 2, jnp.sum(total, axis=0, keepdims=True), out)
    out = jnp.where(pick == 5, jnp.sum(part * unit, axis=0, keepdims=True), out)
    vec_o[...] = jnp.where(pick == 6, jnp.sum(part, axis=0, keepdims=True), out)
    vec_o[3:4, 0:rows] = row_of_sums(dq_o[...])
    vec_o[4:5, 0:rows] = row_of_sums(dv_o[...])


def self_weights(items, x_ref, gain, shift, *refs):
    dqkv, o, g1, vecs = (refs[k * items : (k + 1) * items] for k in range(4))
    keep_o, send_o, whole = refs[4 * items :]
    rows = o[0].shape[0]
    span = range(items)
    normed = []
    for k in span:
        unit, _ = norm_parts(x_ref[k].astype(F32))
        normed.append((unit * line(gain) + line(shift)).astype(BF16))
    whole[0 : 3 * rows, :] = sum_of([nn(dqkv[k][...], normed[k]) for k in span])
    whole[3 * rows : 4 * rows, :] = sum_of([nn(o[k][...], g1[k][...]) for k in span])
    whole[4 * rows :, :] = jnp.zeros((whole.shape[0] - 4 * rows, whole.shape[1]), F32)
    whole[4 * rows : 4 * rows + 8, :] = sum_of([v[...] for v in vecs])
    scatter_blocks(whole, keep_o, send_o)


def unpack(near, far, *rest):
    outs, whole = rest[:-1], rest[-1]
    gather_blocks(near, far, whole)
    start = 0
    for out in outs:
        out[...] = whole[start : start + out.shape[0], :]
        start += out.shape[0]


def finish_out(items, *refs):
    x2, pieces, (bias, out, whole) = refs[:items], refs[items : items + 4], refs[items + 4 :]
    for k in range(items):
        total = x2[k][...] + join_halves([p.at[k] for p in pieces], mp_side(), whole) + line(bias)
        out[k] = total.astype(BF16)


def finish_grad(item, dx1, s0, s1, s2, s3, x_ref, gain, *rest):
    out, whole = rest[-2:]
    grad_in = join_halves((s0, s1, s2, s3), mp_side(), whole)
    grad, _, _ = norm_back(x_ref[item].astype(F32), line(gain), grad_in)
    out[...] = dx1[...] + grad


def finish_memory(kept, far, out):
    for k in range(kept.shape[0]):
        out[k] = kept[k].astype(F32) + far[k].astype(F32)


def both(left, right):
    return (left.astype(F32) + right.astype(F32)).astype(BF16)


def add_rows(left, right, out):
    out[...] = both(left[...], right[...])


def add_parts(left, *rest):
    parts, out = rest[:-1], rest[-1]
    start = 0
    for part in parts:
        spot = slice(start, start + part.shape[0])
        out[spot] = both(left[spot], part[...])
        start += part.shape[0]


def add_stack(count, *refs):
    out = refs[-1]
    each = (len(refs) - 1) // count
    for k in range(count):
        add_parts(*refs[k * each : (k + 1) * each], out.at[k])


def add_memory(count, *refs):
    left, right, (kept, sent) = refs[:count], refs[count : 2 * count], refs[2 * count :]
    for k in range(count):
        kept[k] = both(left[k][0], right[k][0])
        sent[k] = both(left[k][1], right[k][1])


def add_split(left, right, keep, send):
    half = keep.shape[0]
    keep[...] = both(left[0:half], right[0:half])
    send[...] = both(left[half:], right[half:])


def stack_pair(left, right, out):
    half = left.shape[0]
    out[0:half] = left[...]
    out[half:] = right[...]


SCALARS = pl.BlockSpec(memory_space=pltpu.SMEM)
LEFT = pl.BlockSpec(memory_space=pl.ANY)
AWAY = pl.BlockSpec(memory_space=pltpu.HBM)
NEAR = pl.BlockSpec(memory_space=pltpu.VMEM)
FAR = pl.BlockSpec(memory_space=pltpu.VMEM)


def chosen(array, item):
    rest = (0,) * (len(array.shape) - 1)
    return pl.BlockSpec((None,) + tuple(array.shape[1:]), lambda *_: (item,) + rest)


def shape(dims, dtype):
    return jax.ShapeDtypeStruct(dims, dtype)


def near_shape(dims, dtype=BF16):
    return pltpu.VMEM(dims, dtype)


def near_like(array, dims=None):
    return pltpu.VMEM(tuple(dims or array.shape), array.dtype)


class Order:
    def __init__(self):
        self.tick = None

    def run(self, body, cost, operands, outs, scratch=(), specs=None, out_specs=None, aliases=None):
        specs = specs or {}
        placed, in_specs = [], []
        for k, array in enumerate(operands):
            spec = specs.get(k, SCALARS if array.dtype == jnp.int32 else NEAR)
            if spec is NEAR:
                array = pltpu.with_memory_space_constraint(array, pltpu.VMEM)
            elif spec is AWAY:
                array = pltpu.with_memory_space_constraint(array, pltpu.HBM)
            placed.append(array)
            in_specs.append(spec)
        count = len(placed)
        if self.tick is not None:
            placed.append(pltpu.with_memory_space_constraint(self.tick, pltpu.VMEM))
            in_specs.append(NEAR)
        given, made = len(placed), len(outs)

        def whole_body(*refs):
            tick = refs[given + made]
            tick[...] = jnp.zeros(tick.shape, tick.dtype)
            body(*refs[:count], *refs[given : given + made], *refs[given + made + 1 :])

        inner = body
        while isinstance(inner, functools.partial):
            inner = inner.func
        results = pl.pallas_call(
            whole_body,
            name=inner.__name__,
            grid=(1,),
            in_specs=in_specs,
            out_specs=list(out_specs or [NEAR] * made) + [NEAR],
            out_shape=list(outs) + [near_shape((8, 128), F32)],
            scratch_shapes=list(scratch),
            input_output_aliases=aliases or {},
            cost_estimate=pl.CostEstimate(flops=int(cost * COST), transcendentals=0, bytes_accessed=1),
            compiler_params=pltpu.CompilerParams(vmem_limit_bytes=VMEM_BYTES),
        )(*placed)
        self.tick = results[-1]
        return results[:-1]


def swap(value, axis, size, bit):
    return lax.ppermute(value, axis, [(k, k ^ bit) for k in range(size)])


class MpSum:
    def __init__(self, order, size, keep, *sends):
        self.order, self.size, self.keep = order, size, keep
        self.near = [swap(send, "mp", size, 1) for send in sends]

    def add(self):
        own = self.order.run(add_parts, 0.5, (self.keep, *self.near), (near_like(self.keep),))[0]
        self.spread(own)

    def spread(self, own):
        self.own = own
        self.far = swap(own, "mp", self.size, 2)
        self.other = swap(own, "mp", self.size, 1)

    def pieces(self):
        far = self.far
        if self.order.tick is not None:
            far = lax.optimization_barrier((far, self.order.tick))[0]
        return self.own, far, self.other, swap(far, "mp", self.size, 1)


class DpSum:
    def __init__(self, order, size, keep, send):
        self.order, self.size = order, size
        self.keep, self.near = keep, swap(send, "dp", size, 1)
        self.stage = 0

    def step(self):
        dims = self.keep.shape
        if self.stage < 2:
            out = near_like(self.keep, (dims[0] // 2,) + dims[1:])
            self.keep, send = self.order.run(add_split, 0.7, (self.keep, self.near), (out, out))
            self.near = swap(send, "dp", self.size, 2 << self.stage)
        elif self.stage == 2:
            self.keep = self.order.run(add_rows, 0.5, (self.keep, self.near), (near_like(self.keep),))[0]
            bit = 8
            while bit < self.size:
                other = swap(self.keep, "dp", self.size, bit)
                self.keep = self.order.run(add_rows, 0.5, (self.keep, other), (near_like(self.keep),))[0]
                bit *= 2
            self.near = swap(self.keep, "dp", self.size, 4)
        else:
            out = near_like(self.keep, (dims[0] * 2,) + dims[1:])
            self.keep = self.order.run(stack_pair, 0.5, (self.keep, self.near), (out,))[0]
            self.near = swap(self.keep, "dp", self.size, 2 if self.stage == 3 else 1)
        self.stage += 1

    def unpack(self, outs):
        rows = 8 * self.keep.shape[1]
        specs = [pl.BlockSpec(o.shape, lambda *_: (0, 0)) for o in outs]
        return self.order.run(
            unpack, 3, (self.keep, self.near), outs, (pltpu.VMEM((rows, outs[0].shape[1]), F32),), None, specs
        )


def shards(sizes, *arguments):
    (
        hidden, encoder, lengths, tasks, frames, out_grad,
        gain_self, shift_self, query_self, qbias_self, key_self, value_self, vbias_self, output_self, obias_self,
        gain_cross, shift_cross, query_cross, qbias_cross, key_cross, value_cross, vbias_cross, output_cross, obias_cross,
        gain_feed, shift_feed, expand_weight, expand_bias, contract_weight, contract_bias,
    ) = arguments
    n_mp, n_dp = sizes["mp"], sizes["dp"]
    items, length, width = hidden.shape
    memory_len = encoder.shape[1]
    rows = query_self.shape[1]
    heads = rows // HEAD
    units = expand_weight.shape[1]
    wide = -(-memory_len // 512) * 512
    chunk = 512
    half = length // 2
    wq1, wk1, wv1 = query_self.T, key_self.T, value_self.T
    wq2, wk2, wv2 = query_cross.T, key_cross.T, value_cross.T

    low_rows = near_shape((rows, length))
    mem_rows = near_shape((rows, wide))
    half_outs = (near_shape((half, width)), near_shape((half // 2, width)), near_shape((half - half // 2, width)))
    state = near_shape((length, width), F32)
    low_state = near_shape((length, width))
    unit_state = near_shape((length, units))
    vec_out = near_shape((8, width), F32)
    lse_out = near_shape((8, length), F32)
    aug_out = near_shape((heads, AUG, length))
    aug_mem = near_shape((heads, AUG, wide))
    mem_half = near_shape((2, rows, memory_len))
    whole = pltpu.VMEM((length, width), F32)
    aug = pltpu.VMEM((AUG, length), BF16)
    row_scratch = pltpu.VMEM((rows, length), BF16)
    span = range(items)
    bind = functools.partial
    order = Order()

    def mp_sum(*parts):
        return MpSum(order, n_mp, *parts)

    def pack_outs(count):
        return (near_shape((4, count // 8, width)),) * 2, (pltpu.VMEM((count, width), F32),)

    def keys(i):
        return order.run(
            bind(cross_keys, i), 3, (frames, encoder, wk2, wv2, vbias_cross),
            (aug_mem, aug_mem), (), {1: chosen(encoder, i)},
        )

    self_out, self_sum, cross_kv = [], [], []
    loads = (
        hidden, gain_self, shift_self, wq1, qbias_self, wk1, wv1, vbias_self, output_self,
        wk2, wv2, vbias_cross, obias_self, gain_cross, shift_cross, wq2, qbias_cross, output_cross,
        out_grad, obias_cross, gain_feed, shift_feed, expand_weight, expand_bias, contract_weight, contract_bias,
    )
    self_outs = (low_rows, aug_out, aug_out, low_rows, lse_out, *half_outs)
    for i in span:
        if i == 0:
            out = order.run(
                bind(first_forward, i, 9, len(loads)), 4, (lengths, *loads),
                self_outs + tuple(near_like(a) for a in loads), (aug, pltpu.SemaphoreType.DMA((len(loads),))),
                {k + 1: AWAY for k in range(len(loads))},
            )
            near = out[8:]
            hidden, gain_self, shift_self, wq1, qbias_self, wk1, wv1, vbias_self, output_self = near[:9]
            wk2, wv2, vbias_cross, obias_self, gain_cross, shift_cross, wq2, qbias_cross, output_cross = near[9:18]
            out_grad, obias_cross, gain_feed, shift_feed, expand_weight, expand_bias, contract_weight, contract_bias = near[18:]
        else:
            operands = (lengths, hidden, gain_self, shift_self, wq1, qbias_self, wk1, wv1, vbias_self, output_self)
            out = order.run(bind(self_forward, i), 4, operands, self_outs, (aug,))
        self_out.append(out)
        self_sum.append(mp_sum(*out[5:8]))
    for i in span:
        self_sum[i].add()
        if i == 0:
            cross_kv.append(keys(0))

    cross_out, cross_sum = [], []
    for i in span:
        out = order.run(
            bind(cross_forward, i, chunk), 6,
            (hidden, *self_sum[i].pieces(), obias_self, gain_cross, shift_cross, wq2, qbias_cross, output_cross, *cross_kv[i]),
            (state, low_state, low_rows, low_rows, lse_out, *half_outs), (whole, aug),
        )
        cross_out.append(out)
        cross_sum.append(mp_sum(*out[5:8]))
        if len(cross_kv) < items:
            cross_kv.append(keys(i + 1))
        cross_sum[i].add()

    feed_out, feed_sum, block_sum = [], [], []
    for i in span:
        out = order.run(
            bind(feed, i), 4,
            (lengths, tasks, cross_out[i][0], *cross_sum[i].pieces(), out_grad, obias_cross, gain_feed, shift_feed, expand_weight, expand_bias, contract_weight),
            (state, low_state, unit_state, unit_state, low_state, vec_out, *half_outs), (whole,),
        )
        feed_out.append(out)
        feed_sum.append(mp_sum(*out[6:9]))
        block_sum.append(mp_sum(*order.run(feed_out_part, 1, (out[2], contract_weight), half_outs)))
        feed_sum[i].add()
    outs, scratch = pack_outs(width + units + 64)
    feed_dp = DpSum(
        order, n_dp, *order.run(
            bind(feed_weights, items), 4, [out[k] for k in (1, 3, 2, 4, 5) for out in feed_out], outs, scratch
        )
    )

    back_out, back_sum, memory_parts = [], [], []
    for i in span:
        _, _, q2, o2, lse2 = cross_out[i][:5]
        out = order.run(
            bind(cross_backward, i, chunk), 9,
            (lengths, tasks, feed_out[i][0], *feed_sum[i].pieces(), out_grad, gain_feed, output_cross, wq2, *cross_kv[i], q2, o2, lse2),
            (state, low_state, low_rows, mem_rows, mem_rows, vec_out, *half_outs), (whole, aug, aug, row_scratch),
        )
        back_out.append(out)
        back_sum.append(mp_sum(*out[6:9]))
        keep, send = order.run(memory_grad, 2, (wk2, wv2, out[3], out[4]), (mem_half, mem_half))
        memory_parts.append((keep, swap(send, "mp", n_mp, 1)))
        back_sum[i].add()
    feed_dp.step()

    self_back, last_sum = [], []
    for i in span:
        q1, ka1, va1, o1, lse1 = self_out[i][:5]
        out = order.run(
            bind(self_backward, i), 5,
            (cross_out[i][0], *back_sum[i].pieces(), back_out[i][0], hidden, gain_cross, output_self, wq1, wk1, wv1, ka1, va1, q1, o1, lse1),
            (state, low_state, near_shape((3 * rows, length)), vec_out, *half_outs), (whole, aug, aug, row_scratch),
        )
        self_back.append(out)
        last_sum.append(mp_sum(*out[4:7]))
        outs, scratch = pack_outs(4 * rows + 64)
        if i == 0:
            operands = [encoder] + [out[2] for out in back_out] + [out[1] for out in cross_out] + [out[3] for out in cross_out]
            operands += [out[1] for out in back_out] + [out[3] for out in back_out] + [out[4] for out in back_out]
            operands += [out[5] for out in back_out]
            cross_dp = DpSum(
                order, n_dp, *order.run(
                    bind(cross_weights, items), 3, operands, outs, scratch,
                    {0: pl.BlockSpec(encoder.shape, lambda *_: (0, 0, 0))},
                )
            )
            last_sum[i].add()
            feed_dp.step()
        if i == items - 1:
            operands = [hidden, gain_self, shift_self] + [out[2] for out in self_back] + [out[3] for out in self_out]
            operands += [out[1] for out in self_back] + [out[3] for out in self_back]
            self_dp = DpSum(order, n_dp, *order.run(bind(self_weights, items), 3, operands, outs, scratch))
        if i > 0:
            last_sum[i].add()

    feed_dp.step()
    cross_dp.step()
    block_half = near_shape((items, half, width))
    stacked = order.run(
        bind(add_stack, items), 1, [a for s in block_sum for a in (s.keep, *s.near)], (block_half,)
    )[0]
    block_sum[0].spread(stacked)
    memory_out = near_shape((items, rows, memory_len))
    kept, sent = order.run(
        bind(add_memory, items), 1, [p[0] for p in memory_parts] + [p[1] for p in memory_parts], (memory_out, memory_out)
    )
    memory_far = swap(sent, "mp", n_mp, 2)
    cross_dp.step()
    hidden_grad = None
    grad_shape = shape(hidden.shape, F32)
    for i in span:
        extra = () if hidden_grad is None else (hidden_grad,)
        hidden_grad = order.run(
            bind(finish_grad, i), 2,
            (self_back[i][0], *last_sum[i].pieces(), hidden, gain_self, *extra), (grad_shape,), (whole,),
            {7: LEFT}, [chosen(grad_shape, i)], {7: 0} if extra else {},
        )[0]
    self_dp.step()
    feed_dp.step()
    cross_dp.step()
    self_dp.step()
    block_shape = shape(hidden.shape, BF16)
    block_out = order.run(
        bind(finish_out, items), 3, [out[0] for out in feed_out] + list(block_sum[0].pieces()) + [contract_bias],
        (block_shape,), (whole,), None, [pl.BlockSpec(hidden.shape, lambda *_: (0, 0, 0))],
    )[0]
    feed_dp.step()
    cross_dp.step()
    self_dp.step()
    encoder_grad = order.run(
        finish_memory, 2, (kept, memory_far), (shape((items, rows, memory_len), F32),), (), None,
        [pl.BlockSpec((items, rows, memory_len), lambda *_: (0, 0, 0))],
    )[0].transpose(0, 2, 1)
    cross_dp.step()
    self_dp.step()
    self_dp.step()

    matrix = shape((rows, width), F32)
    outs = (matrix, matrix, matrix, matrix, shape((8, width), F32))
    feed_grads = feed_dp.unpack((shape((width, width), F32), shape((units, width), F32), shape((8, width), F32)))
    cross_grads = cross_dp.unpack(outs)
    self_grads = self_dp.unpack(outs)
    norm_rows = self_grads[4]
    norm_rows = norm_rows + swap(norm_rows, "mp", n_mp, 1)
    norm_rows = norm_rows + swap(norm_rows, "mp", n_mp, 2)
    return (
        block_out,
        hidden_grad,
        encoder_grad,
        norm_rows[5],
        norm_rows[6],
        self_grads[0].T,
        self_grads[4][3, 0:rows],
        self_grads[1].T,
        self_grads[2].T,
        self_grads[4][4, 0:rows],
        self_grads[3],
        self_grads[4][2],
        self_grads[4][0],
        self_grads[4][1],
        cross_grads[0].T,
        cross_grads[4][3, 0:rows],
        cross_grads[1].T,
        cross_grads[2].T,
        cross_grads[4][4, 0:rows],
        cross_grads[3],
        cross_grads[4][2],
        cross_grads[4][0],
        cross_grads[4][1],
        feed_grads[0],
        feed_grads[2][1],
        feed_grads[1],
        feed_grads[2][0],
    )


def solution(mesh):
    column, row, flat = P(None, "mp"), P("mp", None), P("mp")
    cube = P("dp", None, None)
    attention = (P(), P(), column, flat, column, column, flat, row, P())
    grads = (P(), P(), column, flat, column, column, flat, row, P())
    return jax.shard_map(
        functools.partial(shards, dict(mesh.shape)),
        mesh=mesh,
        in_specs=(cube, cube, P("dp"), P("dp"), P("dp"), cube)
        + attention
        + attention
        + (P(), P(), column, flat, row, P()),
        out_specs=(cube, cube, P("dp", None, "mp")) + grads + grads + (P(), P(), column, flat, row, P()),
        check_vma=False,
    )
```

```python
import functools
import math

import jax
import jax.numpy as jnp
from jax import lax
from jax.experimental import pallas as pl
from jax.experimental.pallas import tpu as pltpu
from jax.sharding import PartitionSpec as P

HEAD = 64
AUG = 80
EPS = 1e-05
NEG = -1e30
F32 = jnp.float32
BF16 = jnp.bfloat16
ROOT_HALF = math.sqrt(0.5)
INV_ROOT_TAU = 1.0 / math.sqrt(2.0 * math.pi)
VMEM_BYTES = 20 * 1024 * 1024
COST = 1
ORDER = ("P", "AB", "FXl", "M", "a", "FXSm", "N", "b", "FXS", "ge", "FXSc", "XS", "u", "S", "v", "o", "w")


def dot(left, right, left_dim, right_dim):
    return lax.dot_general(
        left, right, (((left_dim,), (right_dim,)), ((), ())), preferred_element_type=F32
    )


def nn(left, right):
    return dot(left, right, 1, 0)


def nt(left, right):
    return dot(left, right, 1, 1)


def tn(left, right):
    return dot(left, right, 0, 0)


def iota(shape, axis):
    return lax.broadcasted_iota(jnp.int32, shape, axis)


def norm_parts(values):
    centred = values - jnp.mean(values, axis=-1, keepdims=True)
    spread = jnp.mean(centred * centred, axis=-1, keepdims=True)
    scale = lax.rsqrt(spread + EPS)
    return centred * scale, scale


def norm_back(values, gain, upstream):
    unit, scale = norm_parts(values)
    inner = upstream * gain
    first = jnp.mean(inner, axis=-1, keepdims=True)
    second = jnp.mean(inner * unit, axis=-1, keepdims=True)
    grad = scale * (inner - first - unit * second)
    return (
        grad,
        jnp.sum(upstream * unit, axis=0, keepdims=True),
        jnp.sum(upstream, axis=0, keepdims=True),
    )


def line(ref):
    return ref[...].astype(F32).reshape(1, ref.shape[0])


def column_bias(ref, count):
    first = jnp.where(iota((16, ref.shape[0]), 0) == 0, line(ref), 0.0).astype(BF16)
    return tn(first, jnp.ones((16, count), BF16))


def mp_side():
    return lax.axis_index("mp") % 2


def key_extra(count, limit):
    rows = iota((16, count), 0)
    hidden_keys = jnp.where(iota((16, count), 1) < limit, 0.0, NEG)
    ones = jnp.where(rows < 4, 1.0, 0.0)
    return jnp.where(rows == 0, hidden_keys, ones).astype(BF16)


def value_extra(count):
    return jnp.where(iota((16, count), 0) < 3, 1.0, 0.0).astype(BF16)


def three_parts(row):
    high = row.astype(BF16)
    rest = row - high.astype(F32)
    middle = rest.astype(BF16)
    last = (rest - middle.astype(F32)).astype(BF16)
    return high.astype(F32), middle.astype(F32), last.astype(F32)


def split_rows(rows, row, first, with_one):
    high, middle, last = three_parts(row)
    base = jnp.where(rows == 0, 1.0, 0.0) if with_one else jnp.zeros(rows.shape, F32)
    out = jnp.where(rows == first, high, base)
    out = jnp.where(rows == first + 1, middle, out)
    return jnp.where(rows == first + 2, last, out).astype(BF16)


def store_halves(part, side, keep_ref, send_ref, rest_ref=None):
    half = part.shape[0] // 2
    edge = send_ref.shape[0]
    low = part.astype(BF16)

    @pl.when(side == 0)
    def _():
        keep_ref[...] = low[:half]
        send_ref[...] = low[half : half + edge]
        if rest_ref is not None:
            rest_ref[...] = low[half + edge :]

    @pl.when(side == 1)
    def _():
        keep_ref[...] = low[half:]
        send_ref[...] = low[:edge]
        if rest_ref is not None:
            rest_ref[...] = low[edge:half]


def join_halves(pieces, side, scratch):
    own, other = pieces
    half = own.shape[0]
    scratch[pl.ds(pl.multiple_of(side * half, 16), half), :] = own[...].astype(F32)
    scratch[pl.ds(pl.multiple_of((1 - side) * half, 16), half), :] = other[...].astype(F32)
    return scratch[...]


def attend_block(keys, queries, keep):
    scores = tn(keys, queries)
    if keep is not None:
        scores = jnp.where(keep, scores, NEG)
    return scores


def causal_mask(count):
    return iota((count, count), 0) <= iota((count, count), 1)


def attention_forward(q_ref, ka_ref, va_ref, qa, o_ref, lse_ref, chunk, causal):
    heads, _, keys = ka_ref.shape
    count = q_ref.shape[1]
    rows = iota((16, count), 0)
    qa[HEAD:AUG, :] = jnp.where(rows == 0, 1.0, 0.0).astype(BF16)
    keep = causal_mask(count) if causal else None
    lse_rows = iota((8, count), 0)
    lse = jnp.zeros((8, count), F32)
    for head in range(heads):
        spot = slice(head * HEAD, (head + 1) * HEAD)
        qa[0:HEAD, :] = q_ref[spot, :]
        queries = qa[...]
        largest = None
        for start in range(0, keys, chunk):
            part = slice(start, start + chunk)
            scores = attend_block(ka_ref[head, :, part], queries, keep)
            top = jnp.max(scores, axis=0, keepdims=True)
            if largest is None:
                powers = jnp.exp(scores - top).astype(BF16)
                mixed = nn(va_ref[head, :, part], powers)
                largest = top
            else:
                newer = jnp.maximum(largest, top)
                powers = jnp.exp(scores - newer).astype(BF16)
                mixed = mixed * jnp.exp(largest - newer) + nn(va_ref[head, :, part], powers)
                largest = newer
        total = mixed[HEAD : HEAD + 1]
        o_ref[spot, :] = (mixed[0:HEAD] / total).astype(BF16)
        lse = jnp.where(lse_rows == head, largest + jnp.log(total), lse)
    lse_ref[...] = lse


def attention_backward(
    q_ref, ka_ref, va_ref, o_ref, lse_ref, do_ref, qa, doa, dq_ref, dk_ref, dv_ref, chunk, causal
):
    heads, _, keys = ka_ref.shape
    count = q_ref.shape[1]
    rows = iota((16, count), 0)
    keep = causal_mask(count) if causal else None
    for head in range(heads):
        spot = slice(head * HEAD, (head + 1) * HEAD)
        queries = q_ref[spot, :]
        mix_grad = do_ref[spot, :]
        qa[0:HEAD, :] = queries
        doa[0:HEAD, :] = mix_grad
        qa[HEAD:AUG, :] = split_rows(rows, -lse_ref[head : head + 1, :], 1, True)
        centre = jnp.sum(
            mix_grad.astype(F32) * o_ref[spot, :].astype(F32), axis=0, keepdims=True
        )
        doa[HEAD:AUG, :] = split_rows(rows, -centre, 0, False)
        query_side = qa[...]
        grad_side = doa[...]
        query_grad = jnp.zeros((HEAD, count), F32)
        for start in range(0, keys, chunk):
            part = slice(start, start + chunk)
            shares = jnp.exp(attend_block(ka_ref[head, :, part], query_side, keep))
            pushed = tn(va_ref[head, :, part], grad_side)
            score_grad = (shares * pushed).astype(BF16)
            dv_ref[spot, part] = nt(mix_grad, shares.astype(BF16)).astype(BF16)
            dk_ref[spot, part] = nt(queries, score_grad).astype(BF16)
            query_grad = query_grad + nn(ka_ref[head, 0:HEAD, part], score_grad)
        dq_ref[spot, :] = (query_grad * 0.125).astype(BF16)


def row_of_sums(matrix):
    ones = jnp.ones((16, matrix.shape[1]), BF16)
    return nt(ones, matrix)[0:1]


def self_forward(item, lengths, x_ref, gain, shift, wq, qbias, wk, wv, vbias, wo, q_o, ka_o, va_o, o_o, lse_o, keep_o, send_o, rest_o, qa):
    count = x_ref.shape[1]
    unit, _ = norm_parts(x_ref[item].astype(F32))
    normed = (unit * line(gain) + line(shift)).astype(BF16)
    queries = (nt(wq[...], normed) + column_bias(qbias, count)).astype(BF16)
    q_o[...] = queries * jnp.asarray(0.125, BF16)
    key_rows = nt(wk[...], normed).astype(BF16)
    value_rows = (nt(wv[...], normed) + column_bias(vbias, count)).astype(BF16)
    extra = key_extra(count, lengths[item])
    other = value_extra(count)
    for head in range(ka_o.shape[0]):
        spot = slice(head * HEAD, (head + 1) * HEAD)
        ka_o[head, 0:HEAD, :] = key_rows[spot]
        ka_o[head, HEAD:AUG, :] = extra
        va_o[head, 0:HEAD, :] = value_rows[spot]
        va_o[head, HEAD:AUG, :] = other
    attention_forward(q_o, ka_o, va_o, qa, o_o, lse_o, count, True)
    store_halves(tn(o_o[...], wo[...]), mp_side(), keep_o, send_o, rest_o)


def first_forward(item, first, count, lengths, *refs):
    sources, targets = refs[:count], refs[count + 8 : 2 * count + 8]
    outs, qa, sems = refs[count : count + 8], refs[-2], refs[-1]
    copies = [pltpu.make_async_copy(s, t, sems.at[k]) for k, (s, t) in enumerate(zip(sources, targets))]
    for copy in copies:
        copy.start()
    for copy in copies[:first]:
        copy.wait()
    self_forward(item, lengths, *targets[:first], *outs, qa)
    for copy in copies[first:]:
        copy.wait()


def cross_keys(item, frames, enc, wk, wv, vbias, ka_o, va_o):
    count = enc.shape[0]
    wide = ka_o.shape[2]
    memory = enc[...]
    key_rows = nt(wk[...], memory).astype(BF16)
    value_rows = (nt(wv[...], memory) + column_bias(vbias, count)).astype(BF16)
    extra = key_extra(wide, frames[item])
    other = value_extra(wide)
    for head in range(ka_o.shape[0]):
        spot = slice(head * HEAD, (head + 1) * HEAD)
        if wide > count:
            ka_o[head, 0:HEAD, wide - 128 :] = jnp.zeros((HEAD, 128), BF16)
            va_o[head, 0:HEAD, wide - 128 :] = jnp.zeros((HEAD, 128), BF16)
        ka_o[head, 0:HEAD, 0:count] = key_rows[spot]
        ka_o[head, HEAD:AUG, :] = extra
        va_o[head, 0:HEAD, 0:count] = value_rows[spot]
        va_o[head, HEAD:AUG, :] = other


def cross_forward(item, chunk, x_ref, s0, s1, obias, gain, shift, wq, qbias, wo, ka, va, x1_o, h2_o, q_o, o_o, lse_o, keep_o, send_o, rest_o, whole, qa):
    count = x_ref.shape[1]
    side = mp_side()
    after = x_ref[item].astype(F32) + join_halves((s0, s1), side, whole) + line(obias)
    x1_o[...] = after
    unit, _ = norm_parts(after)
    normed = (unit * line(gain) + line(shift)).astype(BF16)
    h2_o[...] = normed
    queries = (nt(wq[...], normed) + column_bias(qbias, count)).astype(BF16)
    q_o[...] = queries * jnp.asarray(0.125, BF16)
    attention_forward(q_o, ka, va, qa, o_o, lse_o, chunk, False)
    store_halves(tn(o_o[...], wo[...]), side, keep_o, send_o, rest_o)


def upstream_rows(item, lengths, tasks, og):
    task = tasks[item]
    weight = jnp.where(task == 0, 1.0, jnp.where(task == 1, 0.6, 2.0)).astype(F32)
    valid = iota((og.shape[1], 1), 0) < lengths[item]
    return og[item].astype(F32) * jnp.where(valid, weight, 0.0)


def feed(item, lengths, tasks, x1, s0, s1, og, obias, gain, shift, we, ebias, wc, x2_o, h3_o, a_o, dz_o, gy_o, vec_o, bkeep_o, bsend_o, brest_o, whole):
    side = mp_side()
    after = x1[...] + join_halves((s0, s1), side, whole) + line(obias)
    x2_o[...] = after
    unit, _ = norm_parts(after)
    normed = (unit * line(gain) + line(shift)).astype(BF16)
    h3_o[...] = normed
    before = nn(normed, we[...]) + line(ebias)
    share = 0.5 + 0.5 * lax.erf(before * ROOT_HALF)
    active = (before * share).astype(BF16)
    a_o[...] = active
    slope = share + before * (jnp.exp(before * before * -0.5) * INV_ROOT_TAU)
    grad = upstream_rows(item, lengths, tasks, og)
    low = grad.astype(BF16)
    gy_o[...] = low
    inner = (nt(low, wc[...]) * slope).astype(BF16)
    dz_o[...] = inner
    store_halves(nt(inner, we[...]), side, bkeep_o, bsend_o, brest_o)
    pick = iota((8, vec_o.shape[1]), 0)
    out = jnp.where(pick == 0, jnp.sum(grad, axis=0, keepdims=True), 0.0)
    vec_o[...] = jnp.where(pick == 1, jnp.sum(inner.astype(F32), axis=0, keepdims=True), out)


def feed_out_part(active, wc, keep_o, send_o):
    store_halves(nn(active[...], wc[...]), mp_side(), keep_o, send_o)


def sum_of(refs):
    out = refs[0]
    for other in refs[1:]:
        out = out + other
    return out


def feed_weights(items, *refs):
    h3, dz, a, gy, vecs = (refs[k * items : (k + 1) * items] for k in range(5))
    keep_o, send_o, whole = refs[5 * items :]
    width = h3[0].shape[1]
    edge = width + dz[0].shape[1]
    whole[0:width, :] = sum_of([tn(h3[k][...], dz[k][...]) for k in range(items)])
    whole[width:edge, :] = sum_of([tn(a[k][...], gy[k][...]) for k in range(items)])
    whole[edge:, :] = jnp.zeros((whole.shape[0] - edge, width), F32)
    whole[edge : edge + 8, :] = sum_of([v[...] for v in vecs])
    scatter_blocks(whole, keep_o, send_o, X_FIRST)


def cross_backward(item, chunk, lengths, tasks, x2, s0, s1, og, gain, wo, wq, ka, va, q, o, lse, dx2_o, g2_o, dq_o, dk_o, dv_o, vec_o, keep_o, send_o, rest_o, whole, qa, doa, do):
    side = mp_side()
    grad_in = join_halves((s0, s1), side, whole)
    grad, gain_row, shift_row = norm_back(x2[...], line(gain), grad_in)
    total = upstream_rows(item, lengths, tasks, og) + grad
    dx2_o[...] = total
    low = total.astype(BF16)
    g2_o[...] = low
    do[...] = nt(wo[...], low).astype(BF16)
    attention_backward(q, ka, va, o, lse, do, qa, doa, dq_o, dk_o, dv_o, chunk, False)
    store_halves(tn(dq_o[...], wq[...]), side, keep_o, send_o, rest_o)
    pick = iota((8, vec_o.shape[1]), 0)
    out = jnp.where(pick == 0, gain_row, 0.0)
    out = jnp.where(pick == 1, shift_row, out)
    vec_o[...] = jnp.where(pick == 2, jnp.sum(total, axis=0, keepdims=True), out)
    vec_o[3:4, 0 : dq_o.shape[0]] = row_of_sums(dq_o[...])
    vec_o[4:5, 0 : dq_o.shape[0]] = row_of_sums(dv_o[...])


def memory_grad(wk, wv, dk, dv, keep_o, send_o):
    count = keep_o.shape[2]
    position = lax.axis_index("mp")
    rows = keep_o.shape[1]
    whole = (tn(wk[...], dk[...]) + tn(wv[...], dv[...])).astype(BF16)
    for block in range(4):
        piece = whole[block * rows : (block + 1) * rows, 0:count]
        relative = lax.bitwise_xor(position, block)
        slot = relative // 2

        @pl.when(relative % 2 == 0)
        def _():
            keep_o[slot] = piece

        @pl.when(relative % 2 == 1)
        def _():
            send_o[slot] = piece


X_FIRST = (1, 2, 4)
Z_FIRST = (2, 4, 1)


def place_of(block, steps):
    place = 0
    for bit in steps:
        place = place * 2 + block // bit % 2
    return place


def scatter_blocks(whole, keep_o, send_o, steps):
    position = lax.axis_index("dp") % 8
    rows = keep_o.shape[1]
    for block in range(8):
        place = place_of(lax.bitwise_xor(position, block), steps)
        piece = whole[block * rows : (block + 1) * rows, :].astype(BF16)

        @pl.when(place < 4)
        def _():
            keep_o[place] = piece

        @pl.when(place >= 4)
        def _():
            send_o[place - 4] = piece


def gather_blocks(near, far, whole, steps):
    position = lax.axis_index("dp") % 8
    rows = near.shape[1]
    for block in range(8):
        place = place_of(lax.bitwise_xor(position, block), steps)
        spot = slice(block * rows, (block + 1) * rows)

        @pl.when(place < 4)
        def _():
            whole[spot, :] = near[place].astype(F32)

        @pl.when(place >= 4)
        def _():
            whole[spot, :] = far[place - 4].astype(F32)


def cross_weights(items, enc, *refs):
    dq, h2, o, g2, dk, dv, vecs = (refs[k * items : (k + 1) * items] for k in range(7))
    keep_o, send_o, whole = refs[7 * items :]
    rows = dq[0].shape[0]
    count = enc.shape[1]
    span = range(items)
    whole[0:rows, :] = sum_of([nn(dq[k][...], h2[k][...]) for k in span])
    whole[rows : 2 * rows, :] = sum_of([nn(dk[k][:, 0:count], enc[k]) for k in span])
    whole[2 * rows : 3 * rows, :] = sum_of([nn(dv[k][:, 0:count], enc[k]) for k in span])
    whole[3 * rows : 4 * rows, :] = sum_of([nn(o[k][...], g2[k][...]) for k in span])
    whole[4 * rows :, :] = jnp.zeros((whole.shape[0] - 4 * rows, whole.shape[1]), F32)
    whole[4 * rows : 4 * rows + 8, :] = sum_of([v[...] for v in vecs])
    scatter_blocks(whole, keep_o, send_o, X_FIRST)


def self_backward(item, x1, s0, s1, dx2, x_ref, gain, wo, wq, wk, wv, ka, va, q, o, lse, dx1_o, g1_o, dqkv_o, vec_o, keep_o, send_o, whole, qa, doa, do):
    side = mp_side()
    grad_in = join_halves((s0, s1), side, whole)
    grad, gain_row, shift_row = norm_back(x1[...], line(gain), grad_in)
    total = dx2[...] + grad
    dx1_o[...] = total
    low = total.astype(BF16)
    g1_o[...] = low
    do[...] = nt(wo[...], low).astype(BF16)
    rows = do.shape[0]
    dq_o = dqkv_o.at[0:rows]
    dk_o = dqkv_o.at[rows : 2 * rows]
    dv_o = dqkv_o.at[2 * rows : 3 * rows]
    attention_backward(q, ka, va, o, lse, do, qa, doa, dq_o, dk_o, dv_o, q.shape[1], True)
    part = tn(dq_o[...], wq[...]) + tn(dk_o[...], wk[...]) + tn(dv_o[...], wv[...])
    store_halves(part, side, keep_o, send_o)
    unit, _ = norm_parts(x_ref[item].astype(F32))
    pick = iota((8, vec_o.shape[1]), 0)
    out = jnp.where(pick == 0, gain_row, 0.0)
    out = jnp.where(pick == 1, shift_row, out)
    out = jnp.where(pick == 2, jnp.sum(total, axis=0, keepdims=True), out)
    out = jnp.where(pick == 5, jnp.sum(part * unit, axis=0, keepdims=True), out)
    vec_o[...] = jnp.where(pick == 6, jnp.sum(part, axis=0, keepdims=True), out)
    vec_o[3:4, 0:rows] = row_of_sums(dq_o[...])
    vec_o[4:5, 0:rows] = row_of_sums(dv_o[...])


def self_weights(items, x_ref, gain, shift, *refs):
    dqkv, o, g1, vecs = (refs[k * items : (k + 1) * items] for k in range(4))
    keep_o, send_o, whole = refs[4 * items :]
    rows = o[0].shape[0]
    span = range(items)
    normed = []
    for k in span:
        unit, _ = norm_parts(x_ref[k].astype(F32))
        normed.append((unit * line(gain) + line(shift)).astype(BF16))
    whole[0 : 3 * rows, :] = sum_of([nn(dqkv[k][...], normed[k]) for k in span])
    whole[3 * rows : 4 * rows, :] = sum_of([nn(o[k][...], g1[k][...]) for k in span])
    whole[4 * rows :, :] = jnp.zeros((whole.shape[0] - 4 * rows, whole.shape[1]), F32)
    whole[4 * rows : 4 * rows + 8, :] = sum_of([v[...] for v in vecs])
    scatter_blocks(whole, keep_o, send_o, X_FIRST)


def unpack(matrices, lines, steps, near, far, *rest):
    outs, whole = rest[:-1], rest[-1]
    gather_blocks(near, far, whole, steps)
    start = 0
    for out in outs[:matrices]:
        out[...] = whole[start : start + out.shape[0], :]
        start += out.shape[0]
    for k, out in enumerate(outs[matrices : matrices + lines]):
        out[...] = whole[start + k : start + k + 1, 0 : out.shape[0]].reshape(out.shape)
    for out in outs[matrices + lines :]:
        out[...] = whole[start : start + out.shape[0], :]


def finish_out(items, *refs):
    x2, pieces, (bias, out, whole) = refs[:items], refs[items : items + 2], refs[items + 2 :]
    for k in range(items):
        total = x2[k][...] + join_halves([p.at[k] for p in pieces], mp_side(), whole) + line(bias)
        out[k] = total.astype(BF16)


def finish_grad(items, *refs):
    dx1, pieces, (x_ref, gain, out, whole) = refs[:items], refs[items : items + 2], refs[items + 2 :]
    for k in range(items):
        grad_in = join_halves([p.at[k] for p in pieces], mp_side(), whole)
        grad, _, _ = norm_back(x_ref[k].astype(F32), line(gain), grad_in)
        out[k] = dx1[k][...] + grad


def finish_memory(kept, far, out):
    for k in range(kept.shape[0]):
        out[k] = kept[k].astype(F32) + far[k].astype(F32)


def both(left, right):
    return (left.astype(F32) + right.astype(F32)).astype(BF16)


def add_rows(left, right, out):
    out[...] = both(left[...], right[...])


def add_parts(left, *rest):
    parts, out = rest[:-1], rest[-1]
    start = 0
    for part in parts:
        spot = slice(start, start + part.shape[0])
        out[spot] = both(left[spot], part[...])
        start += part.shape[0]


def add_stack(count, *refs):
    out = refs[-1]
    each = (len(refs) - 1) // count
    for k in range(count):
        add_parts(*refs[k * each : (k + 1) * each], out.at[k])


def add_memory(count, *refs):
    left, right, (kept, sent) = refs[:count], refs[count : 2 * count], refs[2 * count :]
    for k in range(count):
        kept[k] = both(left[k][0], right[k][0])
        sent[k] = both(left[k][1], right[k][1])


def add_split(left, right, keep, send):
    half = keep.shape[0]
    keep[...] = both(left[0:half], right[0:half])
    send[...] = both(left[half:], right[half:])


def together(steps, *refs):
    given = sum(step[1] for step in steps)
    ins, outs = refs[:given], refs[given:]
    for body, takes, gives in steps:
        body(*ins[:takes], *outs[:gives])
        ins, outs = ins[takes:], outs[gives:]


def stack_pair(left, right, out):
    half = left.shape[0]
    out[0:half] = left[...]
    out[half:] = right[...]


SCALARS = pl.BlockSpec(memory_space=pltpu.SMEM)
LEFT = pl.BlockSpec(memory_space=pl.ANY)
AWAY = pl.BlockSpec(memory_space=pltpu.HBM)
NEAR = pl.BlockSpec(memory_space=pltpu.VMEM)
FAR = pl.BlockSpec(memory_space=pltpu.VMEM)


def chosen(array, item):
    rest = (0,) * (len(array.shape) - 1)
    return pl.BlockSpec((None,) + tuple(array.shape[1:]), lambda *_: (item,) + rest)


def shape(dims, dtype):
    return jax.ShapeDtypeStruct(dims, dtype)


def near_shape(dims, dtype=BF16):
    return pltpu.VMEM(dims, dtype)


def near_like(array, dims=None):
    return pltpu.VMEM(tuple(dims or array.shape), array.dtype)


class Order:
    def __init__(self):
        self.tick = None

    def later(self, value):
        return lax.optimization_barrier((value, self.tick))[0]

    def run(self, body, cost, operands, outs, scratch=(), specs=None, out_specs=None, aliases=None):
        specs = specs or {}
        placed, in_specs = [], []
        for k, array in enumerate(operands):
            spec = specs.get(k, SCALARS if array.dtype == jnp.int32 else NEAR)
            if spec is NEAR:
                array = pltpu.with_memory_space_constraint(array, pltpu.VMEM)
            elif spec is AWAY:
                array = pltpu.with_memory_space_constraint(array, pltpu.HBM)
            placed.append(array)
            in_specs.append(spec)
        count = len(placed)
        if self.tick is not None:
            placed.append(pltpu.with_memory_space_constraint(self.tick, pltpu.VMEM))
            in_specs.append(NEAR)
        given, made = len(placed), len(outs)

        def whole_body(*refs):
            tick = refs[given + made]
            tick[...] = jnp.zeros(tick.shape, tick.dtype)
            body(*refs[:count], *refs[given : given + made], *refs[given + made + 1 :])

        inner = body
        while isinstance(inner, functools.partial):
            inner = inner.func
        results = pl.pallas_call(
            whole_body,
            name=inner.__name__,
            grid=(1,),
            in_specs=in_specs,
            out_specs=list(out_specs or [NEAR] * made) + [NEAR],
            out_shape=list(outs) + [near_shape((8, 128), F32)],
            scratch_shapes=list(scratch),
            input_output_aliases=aliases or {},
            cost_estimate=pl.CostEstimate(flops=int(cost * COST), transcendentals=0, bytes_accessed=1),
            compiler_params=pltpu.CompilerParams(vmem_limit_bytes=VMEM_BYTES),
        )(*placed)
        self.tick = results[-1]
        return results[:-1]


def run_together(order, jobs):
    steps = [(body, len(operands), len(outs)) for body, operands, outs, _ in jobs]
    results = order.run(
        functools.partial(together, steps), 1, [a for job in jobs for a in job[1]], [o for job in jobs for o in job[2]]
    )
    for _, _, outs, then in jobs:
        then(*results[: len(outs)])
        results = results[len(outs) :]


def swap(value, axis, size, bit):
    return lax.ppermute(value, axis, [(k, k ^ bit) for k in range(size)])


class MpSum:
    def __init__(self, order, size, keep, *sends):
        self.order, self.size, self.keep = order, size, keep
        self.near = [swap(send, "mp", size, 1) for send in sends]

    def add(self):
        own = self.order.run(add_parts, 0.5, (self.keep, *self.near), (near_like(self.keep),))[0]
        self.spread(own)

    def spread(self, own):
        self.own = own
        self.far = swap(own, "mp", self.size, 2)

    def meet(self):
        run_together(self.order, [self.meet_job()])

    def meet_job(self):
        return add_rows, (self.own, self.far), (near_like(self.own),), self.share

    def share(self, total):
        self.pieces = total, swap(total, "mp", self.size, 1)


class PairSum(MpSum):
    def __init__(self, order, size, keeps, sends):
        self.order, self.size, self.keeps = order, size, keeps
        self.near = [swap(send, "mp", size, 1) for send in sends]

    def job(self):
        count = len(self.keeps)
        stack = near_like(self.keeps[0], (count,) + self.keeps[0].shape)
        parts = [part for pair in zip(self.keeps, self.near) for part in pair]
        return functools.partial(add_stack, count), parts, (stack,), self.spread


class DpSum:
    def __init__(self, order, size, steps, keep, send):
        self.order, self.size, self.steps = order, size, steps
        self.keep, self.near = keep, self.swap(send, 0)
        self.stage = 0

    def swap(self, value, step):
        return swap(value, "dp", self.size, self.steps[step])

    def step(self):
        run_together(self.order, [self.job()])

    def job(self):
        dims, stage = self.keep.shape, self.stage
        self.stage += 1
        both_parts = (self.keep, self.near)
        if stage < 2:
            out = near_like(self.keep, (dims[0] // 2,) + dims[1:])

            def then(keep, send):
                self.keep, self.near = keep, self.swap(send, stage + 1)

            return add_split, both_parts, (out, out), then
        if stage == 2:

            def then(total):
                bit = 8
                while bit < self.size:
                    other = swap(total, "dp", self.size, bit)
                    total = self.order.run(add_rows, 0.5, (total, other), (near_like(total),))[0]
                    bit *= 2
                self.keep, self.near = total, self.swap(total, 2)

            return add_rows, both_parts, (near_like(self.keep),), then
        out = near_like(self.keep, (dims[0] * 2,) + dims[1:])

        def then(total):
            self.keep, self.near = total, self.swap(total, 4 - stage)

        return stack_pair, both_parts, (out,), then

    def unpack(self, matrices, lines, *more):
        rows = 8 * self.keep.shape[1]
        specs = [pl.BlockSpec(o.shape, lambda *_: (0, 0)) for o in matrices]
        specs += [pl.BlockSpec(o.shape, lambda *_: (0,)) for o in lines] + [NEAR] * len(more)
        return self.order.run(
            functools.partial(unpack, len(matrices), len(lines), self.steps), 3, (self.keep, self.near),
            tuple(matrices) + tuple(lines) + more, (pltpu.VMEM((rows, matrices[0].shape[1]), F32),), None, specs,
        )


def shards(sizes, *arguments):
    (
        hidden, encoder, lengths, tasks, frames, out_grad,
        gain_self, shift_self, query_self, qbias_self, key_self, value_self, vbias_self, output_self, obias_self,
        gain_cross, shift_cross, query_cross, qbias_cross, key_cross, value_cross, vbias_cross, output_cross, obias_cross,
        gain_feed, shift_feed, expand_weight, expand_bias, contract_weight, contract_bias,
    ) = arguments
    n_mp, n_dp = sizes["mp"], sizes["dp"]
    items, length, width = hidden.shape
    memory_len = encoder.shape[1]
    rows = query_self.shape[1]
    heads = rows // HEAD
    units = expand_weight.shape[1]
    wide = -(-memory_len // 512) * 512
    chunk = 512
    half = length // 2
    wq1, wk1, wv1 = query_self.T, key_self.T, value_self.T
    wq2, wk2, wv2 = query_cross.T, key_cross.T, value_cross.T

    low_rows = near_shape((rows, length))
    mem_rows = near_shape((rows, wide))
    half_outs = (near_shape((half, width)), near_shape((half // 2, width)), near_shape((half - half // 2, width)))
    state = near_shape((length, width), F32)
    low_state = near_shape((length, width))
    unit_state = near_shape((length, units))
    vec_out = near_shape((8, width), F32)
    lse_out = near_shape((8, length), F32)
    aug_out = near_shape((heads, AUG, length))
    aug_mem = near_shape((heads, AUG, wide))
    mem_half = near_shape((2, rows, memory_len))
    pair_outs = (near_shape((half, width)), near_shape((half, width)))
    whole = pltpu.VMEM((length, width), F32)
    aug = pltpu.VMEM((AUG, length), BF16)
    row_scratch = pltpu.VMEM((rows, length), BF16)
    span = range(items)
    bind = functools.partial
    order = Order()

    def mp_sum(*parts):
        return MpSum(order, n_mp, *parts)

    def pack_outs(count):
        return (near_shape((4, count // 8, width)),) * 2, (pltpu.VMEM((count, width), F32),)

    def keys(i):
        return order.run(
            bind(cross_keys, i), 3, (frames, encoder, wk2, wv2, vbias_cross),
            (aug_mem, aug_mem), (), {1: chosen(encoder, i)},
        )

    self_out, self_sum, cross_kv = [], [], []
    loads = (
        hidden, gain_self, shift_self, wq1, qbias_self, wk1, wv1, vbias_self, output_self,
        wk2, wv2, vbias_cross, obias_self, gain_cross, shift_cross, wq2, qbias_cross, output_cross,
        out_grad, obias_cross, gain_feed, shift_feed, expand_weight, expand_bias, contract_weight, contract_bias,
    )
    self_outs = (low_rows, aug_out, aug_out, low_rows, lse_out, *half_outs)
    for i in span:
        if i == 0:
            out = order.run(
                bind(first_forward, i, 9, len(loads)), 4, (lengths, *loads),
                self_outs + tuple(near_like(a) for a in loads), (aug, pltpu.SemaphoreType.DMA((len(loads),))),
                {k + 1: AWAY for k in range(len(loads))},
            )
            near = out[8:]
            hidden, gain_self, shift_self, wq1, qbias_self, wk1, wv1, vbias_self, output_self = near[:9]
            wk2, wv2, vbias_cross, obias_self, gain_cross, shift_cross, wq2, qbias_cross, output_cross = near[9:18]
            out_grad, obias_cross, gain_feed, shift_feed, expand_weight, expand_bias, contract_weight, contract_bias = near[18:]
        else:
            operands = (lengths, hidden, gain_self, shift_self, wq1, qbias_self, wk1, wv1, vbias_self, output_self)
            out = order.run(bind(self_forward, i), 4, operands, self_outs, (aug,))
        self_out.append(out)
        self_sum.append(mp_sum(*out[5:8]))
    for i in span:
        self_sum[i].add()
        cross_kv.append(keys(i))

    cross_out, cross_sum = [], []
    for i in span:
        self_sum[i].meet()
        out = order.run(
            bind(cross_forward, i, chunk), 6,
            (hidden, *self_sum[i].pieces, obias_self, gain_cross, shift_cross, wq2, qbias_cross, output_cross, *cross_kv[i]),
            (state, low_state, low_rows, low_rows, lse_out, *half_outs), (whole, aug),
        )
        cross_out.append(out)
        cross_sum.append(mp_sum(*out[5:8]))
        cross_sum[i].add()

    feed_out, feed_sum = [], []
    for i in span:
        cross_sum[i].meet()
        out = order.run(
            bind(feed, i), 4,
            (lengths, tasks, cross_out[i][0], *cross_sum[i].pieces, out_grad, obias_cross, gain_feed, shift_feed, expand_weight, expand_bias, contract_weight),
            (state, low_state, unit_state, unit_state, low_state, vec_out, *half_outs), (whole,),
        )
        feed_out.append(out)
        feed_sum.append(mp_sum(*out[6:9]))
        feed_sum[i].add()
    back_out, back_sum = [], []
    for i in span:
        _, _, q2, o2, lse2 = cross_out[i][:5]
        feed_sum[i].meet()
        if i == 0:
            outs, scratch = pack_outs(width + units + 64)
            operands = [out[k] for k in (1, 3, 2, 4, 5) for out in feed_out]
            feed_dp = DpSum(order, n_dp, X_FIRST, *order.run(bind(feed_weights, items), 2, operands, outs, scratch))
        out = order.run(
            bind(cross_backward, i, chunk), 9,
            (lengths, tasks, feed_out[i][0], *feed_sum[i].pieces, out_grad, gain_feed, output_cross, wq2, *cross_kv[i], q2, o2, lse2),
            (state, low_state, low_rows, mem_rows, mem_rows, vec_out, *half_outs), (whole, aug, aug, row_scratch),
        )
        back_out.append(out)
        back_sum.append(mp_sum(*out[6:9]))
        back_sum[i].add()

    self_back = []
    outs, scratch = pack_outs(4 * rows + 64)
    for i in span:
        q1, ka1, va1, o1, lse1 = self_out[i][:5]
        back_sum[i].meet()
        if i == 0:
            feed_dp.step()
        out = order.run(
            bind(self_backward, i), 5,
            (cross_out[i][0], *back_sum[i].pieces, back_out[i][0], hidden, gain_cross, output_self, wq1, wk1, wv1, ka1, va1, q1, o1, lse1),
            (state, low_state, near_shape((3 * rows, length)), vec_out, *pair_outs), (whole, aug, aug, row_scratch),
        )
        self_back.append(out)
        if i == 0:
            operands = [encoder] + [out[2] for out in back_out] + [out[1] for out in cross_out] + [out[3] for out in cross_out]
            operands += [out[1] for out in back_out] + [out[3] for out in back_out] + [out[4] for out in back_out]
            operands += [out[5] for out in back_out]
            made = order.run(
                bind(cross_weights, items), 3, operands, outs, scratch,
                {0: pl.BlockSpec(encoder.shape, lambda *_: (0, 0, 0))},
            )
            cross_dp = DpSum(order, n_dp, X_FIRST, *made)
    operands = [hidden, gain_self, shift_self] + [out[2] for out in self_back] + [out[3] for out in self_out]
    operands += [out[1] for out in self_back] + [out[3] for out in self_back]
    grad_shape, block_shape = shape(hidden.shape, F32), shape(hidden.shape, BF16)
    mem_half, memory_out = near_shape((2, rows, memory_len)), near_shape((items, rows, memory_len))
    line_out, bias_out, matrix = shape((width,), F32), shape((rows,), F32), shape((rows, width), F32)
    lines = (line_out, line_out, line_out, bias_out, bias_out)
    whole_cube = [pl.BlockSpec(hidden.shape, lambda *_: (0, 0, 0))]
    got = {}

    def pack_self():
        got["S"] = DpSum(order, n_dp, X_FIRST, *order.run(bind(self_weights, items), 3, operands, outs, scratch))

    def last_finish():
        got["hidden"] = order.run(
            bind(finish_grad, items), 4, [out[0] for out in self_back] + list(got["last"].pieces) + [hidden, gain_self],
            (grad_shape,), (whole,), None, whole_cube,
        )[0]

    def memory(i):
        part = order.run(memory_grad, 2, (wk2, wv2, back_out[i][3], back_out[i][4]), (mem_half, mem_half))
        got["m", i] = part

    def memory_swap():
        for i in span:
            keep, send = got["m", i]
            got["m", i] = keep, swap(order.later(send), "mp", n_mp, 1)

    def memory_finish():
        got["encoder"] = order.run(
            finish_memory, 2, got["far"], (shape((items, rows, memory_len), F32),), (), None,
            [pl.BlockSpec((items, rows, memory_len), lambda *_: (0, 0, 0))],
        )[0].transpose(0, 2, 1)

    def block_part(i):
        keep, send = order.run(feed_out_part, 1, (feed_out[i][2], contract_weight), pair_outs)
        got["b", i] = keep, send

    def block_finish():
        got["out"] = order.run(
            bind(finish_out, items), 3, [out[0] for out in feed_out] + list(got["block"].pieces) + [contract_bias],
            (block_shape,), (whole,), None, whole_cube,
        )[0]

    def unpack_feed():
        got["f"] = feed_dp.unpack(
            (shape((width, width), F32), shape((units, width), F32)), (line_out, shape((units,), F32))
        )

    def unpack_cross():
        got["x"] = cross_dp.unpack((matrix,) * 4, lines)

    def unpack_self():
        got["s"] = got["S"].unpack((matrix,) * 4, lines, near_shape((8, width), F32))

    def job(which):
        if which in "FXS":
            return {"F": feed_dp, "X": cross_dp, "S": got.get("S")}[which].job()
        if which == "l":
            got["last"] = PairSum(order, n_mp, [out[4] for out in self_back], [out[5] for out in self_back])
            return got["last"].job()
        if which == "b":
            return got["block"].job()
        if which == "m":
            return got["last"].meet_job()
        if which == "c":
            return got["block"].meet_job()
        parts = [got["m", i] for i in span]

        def then(kept, sent):
            got["far"] = kept, swap(sent, "mp", n_mp, 2)

        return bind(add_memory, items), [p[0] for p in parts] + [p[1] for p in parts], (memory_out, memory_out), then

    def block_swap():
        sends = [order.later(got["b", i][1]) for i in span]
        got["block"] = PairSum(order, n_mp, [got["b", i][0] for i in span], sends)

    acts = dict(
        M=memory_swap, N=block_swap, P=pack_self, g=last_finish, A=lambda: [memory(i) for i in span], e=memory_finish,
        B=lambda: [block_part(i) for i in span], o=block_finish, u=unpack_feed, v=unpack_cross, w=unpack_self,
    )
    for word in ORDER:
        if word[0] in acts:
            for act in word:
                acts[act]()
        else:
            run_together(order, [job(which) for which in word])
    cross_grads, self_grads, feed_grads = got["x"], got["s"], got["f"]
    hidden_grad, encoder_grad, block_out = got["hidden"], got["encoder"], got["out"]
    norm_rows = self_grads[9]
    norm_rows = norm_rows + swap(norm_rows, "mp", n_mp, 1) + (swap(norm_rows, "mp", n_mp, 2) + swap(norm_rows, "mp", n_mp, 3))
    return (
        block_out,
        hidden_grad,
        encoder_grad,
        norm_rows[5],
        norm_rows[6],
        self_grads[0].T,
        self_grads[7],
        self_grads[1].T,
        self_grads[2].T,
        self_grads[8],
        self_grads[3],
        self_grads[6],
        self_grads[4],
        self_grads[5],
        cross_grads[0].T,
        cross_grads[7],
        cross_grads[1].T,
        cross_grads[2].T,
        cross_grads[8],
        cross_grads[3],
        cross_grads[6],
        cross_grads[4],
        cross_grads[5],
        feed_grads[0],
        feed_grads[3],
        feed_grads[1],
        feed_grads[2],
    )


def solution(mesh):
    column, row, flat = P(None, "mp"), P("mp", None), P("mp")
    cube = P("dp", None, None)
    attention = (P(), P(), column, flat, column, column, flat, row, P())
    grads = (P(), P(), column, flat, column, column, flat, row, P())
    return jax.shard_map(
        functools.partial(shards, dict(mesh.shape)),
        mesh=mesh,
        in_specs=(cube, cube, P("dp"), P("dp"), P("dp"), cube)
        + attention
        + attention
        + (P(), P(), column, flat, row, P()),
        out_specs=(cube, cube, P("dp", None, "mp")) + grads + grads + (P(), P(), column, flat, row, P()),
        check_vma=False,
    )
```

```python
import functools
import math

import jax
import jax.numpy as jnp
from jax import lax
from jax.experimental import pallas as pl
from jax.experimental.pallas import tpu as pltpu
from jax.sharding import PartitionSpec as P

HEAD = 64
AUG = 80
EPS = 1e-05
NEG = -1e30
F32 = jnp.float32
BF16 = jnp.bfloat16
ROOT_HALF = math.sqrt(0.5)
INV_ROOT_TAU = 1.0 / math.sqrt(2.0 * math.pi)
VMEM_BYTES = 20 * 1024 * 1024
COST = 1
ORDER = ("VAP", "B", "FX", "M", "FXSa", "FXSl", "e", "N", "b", "FXSm", "XSc", "u", "S", "g", "v", "o", "w")


def dot(left, right, left_dim, right_dim):
    return lax.dot_general(
        left, right, (((left_dim,), (right_dim,)), ((), ())), preferred_element_type=F32
    )


def nn(left, right):
    return dot(left, right, 1, 0)


def nt(left, right):
    return dot(left, right, 1, 1)


def tn(left, right):
    return dot(left, right, 0, 0)


def iota(shape, axis):
    return lax.broadcasted_iota(jnp.int32, shape, axis)


def norm_parts(values):
    centred = values - jnp.mean(values, axis=-1, keepdims=True)
    spread = jnp.mean(centred * centred, axis=-1, keepdims=True)
    scale = lax.rsqrt(spread + EPS)
    return centred * scale, scale


def norm_back(values, gain, upstream):
    unit, scale = norm_parts(values)
    inner = upstream * gain
    first = jnp.mean(inner, axis=-1, keepdims=True)
    second = jnp.mean(inner * unit, axis=-1, keepdims=True)
    grad = scale * (inner - first - unit * second)
    return (
        grad,
        jnp.sum(upstream * unit, axis=0, keepdims=True),
        jnp.sum(upstream, axis=0, keepdims=True),
    )


def line(ref):
    return ref[...].astype(F32).reshape(1, ref.shape[0])


def column_bias(ref, count):
    first = jnp.where(iota((16, ref.shape[0]), 0) == 0, line(ref), 0.0).astype(BF16)
    return tn(first, jnp.ones((16, count), BF16))


def mp_side():
    return lax.axis_index("mp") % 2


def key_extra(count, limit):
    rows = iota((16, count), 0)
    hidden_keys = jnp.where(iota((16, count), 1) < limit, 0.0, NEG)
    ones = jnp.where(rows < 4, 1.0, 0.0)
    return jnp.where(rows == 0, hidden_keys, ones).astype(BF16)


def value_extra(count):
    return jnp.where(iota((16, count), 0) < 3, 1.0, 0.0).astype(BF16)


def three_parts(row):
    high = row.astype(BF16)
    rest = row - high.astype(F32)
    middle = rest.astype(BF16)
    last = (rest - middle.astype(F32)).astype(BF16)
    return high.astype(F32), middle.astype(F32), last.astype(F32)


def split_rows(rows, row, first, with_one):
    high, middle, last = three_parts(row)
    base = jnp.where(rows == 0, 1.0, 0.0) if with_one else jnp.zeros(rows.shape, F32)
    out = jnp.where(rows == first, high, base)
    out = jnp.where(rows == first + 1, middle, out)
    return jnp.where(rows == first + 2, last, out).astype(BF16)


def store_halves(part, side, keep_ref, send_ref, rest_ref=None):
    half = part.shape[0] // 2
    edge = send_ref.shape[0]
    low = part.astype(BF16)

    @pl.when(side == 0)
    def _():
        keep_ref[...] = low[:half]
        send_ref[...] = low[half : half + edge]
        if rest_ref is not None:
            rest_ref[...] = low[half + edge :]

    @pl.when(side == 1)
    def _():
        keep_ref[...] = low[half:]
        send_ref[...] = low[:edge]
        if rest_ref is not None:
            rest_ref[...] = low[edge:half]


def join_halves(pieces, side, scratch):
    own, other = pieces
    half = own.shape[0]
    scratch[pl.ds(pl.multiple_of(side * half, 16), half), :] = own[...].astype(F32)
    scratch[pl.ds(pl.multiple_of((1 - side) * half, 16), half), :] = other[...].astype(F32)
    return scratch[...]


def attend_block(keys, queries, keep):
    scores = tn(keys, queries)
    if keep is not None:
        scores = jnp.where(keep, scores, NEG)
    return scores


def causal_mask(count):
    return iota((count, count), 0) <= iota((count, count), 1)


def attention_forward(q_ref, ka_ref, va_ref, qa, o_ref, lse_ref, chunk, causal):
    heads, _, keys = ka_ref.shape
    count = q_ref.shape[1]
    rows = iota((16, count), 0)
    qa[HEAD:AUG, :] = jnp.where(rows == 0, 1.0, 0.0).astype(BF16)
    keep = causal_mask(count) if causal else None
    lse_rows = iota((8, count), 0)
    lse = jnp.zeros((8, count), F32)
    for head in range(heads):
        spot = slice(head * HEAD, (head + 1) * HEAD)
        qa[0:HEAD, :] = q_ref[spot, :]
        queries = qa[...]
        largest = None
        for start in range(0, keys, chunk):
            part = slice(start, start + chunk)
            scores = attend_block(ka_ref[head, :, part], queries, keep)
            top = jnp.max(scores, axis=0, keepdims=True)
            if largest is None:
                powers = jnp.exp(scores - top).astype(BF16)
                mixed = nn(va_ref[head, :, part], powers)
                largest = top
            else:
                newer = jnp.maximum(largest, top)
                powers = jnp.exp(scores - newer).astype(BF16)
                mixed = mixed * jnp.exp(largest - newer) + nn(va_ref[head, :, part], powers)
                largest = newer
        total = mixed[HEAD : HEAD + 1]
        o_ref[spot, :] = (mixed[0:HEAD] / total).astype(BF16)
        lse = jnp.where(lse_rows == head, largest + jnp.log(total), lse)
    lse_ref[...] = lse


def attention_backward(
    q_ref, ka_ref, va_ref, o_ref, lse_ref, do_ref, qa, doa, dq_ref, dk_ref, dv_ref, chunk, causal
):
    heads, _, keys = ka_ref.shape
    count = q_ref.shape[1]
    rows = iota((16, count), 0)
    keep = causal_mask(count) if causal else None
    for head in range(heads):
        spot = slice(head * HEAD, (head + 1) * HEAD)
        queries = q_ref[spot, :]
        mix_grad = do_ref[spot, :]
        qa[0:HEAD, :] = queries
        doa[0:HEAD, :] = mix_grad
        qa[HEAD:AUG, :] = split_rows(rows, -lse_ref[head : head + 1, :], 1, True)
        centre = jnp.sum(
            mix_grad.astype(F32) * o_ref[spot, :].astype(F32), axis=0, keepdims=True
        )
        doa[HEAD:AUG, :] = split_rows(rows, -centre, 0, False)
        query_side = qa[...]
        grad_side = doa[...]
        query_grad = jnp.zeros((HEAD, count), F32)
        for start in range(0, keys, chunk):
            part = slice(start, start + chunk)
            shares = jnp.exp(attend_block(ka_ref[head, :, part], query_side, keep))
            pushed = tn(va_ref[head, :, part], grad_side)
            score_grad = (shares * pushed).astype(BF16)
            dv_ref[spot, part] = nt(mix_grad, shares.astype(BF16)).astype(BF16)
            dk_ref[spot, part] = nt(queries, score_grad).astype(BF16)
            query_grad = query_grad + nn(ka_ref[head, 0:HEAD, part], score_grad)
        dq_ref[spot, :] = (query_grad * 0.125).astype(BF16)


def row_of_sums(matrix):
    ones = jnp.ones((16, matrix.shape[1]), BF16)
    return nt(ones, matrix)[0:1]


def self_forward(item, lengths, x_ref, gain, shift, wq, qbias, wk, wv, vbias, wo, q_o, ka_o, va_o, o_o, lse_o, keep_o, send_o, rest_o, qa):
    count = x_ref.shape[1]
    unit, _ = norm_parts(x_ref[item].astype(F32))
    normed = (unit * line(gain) + line(shift)).astype(BF16)
    queries = (nt(wq[...], normed) + column_bias(qbias, count)).astype(BF16)
    q_o[...] = queries * jnp.asarray(0.125, BF16)
    key_rows = nt(wk[...], normed).astype(BF16)
    value_rows = (nt(wv[...], normed) + column_bias(vbias, count)).astype(BF16)
    extra = key_extra(count, lengths[item])
    other = value_extra(count)
    for head in range(ka_o.shape[0]):
        spot = slice(head * HEAD, (head + 1) * HEAD)
        ka_o[head, 0:HEAD, :] = key_rows[spot]
        ka_o[head, HEAD:AUG, :] = extra
        va_o[head, 0:HEAD, :] = value_rows[spot]
        va_o[head, HEAD:AUG, :] = other
    attention_forward(q_o, ka_o, va_o, qa, o_o, lse_o, count, True)
    store_halves(tn(o_o[...], wo[...]), mp_side(), keep_o, send_o, rest_o)


def first_forward(item, first, count, lengths, *refs):
    sources, targets = refs[:count], refs[count + 8 : 2 * count + 8]
    outs, qa, sems = refs[count : count + 8], refs[-2], refs[-1]
    copies = [pltpu.make_async_copy(s, t, sems.at[k]) for k, (s, t) in enumerate(zip(sources, targets))]
    for copy in copies:
        copy.start()
    for copy in copies[:first]:
        copy.wait()
    self_forward(item, lengths, *targets[:first], *outs, qa)
    for copy in copies[first:]:
        copy.wait()


def cross_keys(item, frames, enc, wk, wv, vbias, ka_o, va_o):
    count = enc.shape[0]
    wide = ka_o.shape[2]
    memory = enc[...]
    key_rows = nt(wk[...], memory).astype(BF16)
    value_rows = (nt(wv[...], memory) + column_bias(vbias, count)).astype(BF16)
    extra = key_extra(wide, frames[item])
    other = value_extra(wide)
    for head in range(ka_o.shape[0]):
        spot = slice(head * HEAD, (head + 1) * HEAD)
        if wide > count:
            ka_o[head, 0:HEAD, wide - 128 :] = jnp.zeros((HEAD, 128), BF16)
            va_o[head, 0:HEAD, wide - 128 :] = jnp.zeros((HEAD, 128), BF16)
        ka_o[head, 0:HEAD, 0:count] = key_rows[spot]
        ka_o[head, HEAD:AUG, :] = extra
        va_o[head, 0:HEAD, 0:count] = value_rows[spot]
        va_o[head, HEAD:AUG, :] = other


def cross_forward(item, chunk, x_ref, s0, s1, obias, gain, shift, wq, qbias, wo, ka, va, x1_o, h2_o, q_o, o_o, lse_o, keep_o, send_o, rest_o, whole, qa):
    count = x_ref.shape[1]
    side = mp_side()
    after = x_ref[item].astype(F32) + join_halves((s0, s1), side, whole) + line(obias)
    x1_o[...] = after
    unit, _ = norm_parts(after)
    normed = (unit * line(gain) + line(shift)).astype(BF16)
    h2_o[...] = normed
    queries = (nt(wq[...], normed) + column_bias(qbias, count)).astype(BF16)
    q_o[...] = queries * jnp.asarray(0.125, BF16)
    attention_forward(q_o, ka, va, qa, o_o, lse_o, chunk, False)
    store_halves(tn(o_o[...], wo[...]), side, keep_o, send_o, rest_o)


def upstream_rows(item, lengths, tasks, og):
    task = tasks[item]
    weight = jnp.where(task == 0, 1.0, jnp.where(task == 1, 0.6, 2.0)).astype(F32)
    valid = iota((og.shape[1], 1), 0) < lengths[item]
    return og[item].astype(F32) * jnp.where(valid, weight, 0.0)


def feed(item, lengths, tasks, x1, s0, s1, og, obias, gain, shift, we, ebias, wc, x2_o, h3_o, a_o, dz_o, gy_o, vec_o, bkeep_o, bsend_o, brest_o, whole):
    side = mp_side()
    after = x1[...] + join_halves((s0, s1), side, whole) + line(obias)
    x2_o[...] = after
    unit, _ = norm_parts(after)
    normed = (unit * line(gain) + line(shift)).astype(BF16)
    h3_o[...] = normed
    before = nn(normed, we[...]) + line(ebias)
    share = 0.5 + 0.5 * lax.erf(before * ROOT_HALF)
    active = (before * share).astype(BF16)
    a_o[...] = active
    slope = share + before * (jnp.exp(before * before * -0.5) * INV_ROOT_TAU)
    grad = upstream_rows(item, lengths, tasks, og)
    low = grad.astype(BF16)
    gy_o[...] = low
    inner = (nt(low, wc[...]) * slope).astype(BF16)
    dz_o[...] = inner
    store_halves(nt(inner, we[...]), side, bkeep_o, bsend_o, brest_o)
    pick = iota((8, vec_o.shape[1]), 0)
    out = jnp.where(pick == 0, jnp.sum(grad, axis=0, keepdims=True), 0.0)
    vec_o[...] = jnp.where(pick == 1, jnp.sum(inner.astype(F32), axis=0, keepdims=True), out)


def feed_out_part(active, wc, keep_o, send_o):
    store_halves(nn(active[...], wc[...]), mp_side(), keep_o, send_o)


def sum_of(refs):
    out = refs[0]
    for other in refs[1:]:
        out = out + other
    return out


def feed_weights(items, *refs):
    h3, dz, a, gy, vecs = (refs[k * items : (k + 1) * items] for k in range(5))
    keep_o, send_o, whole = refs[5 * items :]
    width = h3[0].shape[1]
    edge = width + dz[0].shape[1]
    whole[0:width, :] = sum_of([tn(h3[k][...], dz[k][...]) for k in range(items)])
    whole[width:edge, :] = sum_of([tn(a[k][...], gy[k][...]) for k in range(items)])
    whole[edge:, :] = jnp.zeros((whole.shape[0] - edge, width), F32)
    whole[edge : edge + 8, :] = sum_of([v[...] for v in vecs])
    scatter_blocks(whole, keep_o, send_o, X_FIRST)


def cross_backward(item, chunk, lengths, tasks, x2, s0, s1, og, gain, wo, wq, ka, va, q, o, lse, dx2_o, g2_o, dq_o, dk_o, dv_o, vec_o, keep_o, send_o, rest_o, whole, qa, doa, do):
    side = mp_side()
    grad_in = join_halves((s0, s1), side, whole)
    grad, gain_row, shift_row = norm_back(x2[...], line(gain), grad_in)
    total = upstream_rows(item, lengths, tasks, og) + grad
    dx2_o[...] = total
    low = total.astype(BF16)
    g2_o[...] = low
    do[...] = nt(wo[...], low).astype(BF16)
    attention_backward(q, ka, va, o, lse, do, qa, doa, dq_o, dk_o, dv_o, chunk, False)
    store_halves(tn(dq_o[...], wq[...]), side, keep_o, send_o, rest_o)
    pick = iota((8, vec_o.shape[1]), 0)
    out = jnp.where(pick == 0, gain_row, 0.0)
    out = jnp.where(pick == 1, shift_row, out)
    vec_o[...] = jnp.where(pick == 2, jnp.sum(total, axis=0, keepdims=True), out)
    vec_o[3:4, 0 : dq_o.shape[0]] = row_of_sums(dq_o[...])
    vec_o[4:5, 0 : dq_o.shape[0]] = row_of_sums(dv_o[...])


def memory_grad(wk, wv, dk, dv, keep_o, send_o):
    count = keep_o.shape[2]
    position = lax.axis_index("mp")
    rows = keep_o.shape[1]
    whole = (tn(wk[...], dk[...]) + tn(wv[...], dv[...])).astype(BF16)
    for block in range(4):
        piece = whole[block * rows : (block + 1) * rows, 0:count]
        relative = lax.bitwise_xor(position, block)
        slot = relative // 2

        @pl.when(relative % 2 == 0)
        def _():
            keep_o[slot] = piece

        @pl.when(relative % 2 == 1)
        def _():
            send_o[slot] = piece


X_FIRST = (1, 2, 4)
Z_FIRST = (2, 4, 1)


def place_of(block, steps):
    place = 0
    for bit in steps:
        place = place * 2 + block // bit % 2
    return place


def scatter_blocks(whole, keep_o, send_o, steps):
    position = lax.axis_index("dp") % 8
    rows = keep_o.shape[1]
    for block in range(8):
        place = place_of(lax.bitwise_xor(position, block), steps)
        piece = whole[block * rows : (block + 1) * rows, :].astype(BF16)

        @pl.when(place < 4)
        def _():
            keep_o[place] = piece

        @pl.when(place >= 4)
        def _():
            send_o[place - 4] = piece


def gather_blocks(near, far, whole, steps):
    position = lax.axis_index("dp") % 8
    rows = near.shape[1]
    for block in range(8):
        place = place_of(lax.bitwise_xor(position, block), steps)
        spot = slice(block * rows, (block + 1) * rows)

        @pl.when(place < 4)
        def _():
            whole[spot, :] = near[place].astype(F32)

        @pl.when(place >= 4)
        def _():
            whole[spot, :] = far[place - 4].astype(F32)


def cross_weights(items, enc, *refs):
    dq, h2, o, g2, dk, dv, vecs = (refs[k * items : (k + 1) * items] for k in range(7))
    keep_o, send_o, whole = refs[7 * items :]
    rows = dq[0].shape[0]
    count = enc.shape[1]
    span = range(items)
    whole[0:rows, :] = sum_of([nn(dq[k][...], h2[k][...]) for k in span])
    whole[rows : 2 * rows, :] = sum_of([nn(dk[k][:, 0:count], enc[k]) for k in span])
    whole[2 * rows : 3 * rows, :] = sum_of([nn(dv[k][:, 0:count], enc[k]) for k in span])
    whole[3 * rows : 4 * rows, :] = sum_of([nn(o[k][...], g2[k][...]) for k in span])
    whole[4 * rows :, :] = jnp.zeros((whole.shape[0] - 4 * rows, whole.shape[1]), F32)
    whole[4 * rows : 4 * rows + 8, :] = sum_of([v[...] for v in vecs])
    scatter_blocks(whole, keep_o, send_o, X_FIRST)


def self_backward(item, x1, s0, s1, dx2, x_ref, gain, wo, wq, wk, wv, ka, va, q, o, lse, dx1_o, g1_o, dqkv_o, vec_o, keep_o, send_o, whole, qa, doa, do):
    side = mp_side()
    grad_in = join_halves((s0, s1), side, whole)
    grad, gain_row, shift_row = norm_back(x1[...], line(gain), grad_in)
    total = dx2[...] + grad
    dx1_o[...] = total
    low = total.astype(BF16)
    g1_o[...] = low
    do[...] = nt(wo[...], low).astype(BF16)
    rows = do.shape[0]
    dq_o = dqkv_o.at[0:rows]
    dk_o = dqkv_o.at[rows : 2 * rows]
    dv_o = dqkv_o.at[2 * rows : 3 * rows]
    attention_backward(q, ka, va, o, lse, do, qa, doa, dq_o, dk_o, dv_o, q.shape[1], True)
    part = tn(dq_o[...], wq[...]) + tn(dk_o[...], wk[...]) + tn(dv_o[...], wv[...])
    store_halves(part, side, keep_o, send_o)
    unit, _ = norm_parts(x_ref[item].astype(F32))
    pick = iota((8, vec_o.shape[1]), 0)
    out = jnp.where(pick == 0, gain_row, 0.0)
    out = jnp.where(pick == 1, shift_row, out)
    out = jnp.where(pick == 2, jnp.sum(total, axis=0, keepdims=True), out)
    out = jnp.where(pick == 5, jnp.sum(part * unit, axis=0, keepdims=True), out)
    vec_o[...] = jnp.where(pick == 6, jnp.sum(part, axis=0, keepdims=True), out)
    vec_o[3:4, 0:rows] = row_of_sums(dq_o[...])
    vec_o[4:5, 0:rows] = row_of_sums(dv_o[...])


def sum_rows(*refs):
    refs[-1][...] = sum_of([ref[...] for ref in refs[:-1]])


def self_weights(items, x_ref, gain, shift, *refs):
    dqkv, o, g1 = (refs[k * items : (k + 1) * items] for k in range(3))
    vec, near, far, across, keep_o, send_o, whole = refs[3 * items :]
    rows = o[0].shape[0]
    span = range(items)
    normed = []
    for k in span:
        unit, _ = norm_parts(x_ref[k].astype(F32))
        normed.append((unit * line(gain) + line(shift)).astype(BF16))
    whole[0 : 3 * rows, :] = sum_of([nn(dqkv[k][...], normed[k]) for k in span])
    whole[3 * rows : 4 * rows, :] = sum_of([nn(o[k][...], g1[k][...]) for k in span])
    whole[4 * rows :, :] = jnp.zeros((whole.shape[0] - 4 * rows, whole.shape[1]), F32)
    summed = (vec[...] + near[...]) + (far[...] + across[...])
    pick = iota((8, whole.shape[1]), 0)
    whole[4 * rows : 4 * rows + 8, :] = jnp.where((pick == 5) | (pick == 6), summed, vec[...])
    scatter_blocks(whole, keep_o, send_o, X_FIRST)


def unpack(matrices, lines, steps, near, far, *rest):
    outs, whole = rest[:-1], rest[-1]
    gather_blocks(near, far, whole, steps)
    start = 0
    for out in outs[:matrices]:
        out[...] = whole[start : start + out.shape[0], :]
        start += out.shape[0]
    for k, out in enumerate(outs[matrices : matrices + lines]):
        out[...] = whole[start + k : start + k + 1, 0 : out.shape[0]].reshape(out.shape)
    for out in outs[matrices + lines :]:
        out[...] = whole[start : start + out.shape[0], :]


def finish_out(items, *refs):
    x2, pieces, (bias, out, whole) = refs[:items], refs[items : items + 2], refs[items + 2 :]
    for k in range(items):
        total = x2[k][...] + join_halves([p.at[k] for p in pieces], mp_side(), whole) + line(bias)
        out[k] = total.astype(BF16)


def finish_grad(items, *refs):
    dx1, pieces, (x_ref, gain, out, whole) = refs[:items], refs[items : items + 2], refs[items + 2 :]
    for k in range(items):
        grad_in = join_halves([p.at[k] for p in pieces], mp_side(), whole)
        grad, _, _ = norm_back(x_ref[k].astype(F32), line(gain), grad_in)
        out[k] = dx1[k][...] + grad


def finish_memory(kept, far, out):
    for k in range(kept.shape[0]):
        out[k] = kept[k].astype(F32) + far[k].astype(F32)


def both(left, right):
    return (left.astype(F32) + right.astype(F32)).astype(BF16)


def add_rows(left, right, out):
    out[...] = both(left[...], right[...])


def add_parts(left, *rest):
    parts, out = rest[:-1], rest[-1]
    start = 0
    for part in parts:
        spot = slice(start, start + part.shape[0])
        out[spot] = both(left[spot], part[...])
        start += part.shape[0]


def add_stack(count, *refs):
    out = refs[-1]
    each = (len(refs) - 1) // count
    for k in range(count):
        add_parts(*refs[k * each : (k + 1) * each], out.at[k])


def add_memory(count, *refs):
    left, right, (kept, sent) = refs[:count], refs[count : 2 * count], refs[2 * count :]
    for k in range(count):
        kept[k] = both(left[k][0], right[k][0])
        sent[k] = both(left[k][1], right[k][1])


def add_split(left, right, keep, send):
    half = keep.shape[0]
    keep[...] = both(left[0:half], right[0:half])
    send[...] = both(left[half:], right[half:])


def together(steps, *refs):
    given = sum(step[1] for step in steps)
    ins, outs = refs[:given], refs[given:]
    for body, takes, gives in steps:
        body(*ins[:takes], *outs[:gives])
        ins, outs = ins[takes:], outs[gives:]


def stack_pair(left, right, out):
    half = left.shape[0]
    out[0:half] = left[...]
    out[half:] = right[...]


SCALARS = pl.BlockSpec(memory_space=pltpu.SMEM)
LEFT = pl.BlockSpec(memory_space=pl.ANY)
AWAY = pl.BlockSpec(memory_space=pltpu.HBM)
NEAR = pl.BlockSpec(memory_space=pltpu.VMEM)
FAR = pl.BlockSpec(memory_space=pltpu.VMEM)


def chosen(array, item):
    rest = (0,) * (len(array.shape) - 1)
    return pl.BlockSpec((None,) + tuple(array.shape[1:]), lambda *_: (item,) + rest)


def shape(dims, dtype):
    return jax.ShapeDtypeStruct(dims, dtype)


def near_shape(dims, dtype=BF16):
    return pltpu.VMEM(dims, dtype)


def near_like(array, dims=None):
    return pltpu.VMEM(tuple(dims or array.shape), array.dtype)


class Order:
    def __init__(self):
        self.tick = None

    def later(self, value):
        return lax.optimization_barrier((value, self.tick))[0]

    def run(self, body, cost, operands, outs, scratch=(), specs=None, out_specs=None, aliases=None):
        specs = specs or {}
        placed, in_specs = [], []
        for k, array in enumerate(operands):
            spec = specs.get(k, SCALARS if array.dtype == jnp.int32 else NEAR)
            if spec is NEAR:
                array = pltpu.with_memory_space_constraint(array, pltpu.VMEM)
            elif spec is AWAY:
                array = pltpu.with_memory_space_constraint(array, pltpu.HBM)
            placed.append(array)
            in_specs.append(spec)
        count = len(placed)
        if self.tick is not None:
            placed.append(pltpu.with_memory_space_constraint(self.tick, pltpu.VMEM))
            in_specs.append(NEAR)
        given, made = len(placed), len(outs)

        def whole_body(*refs):
            tick = refs[given + made]
            tick[...] = jnp.zeros(tick.shape, tick.dtype)
            body(*refs[:count], *refs[given : given + made], *refs[given + made + 1 :])

        inner = body
        while isinstance(inner, functools.partial):
            inner = inner.func
        results = pl.pallas_call(
            whole_body,
            name=inner.__name__,
            grid=(1,),
            in_specs=in_specs,
            out_specs=list(out_specs or [NEAR] * made) + [NEAR],
            out_shape=list(outs) + [near_shape((8, 128), F32)],
            scratch_shapes=list(scratch),
            input_output_aliases=aliases or {},
            cost_estimate=pl.CostEstimate(flops=int(cost * COST), transcendentals=0, bytes_accessed=1),
            compiler_params=pltpu.CompilerParams(vmem_limit_bytes=VMEM_BYTES),
        )(*placed)
        self.tick = results[-1]
        return results[:-1]


def run_together(order, jobs):
    steps = [(body, len(operands), len(outs)) for body, operands, outs, _ in jobs]
    results = order.run(
        functools.partial(together, steps), 1, [a for job in jobs for a in job[1]], [o for job in jobs for o in job[2]]
    )
    for _, _, outs, then in jobs:
        then(*results[: len(outs)])
        results = results[len(outs) :]


def swap(value, axis, size, bit):
    return lax.ppermute(value, axis, [(k, k ^ bit) for k in range(size)])


class MpSum:
    def __init__(self, order, size, keep, *sends):
        self.order, self.size, self.keep = order, size, keep
        self.near = [swap(send, "mp", size, 1) for send in sends]

    def add(self):
        own = self.order.run(add_parts, 0.5, (self.keep, *self.near), (near_like(self.keep),))[0]
        self.spread(own)

    def spread(self, own):
        self.own = own
        self.far = swap(own, "mp", self.size, 2)

    def meet(self):
        run_together(self.order, [self.meet_job()])

    def meet_job(self):
        return add_rows, (self.own, self.far), (near_like(self.own),), self.share

    def share(self, total):
        self.pieces = total, swap(total, "mp", self.size, 1)


class PairSum(MpSum):
    def __init__(self, order, size, keeps, sends):
        self.order, self.size, self.keeps = order, size, keeps
        self.near = [swap(send, "mp", size, 1) for send in sends]

    def job(self):
        count = len(self.keeps)
        stack = near_like(self.keeps[0], (count,) + self.keeps[0].shape)
        parts = [part for pair in zip(self.keeps, self.near) for part in pair]
        return functools.partial(add_stack, count), parts, (stack,), self.spread


class DpSum:
    def __init__(self, order, size, steps, keep, send):
        self.order, self.size, self.steps = order, size, steps
        self.keep, self.near = keep, self.swap(send, 0)
        self.stage = 0

    def swap(self, value, step):
        return swap(value, "dp", self.size, self.steps[step])

    def step(self):
        run_together(self.order, [self.job()])

    def job(self):
        dims, stage = self.keep.shape, self.stage
        self.stage += 1
        both_parts = (self.keep, self.near)
        if stage < 2:
            out = near_like(self.keep, (dims[0] // 2,) + dims[1:])

            def then(keep, send):
                self.keep, self.near = keep, self.swap(send, stage + 1)

            return add_split, both_parts, (out, out), then
        if stage == 2:

            def then(total):
                bit = 8
                while bit < self.size:
                    other = swap(total, "dp", self.size, bit)
                    total = self.order.run(add_rows, 0.5, (total, other), (near_like(total),))[0]
                    bit *= 2
                self.keep, self.near = total, self.swap(total, 2)

            return add_rows, both_parts, (near_like(self.keep),), then
        out = near_like(self.keep, (dims[0] * 2,) + dims[1:])

        def then(total):
            self.keep, self.near = total, self.swap(total, 4 - stage)

        return stack_pair, both_parts, (out,), then

    def unpack(self, matrices, lines, *more):
        rows = 8 * self.keep.shape[1]
        specs = [pl.BlockSpec(o.shape, lambda *_: (0, 0)) for o in matrices]
        specs += [pl.BlockSpec(o.shape, lambda *_: (0,)) for o in lines] + [NEAR] * len(more)
        return self.order.run(
            functools.partial(unpack, len(matrices), len(lines), self.steps), 3, (self.keep, self.near),
            tuple(matrices) + tuple(lines) + more, (pltpu.VMEM((rows, matrices[0].shape[1]), F32),), None, specs,
        )


def shards(sizes, *arguments):
    (
        hidden, encoder, lengths, tasks, frames, out_grad,
        gain_self, shift_self, query_self, qbias_self, key_self, value_self, vbias_self, output_self, obias_self,
        gain_cross, shift_cross, query_cross, qbias_cross, key_cross, value_cross, vbias_cross, output_cross, obias_cross,
        gain_feed, shift_feed, expand_weight, expand_bias, contract_weight, contract_bias,
    ) = arguments
    n_mp, n_dp = sizes["mp"], sizes["dp"]
    items, length, width = hidden.shape
    memory_len = encoder.shape[1]
    rows = query_self.shape[1]
    heads = rows // HEAD
    units = expand_weight.shape[1]
    wide = -(-memory_len // 512) * 512
    chunk = 512
    half = length // 2
    wq1, wk1, wv1 = query_self.T, key_self.T, value_self.T
    wq2, wk2, wv2 = query_cross.T, key_cross.T, value_cross.T

    low_rows = near_shape((rows, length))
    mem_rows = near_shape((rows, wide))
    half_outs = (near_shape((half, width)), near_shape((half // 2, width)), near_shape((half - half // 2, width)))
    state = near_shape((length, width), F32)
    low_state = near_shape((length, width))
    unit_state = near_shape((length, units))
    vec_out = near_shape((8, width), F32)
    lse_out = near_shape((8, length), F32)
    aug_out = near_shape((heads, AUG, length))
    aug_mem = near_shape((heads, AUG, wide))
    mem_half = near_shape((2, rows, memory_len))
    pair_outs = (near_shape((half, width)), near_shape((half, width)))
    whole = pltpu.VMEM((length, width), F32)
    aug = pltpu.VMEM((AUG, length), BF16)
    row_scratch = pltpu.VMEM((rows, length), BF16)
    span = range(items)
    bind = functools.partial
    order = Order()

    def mp_sum(*parts):
        return MpSum(order, n_mp, *parts)

    def pack_outs(count):
        return (near_shape((4, count // 8, width)),) * 2, (pltpu.VMEM((count, width), F32),)

    def keys(i):
        return order.run(
            bind(cross_keys, i), 3, (frames, encoder, wk2, wv2, vbias_cross),
            (aug_mem, aug_mem), (), {1: chosen(encoder, i)},
        )

    self_out, self_sum, cross_kv = [], [], []
    loads = (
        hidden, gain_self, shift_self, wq1, qbias_self, wk1, wv1, vbias_self, output_self,
        wk2, wv2, vbias_cross, obias_self, gain_cross, shift_cross, wq2, qbias_cross, output_cross,
        out_grad, obias_cross, gain_feed, shift_feed, expand_weight, expand_bias, contract_weight, contract_bias,
    )
    self_outs = (low_rows, aug_out, aug_out, low_rows, lse_out, *half_outs)
    for i in span:
        if i == 0:
            out = order.run(
                bind(first_forward, i, 9, len(loads)), 4, (lengths, *loads),
                self_outs + tuple(near_like(a) for a in loads), (aug, pltpu.SemaphoreType.DMA((len(loads),))),
                {k + 1: AWAY for k in range(len(loads))},
            )
            near = out[8:]
            hidden, gain_self, shift_self, wq1, qbias_self, wk1, wv1, vbias_self, output_self = near[:9]
            wk2, wv2, vbias_cross, obias_self, gain_cross, shift_cross, wq2, qbias_cross, output_cross = near[9:18]
            out_grad, obias_cross, gain_feed, shift_feed, expand_weight, expand_bias, contract_weight, contract_bias = near[18:]
        else:
            operands = (lengths, hidden, gain_self, shift_self, wq1, qbias_self, wk1, wv1, vbias_self, output_self)
            out = order.run(bind(self_forward, i), 4, operands, self_outs, (aug,))
        self_out.append(out)
        self_sum.append(mp_sum(*out[5:8]))
    for i in span:
        self_sum[i].add()
        cross_kv.append(keys(i))

    cross_out, cross_sum = [], []
    for i in span:
        self_sum[i].meet()
        out = order.run(
            bind(cross_forward, i, wide), 6,
            (hidden, *self_sum[i].pieces, obias_self, gain_cross, shift_cross, wq2, qbias_cross, output_cross, *cross_kv[i]),
            (state, low_state, low_rows, low_rows, lse_out, *half_outs), (whole, aug),
        )
        cross_out.append(out)
        cross_sum.append(mp_sum(*out[5:8]))
        cross_sum[i].add()

    feed_out, feed_sum = [], []
    for i in span:
        cross_sum[i].meet()
        out = order.run(
            bind(feed, i), 4,
            (lengths, tasks, cross_out[i][0], *cross_sum[i].pieces, out_grad, obias_cross, gain_feed, shift_feed, expand_weight, expand_bias, contract_weight),
            (state, low_state, unit_state, unit_state, low_state, vec_out, *half_outs), (whole,),
        )
        feed_out.append(out)
        feed_sum.append(mp_sum(*out[6:9]))
        feed_sum[i].add()
    back_out, back_sum = [], []
    for i in span:
        _, _, q2, o2, lse2 = cross_out[i][:5]
        feed_sum[i].meet()
        if i == 0:
            outs, scratch = pack_outs(width + units + 64)
            operands = [out[k] for k in (1, 3, 2, 4, 5) for out in feed_out]
            feed_dp = DpSum(order, n_dp, X_FIRST, *order.run(bind(feed_weights, items), 2, operands, outs, scratch))
        out = order.run(
            bind(cross_backward, i, chunk), 9,
            (lengths, tasks, feed_out[i][0], *feed_sum[i].pieces, out_grad, gain_feed, output_cross, wq2, *cross_kv[i], q2, o2, lse2),
            (state, low_state, low_rows, mem_rows, mem_rows, vec_out, *half_outs), (whole, aug, aug, row_scratch),
        )
        back_out.append(out)
        back_sum.append(mp_sum(*out[6:9]))
        back_sum[i].add()

    self_back = []
    outs, scratch = pack_outs(4 * rows + 64)
    for i in span:
        q1, ka1, va1, o1, lse1 = self_out[i][:5]
        back_sum[i].meet()
        if i == 0:
            feed_dp.step()
        out = order.run(
            bind(self_backward, i), 5,
            (cross_out[i][0], *back_sum[i].pieces, back_out[i][0], hidden, gain_cross, output_self, wq1, wk1, wv1, ka1, va1, q1, o1, lse1),
            (state, low_state, near_shape((3 * rows, length)), vec_out, *pair_outs), (whole, aug, aug, row_scratch),
        )
        self_back.append(out)
        if i == 0:
            operands = [encoder] + [out[2] for out in back_out] + [out[1] for out in cross_out] + [out[3] for out in cross_out]
            operands += [out[1] for out in back_out] + [out[3] for out in back_out] + [out[4] for out in back_out]
            operands += [out[5] for out in back_out]
            made = order.run(
                bind(cross_weights, items), 3, operands, outs, scratch,
                {0: pl.BlockSpec(encoder.shape, lambda *_: (0, 0, 0))},
            )
            cross_dp = DpSum(order, n_dp, X_FIRST, *made)
    operands = [hidden, gain_self, shift_self] + [out[2] for out in self_back] + [out[3] for out in self_out]
    operands += [out[1] for out in self_back]
    grad_shape, block_shape = shape(hidden.shape, F32), shape(hidden.shape, BF16)
    mem_half, memory_out = near_shape((2, rows, memory_len)), near_shape((items, rows, memory_len))
    line_out, bias_out, matrix = shape((width,), F32), shape((rows,), F32), shape((rows, width), F32)
    lines = (line_out, line_out, line_out, bias_out, bias_out)
    whole_cube = [pl.BlockSpec(hidden.shape, lambda *_: (0, 0, 0))]
    got = {}

    def rows_self():
        vec = order.run(sum_rows, 0.3, [out[3] for out in self_back], (vec_out,))[0]
        got["V"] = [vec] + [swap(vec, "mp", n_mp, bit) for bit in (1, 2, 3)]

    def pack_self():
        made = order.run(bind(self_weights, items), 3, operands + got["V"], outs, scratch)
        got["S"] = DpSum(order, n_dp, X_FIRST, *made)

    def last_finish():
        got["hidden"] = order.run(
            bind(finish_grad, items), 4, [out[0] for out in self_back] + list(got["last"].pieces) + [hidden, gain_self],
            (grad_shape,), (whole,), None, whole_cube,
        )[0]

    def memory(i):
        part = order.run(memory_grad, 2, (wk2, wv2, back_out[i][3], back_out[i][4]), (mem_half, mem_half))
        got["m", i] = part

    def memory_swap():
        for i in span:
            keep, send = got["m", i]
            got["m", i] = keep, swap(order.later(send), "mp", n_mp, 1)

    def memory_finish():
        got["encoder"] = order.run(
            finish_memory, 2, got["far"], (shape((items, rows, memory_len), F32),), (), None,
            [pl.BlockSpec((items, rows, memory_len), lambda *_: (0, 0, 0))],
        )[0].transpose(0, 2, 1)

    def block_part(i):
        keep, send = order.run(feed_out_part, 1, (feed_out[i][2], contract_weight), pair_outs)
        got["b", i] = keep, send

    def block_finish():
        got["out"] = order.run(
            bind(finish_out, items), 3, [out[0] for out in feed_out] + list(got["block"].pieces) + [contract_bias],
            (block_shape,), (whole,), None, whole_cube,
        )[0]

    def unpack_feed():
        got["f"] = feed_dp.unpack(
            (shape((width, width), F32), shape((units, width), F32)), (line_out, shape((units,), F32))
        )

    def unpack_cross():
        got["x"] = cross_dp.unpack((matrix,) * 4, lines)

    def unpack_self():
        got["s"] = got["S"].unpack((matrix,) * 4, lines + (line_out, line_out))

    def job(which):
        if which in "FXS":
            return {"F": feed_dp, "X": cross_dp, "S": got.get("S")}[which].job()
        if which == "l":
            got["last"] = PairSum(order, n_mp, [out[4] for out in self_back], [order.later(out[5]) for out in self_back])
            return got["last"].job()
        if which == "b":
            return got["block"].job()
        if which == "m":
            return got["last"].meet_job()
        if which == "c":
            return got["block"].meet_job()
        parts = [got["m", i] for i in span]

        def then(kept, sent):
            got["far"] = kept, swap(sent, "mp", n_mp, 2)

        return bind(add_memory, items), [p[0] for p in parts] + [p[1] for p in parts], (memory_out, memory_out), then

    def block_swap():
        sends = [order.later(got["b", i][1]) for i in span]
        got["block"] = PairSum(order, n_mp, [got["b", i][0] for i in span], sends)

    acts = dict(
        M=memory_swap, N=block_swap, P=pack_self, V=rows_self, g=last_finish, A=lambda: [memory(i) for i in span], e=memory_finish,
        B=lambda: [block_part(i) for i in span], o=block_finish, u=unpack_feed, v=unpack_cross, w=unpack_self,
    )
    for word in ORDER:
        if word[0] in acts:
            for act in word:
                acts[act]()
        else:
            run_together(order, [job(which) for which in word])
    cross_grads, self_grads, feed_grads = got["x"], got["s"], got["f"]
    hidden_grad, encoder_grad, block_out = got["hidden"], got["encoder"], got["out"]
    return (
        block_out,
        hidden_grad,
        encoder_grad,
        self_grads[9],
        self_grads[10],
        self_grads[0].T,
        self_grads[7],
        self_grads[1].T,
        self_grads[2].T,
        self_grads[8],
        self_grads[3],
        self_grads[6],
        self_grads[4],
        self_grads[5],
        cross_grads[0].T,
        cross_grads[7],
        cross_grads[1].T,
        cross_grads[2].T,
        cross_grads[8],
        cross_grads[3],
        cross_grads[6],
        cross_grads[4],
        cross_grads[5],
        feed_grads[0],
        feed_grads[3],
        feed_grads[1],
        feed_grads[2],
    )


def solution(mesh):
    column, row, flat = P(None, "mp"), P("mp", None), P("mp")
    cube = P("dp", None, None)
    attention = (P(), P(), column, flat, column, column, flat, row, P())
    grads = (P(), P(), column, flat, column, column, flat, row, P())
    return jax.shard_map(
        functools.partial(shards, dict(mesh.shape)),
        mesh=mesh,
        in_specs=(cube, cube, P("dp"), P("dp"), P("dp"), cube)
        + attention
        + attention
        + (P(), P(), column, flat, row, P()),
        out_specs=(cube, cube, P("dp", None, "mp")) + grads + grads + (P(), P(), column, flat, row, P()),
        check_vma=False,
    )
```

```python
import functools
import math

import jax
import jax.numpy as jnp
from jax import lax
from jax.experimental import pallas as pl
from jax.experimental.pallas import tpu as pltpu
from jax.sharding import PartitionSpec as P

HEAD = 64
AUG = 80
EPS = 1e-05
NEG = -1e30
F32 = jnp.float32
BF16 = jnp.bfloat16
ROOT_HALF = math.sqrt(0.5)
INV_ROOT_TAU = 1.0 / math.sqrt(2.0 * math.pi)
VMEM_BYTES = 20 * 1024 * 1024
COST = 1
ORDER = ("VAP", "B", "FX", "M", "FXSa", "FXSl", "e", "N", "b", "FXSm", "XSc", "u", "S", "g", "v", "o", "w")


def dot(left, right, left_dim, right_dim):
    return lax.dot_general(
        left, right, (((left_dim,), (right_dim,)), ((), ())), preferred_element_type=F32
    )


def nn(left, right):
    return dot(left, right, 1, 0)


def nt(left, right):
    return dot(left, right, 1, 1)


def tn(left, right):
    return dot(left, right, 0, 0)


def iota(shape, axis):
    return lax.broadcasted_iota(jnp.int32, shape, axis)


def norm_parts(values):
    centred = values - jnp.mean(values, axis=-1, keepdims=True)
    spread = jnp.mean(centred * centred, axis=-1, keepdims=True)
    scale = lax.rsqrt(spread + EPS)
    return centred * scale, scale


def norm_back(values, gain, upstream):
    unit, scale = norm_parts(values)
    inner = upstream * gain
    first = jnp.mean(inner, axis=-1, keepdims=True)
    second = jnp.mean(inner * unit, axis=-1, keepdims=True)
    grad = scale * (inner - first - unit * second)
    return (
        grad,
        jnp.sum(upstream * unit, axis=0, keepdims=True),
        jnp.sum(upstream, axis=0, keepdims=True),
    )


def line(ref):
    return ref[...].astype(F32).reshape(1, ref.shape[0])


def column_bias(ref, count):
    first = jnp.where(iota((16, ref.shape[0]), 0) == 0, line(ref), 0.0).astype(BF16)
    return tn(first, jnp.ones((16, count), BF16))


def mp_side():
    return lax.axis_index("mp") % 2


def key_extra(count, limit):
    rows = iota((16, count), 0)
    hidden_keys = jnp.where(iota((16, count), 1) < limit, 0.0, NEG)
    ones = jnp.where(rows < 4, 1.0, 0.0)
    return jnp.where(rows == 0, hidden_keys, ones).astype(BF16)


def value_extra(count):
    return jnp.where(iota((16, count), 0) < 3, 1.0, 0.0).astype(BF16)


def three_parts(row):
    high = row.astype(BF16)
    rest = row - high.astype(F32)
    middle = rest.astype(BF16)
    last = (rest - middle.astype(F32)).astype(BF16)
    return high.astype(F32), middle.astype(F32), last.astype(F32)


def split_rows(rows, row, first, with_one):
    high, middle, last = three_parts(row)
    base = jnp.where(rows == 0, 1.0, 0.0) if with_one else jnp.zeros(rows.shape, F32)
    out = jnp.where(rows == first, high, base)
    out = jnp.where(rows == first + 1, middle, out)
    return jnp.where(rows == first + 2, last, out).astype(BF16)


def store_halves(part, side, keep_ref, send_ref, rest_ref=None):
    half = part.shape[0] // 2
    edge = send_ref.shape[0]
    low = part.astype(BF16)

    @pl.when(side == 0)
    def _():
        keep_ref[...] = low[:half]
        send_ref[...] = low[half : half + edge]
        if rest_ref is not None:
            rest_ref[...] = low[half + edge :]

    @pl.when(side == 1)
    def _():
        keep_ref[...] = low[half:]
        send_ref[...] = low[:edge]
        if rest_ref is not None:
            rest_ref[...] = low[edge:half]


def join_halves(pieces, side, scratch):
    own, other = pieces
    half = own.shape[0]
    scratch[pl.ds(pl.multiple_of(side * half, 16), half), :] = own[...].astype(F32)
    scratch[pl.ds(pl.multiple_of((1 - side) * half, 16), half), :] = other[...].astype(F32)
    return scratch[...]


def attend_block(keys, queries, keep):
    scores = tn(keys, queries)
    if keep is not None:
        scores = jnp.where(keep, scores, NEG)
    return scores


def causal_mask(count):
    return iota((count, count), 0) <= iota((count, count), 1)


def attention_forward(q_ref, ka_ref, va_ref, qa, o_ref, lse_ref, chunk, causal):
    heads, _, keys = ka_ref.shape
    count = q_ref.shape[1]
    rows = iota((16, count), 0)
    qa[HEAD:AUG, :] = jnp.where(rows == 0, 1.0, 0.0).astype(BF16)
    keep = causal_mask(count) if causal else None
    lse_rows = iota((8, count), 0)
    lse = jnp.zeros((8, count), F32)
    for head in range(heads):
        spot = slice(head * HEAD, (head + 1) * HEAD)
        qa[0:HEAD, :] = q_ref[spot, :]
        queries = qa[...]
        largest = None
        for start in range(0, keys, chunk):
            part = slice(start, start + chunk)
            scores = attend_block(ka_ref[head, :, part], queries, keep)
            top = jnp.max(scores, axis=0, keepdims=True)
            if largest is None:
                powers = jnp.exp(scores - top).astype(BF16)
                mixed = nn(va_ref[head, :, part], powers)
                largest = top
            else:
                newer = jnp.maximum(largest, top)
                powers = jnp.exp(scores - newer).astype(BF16)
                mixed = mixed * jnp.exp(largest - newer) + nn(va_ref[head, :, part], powers)
                largest = newer
        total = mixed[HEAD : HEAD + 1]
        o_ref[spot, :] = (mixed[0:HEAD] / total).astype(BF16)
        lse = jnp.where(lse_rows == head, largest + jnp.log(total), lse)
    lse_ref[...] = lse


def attention_backward(
    q_ref, ka_ref, va_ref, o_ref, lse_ref, do_ref, qa, doa, dq_ref, dk_ref, dv_ref, chunk, causal
):
    heads, _, keys = ka_ref.shape
    count = q_ref.shape[1]
    rows = iota((16, count), 0)
    keep = causal_mask(count) if causal else None
    for head in range(heads):
        spot = slice(head * HEAD, (head + 1) * HEAD)
        queries = q_ref[spot, :]
        mix_grad = do_ref[spot, :]
        qa[0:HEAD, :] = queries
        doa[0:HEAD, :] = mix_grad
        qa[HEAD:AUG, :] = split_rows(rows, -lse_ref[head : head + 1, :], 1, True)
        centre = jnp.sum(
            mix_grad.astype(F32) * o_ref[spot, :].astype(F32), axis=0, keepdims=True
        )
        doa[HEAD:AUG, :] = split_rows(rows, -centre, 0, False)
        query_side = qa[...]
        grad_side = doa[...]
        query_grad = jnp.zeros((HEAD, count), F32)
        for start in range(0, keys, chunk):
            part = slice(start, start + chunk)
            shares = jnp.exp(attend_block(ka_ref[head, :, part], query_side, keep))
            pushed = tn(va_ref[head, :, part], grad_side)
            score_grad = (shares * pushed).astype(BF16)
            dv_ref[spot, part] = nt(mix_grad, shares.astype(BF16)).astype(BF16)
            dk_ref[spot, part] = nt(queries, score_grad).astype(BF16)
            query_grad = query_grad + nn(ka_ref[head, 0:HEAD, part], score_grad)
        dq_ref[spot, :] = (query_grad * 0.125).astype(BF16)


def row_of_sums(matrix):
    ones = jnp.ones((16, matrix.shape[1]), BF16)
    return nt(ones, matrix)[0:1]


def self_forward(item, lengths, x_ref, gain, shift, wq, qbias, wk, wv, vbias, wo, q_o, ka_o, va_o, o_o, lse_o, keep_o, send_o, rest_o, qa):
    count = x_ref.shape[1]
    unit, _ = norm_parts(x_ref[item].astype(F32))
    normed = (unit * line(gain) + line(shift)).astype(BF16)
    queries = (nt(wq[...], normed) + column_bias(qbias, count)).astype(BF16)
    q_o[...] = queries * jnp.asarray(0.125, BF16)
    key_rows = nt(wk[...], normed).astype(BF16)
    value_rows = (nt(wv[...], normed) + column_bias(vbias, count)).astype(BF16)
    extra = key_extra(count, lengths[item])
    other = value_extra(count)
    for head in range(ka_o.shape[0]):
        spot = slice(head * HEAD, (head + 1) * HEAD)
        ka_o[head, 0:HEAD, :] = key_rows[spot]
        ka_o[head, HEAD:AUG, :] = extra
        va_o[head, 0:HEAD, :] = value_rows[spot]
        va_o[head, HEAD:AUG, :] = other
    attention_forward(q_o, ka_o, va_o, qa, o_o, lse_o, count, True)
    store_halves(tn(o_o[...], wo[...]), mp_side(), keep_o, send_o, rest_o)


def first_forward(item, first, count, lengths, *refs):
    sources, targets = refs[:count], refs[count + 8 : 2 * count + 8]
    outs, qa, sems = refs[count : count + 8], refs[-2], refs[-1]
    copies = [pltpu.make_async_copy(s, t, sems.at[k]) for k, (s, t) in enumerate(zip(sources, targets))]
    for copy in copies:
        copy.start()
    for copy in copies[:first]:
        copy.wait()
    self_forward(item, lengths, *targets[:first], *outs, qa)
    for copy in copies[first:]:
        copy.wait()


def cross_keys(item, frames, enc, wk, wv, vbias, ka_o, va_o):
    count = enc.shape[0]
    wide = ka_o.shape[2]
    memory = enc[...]
    key_rows = nt(wk[...], memory).astype(BF16)
    value_rows = (nt(wv[...], memory) + column_bias(vbias, count)).astype(BF16)
    extra = key_extra(wide, frames[item])
    other = value_extra(wide)
    for head in range(ka_o.shape[0]):
        spot = slice(head * HEAD, (head + 1) * HEAD)
        if wide > count:
            ka_o[head, 0:HEAD, wide - 128 :] = jnp.zeros((HEAD, 128), BF16)
            va_o[head, 0:HEAD, wide - 128 :] = jnp.zeros((HEAD, 128), BF16)
        ka_o[head, 0:HEAD, 0:count] = key_rows[spot]
        ka_o[head, HEAD:AUG, :] = extra
        va_o[head, 0:HEAD, 0:count] = value_rows[spot]
        va_o[head, HEAD:AUG, :] = other


def cross_forward(item, chunk, x_ref, s0, s1, obias, gain, shift, wq, qbias, wo, ka, va, x1_o, h2_o, q_o, o_o, lse_o, keep_o, send_o, rest_o, whole, qa):
    count = x_ref.shape[1]
    side = mp_side()
    after = x_ref[item].astype(F32) + join_halves((s0, s1), side, whole) + line(obias)
    x1_o[...] = after
    unit, _ = norm_parts(after)
    normed = (unit * line(gain) + line(shift)).astype(BF16)
    h2_o[...] = normed
    queries = (nt(wq[...], normed) + column_bias(qbias, count)).astype(BF16)
    q_o[...] = queries * jnp.asarray(0.125, BF16)
    attention_forward(q_o, ka, va, qa, o_o, lse_o, chunk, False)
    store_halves(tn(o_o[...], wo[...]), side, keep_o, send_o, rest_o)


def upstream_rows(item, lengths, tasks, og):
    task = tasks[item]
    weight = jnp.where(task == 0, 1.0, jnp.where(task == 1, 0.6, 2.0)).astype(F32)
    valid = iota((og.shape[1], 1), 0) < lengths[item]
    return og[item].astype(F32) * jnp.where(valid, weight, 0.0)


def feed(item, lengths, tasks, x1, s0, s1, og, obias, gain, shift, we, ebias, wc, x2_o, h3_o, a_o, dz_o, gy_o, vec_o, bkeep_o, bsend_o, brest_o, whole):
    side = mp_side()
    after = x1[...] + join_halves((s0, s1), side, whole) + line(obias)
    x2_o[...] = after
    unit, _ = norm_parts(after)
    normed = (unit * line(gain) + line(shift)).astype(BF16)
    h3_o[...] = normed
    before = nn(normed, we[...]) + line(ebias)
    share = 0.5 + 0.5 * lax.erf(before * ROOT_HALF)
    active = (before * share).astype(BF16)
    a_o[...] = active
    slope = share + before * (jnp.exp(before * before * -0.5) * INV_ROOT_TAU)
    grad = upstream_rows(item, lengths, tasks, og)
    low = grad.astype(BF16)
    gy_o[...] = low
    inner = (nt(low, wc[...]) * slope).astype(BF16)
    dz_o[...] = inner
    store_halves(nt(inner, we[...]), side, bkeep_o, bsend_o, brest_o)
    pick = iota((8, vec_o.shape[1]), 0)
    out = jnp.where(pick == 0, jnp.sum(grad, axis=0, keepdims=True), 0.0)
    vec_o[...] = jnp.where(pick == 1, jnp.sum(inner.astype(F32), axis=0, keepdims=True), out)


def feed_out_part(active, wc, keep_o, send_o):
    store_halves(nn(active[...], wc[...]), mp_side(), keep_o, send_o)


def sum_of(refs):
    out = refs[0]
    for other in refs[1:]:
        out = out + other
    return out


def feed_weights(items, *refs):
    h3, dz, a, gy, vecs = (refs[k * items : (k + 1) * items] for k in range(5))
    keep_o, send_o, whole = refs[5 * items :]
    width = h3[0].shape[1]
    edge = width + dz[0].shape[1]
    whole[0:width, :] = sum_of([tn(h3[k][...], dz[k][...]) for k in range(items)])
    whole[width:edge, :] = sum_of([tn(a[k][...], gy[k][...]) for k in range(items)])
    whole[edge:, :] = jnp.zeros((whole.shape[0] - edge, width), F32)
    whole[edge : edge + 8, :] = sum_of([v[...] for v in vecs])
    scatter_blocks(whole, keep_o, send_o, X_FIRST)


def cross_backward(item, chunk, lengths, tasks, x2, s0, s1, og, gain, wo, wq, ka, va, q, o, lse, dx2_o, g2_o, dq_o, dk_o, dv_o, vec_o, keep_o, send_o, rest_o, whole, qa, doa, do):
    side = mp_side()
    grad_in = join_halves((s0, s1), side, whole)
    grad, gain_row, shift_row = norm_back(x2[...], line(gain), grad_in)
    total = upstream_rows(item, lengths, tasks, og) + grad
    dx2_o[...] = total
    low = total.astype(BF16)
    g2_o[...] = low
    do[...] = nt(wo[...], low).astype(BF16)
    attention_backward(q, ka, va, o, lse, do, qa, doa, dq_o, dk_o, dv_o, chunk, False)
    store_halves(tn(dq_o[...], wq[...]), side, keep_o, send_o, rest_o)
    pick = iota((8, vec_o.shape[1]), 0)
    out = jnp.where(pick == 0, gain_row, 0.0)
    out = jnp.where(pick == 1, shift_row, out)
    vec_o[...] = jnp.where(pick == 2, jnp.sum(total, axis=0, keepdims=True), out)
    vec_o[3:4, 0 : dq_o.shape[0]] = row_of_sums(dq_o[...])
    vec_o[4:5, 0 : dq_o.shape[0]] = row_of_sums(dv_o[...])


def memory_grad(wk, wv, dk, dv, keep_o, send_o):
    count = keep_o.shape[2]
    position = lax.axis_index("mp")
    rows = keep_o.shape[1]
    whole = (tn(wk[...], dk[...]) + tn(wv[...], dv[...])).astype(BF16)
    for block in range(4):
        piece = whole[block * rows : (block + 1) * rows, 0:count]
        relative = lax.bitwise_xor(position, block)
        slot = relative // 2

        @pl.when(relative % 2 == 0)
        def _():
            keep_o[slot] = piece

        @pl.when(relative % 2 == 1)
        def _():
            send_o[slot] = piece


X_FIRST = (1, 2, 4)
Z_FIRST = (2, 4, 1)


def place_of(block, steps):
    place = 0
    for bit in steps:
        place = place * 2 + block // bit % 2
    return place


def scatter_blocks(whole, keep_o, send_o, steps):
    position = lax.axis_index("dp") % 8
    rows = keep_o.shape[1]
    for block in range(8):
        place = place_of(lax.bitwise_xor(position, block), steps)
        piece = whole[block * rows : (block + 1) * rows, :].astype(BF16)

        @pl.when(place < 4)
        def _():
            keep_o[place] = piece

        @pl.when(place >= 4)
        def _():
            send_o[place - 4] = piece


def gather_blocks(near, far, whole, steps):
    position = lax.axis_index("dp") % 8
    rows = near.shape[1]
    for block in range(8):
        place = place_of(lax.bitwise_xor(position, block), steps)
        spot = slice(block * rows, (block + 1) * rows)

        @pl.when(place < 4)
        def _():
            whole[spot, :] = near[place].astype(F32)

        @pl.when(place >= 4)
        def _():
            whole[spot, :] = far[place - 4].astype(F32)


def cross_weights(items, enc, *refs):
    dq, h2, o, g2, dk, dv, vecs = (refs[k * items : (k + 1) * items] for k in range(7))
    keep_o, send_o, whole = refs[7 * items :]
    rows = dq[0].shape[0]
    count = enc.shape[1]
    span = range(items)
    whole[0:rows, :] = sum_of([nn(dq[k][...], h2[k][...]) for k in span])
    whole[rows : 2 * rows, :] = sum_of([nn(dk[k][:, 0:count], enc[k]) for k in span])
    whole[2 * rows : 3 * rows, :] = sum_of([nn(dv[k][:, 0:count], enc[k]) for k in span])
    whole[3 * rows : 4 * rows, :] = sum_of([nn(o[k][...], g2[k][...]) for k in span])
    whole[4 * rows :, :] = jnp.zeros((whole.shape[0] - 4 * rows, whole.shape[1]), F32)
    whole[4 * rows : 4 * rows + 8, :] = sum_of([v[...] for v in vecs])
    scatter_blocks(whole, keep_o, send_o, X_FIRST)


def self_backward(item, x1, s0, s1, dx2, x_ref, gain, wo, wq, wk, wv, ka, va, q, o, lse, dx1_o, g1_o, dqkv_o, vec_o, keep_o, send_o, whole, qa, doa, do):
    side = mp_side()
    grad_in = join_halves((s0, s1), side, whole)
    grad, gain_row, shift_row = norm_back(x1[...], line(gain), grad_in)
    total = dx2[...] + grad
    dx1_o[...] = total
    low = total.astype(BF16)
    g1_o[...] = low
    do[...] = nt(wo[...], low).astype(BF16)
    rows = do.shape[0]
    dq_o = dqkv_o.at[0:rows]
    dk_o = dqkv_o.at[rows : 2 * rows]
    dv_o = dqkv_o.at[2 * rows : 3 * rows]
    attention_backward(q, ka, va, o, lse, do, qa, doa, dq_o, dk_o, dv_o, q.shape[1], True)
    part = tn(dq_o[...], wq[...]) + tn(dk_o[...], wk[...]) + tn(dv_o[...], wv[...])
    store_halves(part, side, keep_o, send_o)
    unit, _ = norm_parts(x_ref[item].astype(F32))
    pick = iota((8, vec_o.shape[1]), 0)
    out = jnp.where(pick == 0, gain_row, 0.0)
    out = jnp.where(pick == 1, shift_row, out)
    out = jnp.where(pick == 2, jnp.sum(total, axis=0, keepdims=True), out)
    out = jnp.where(pick == 5, jnp.sum(part * unit, axis=0, keepdims=True), out)
    vec_o[...] = jnp.where(pick == 6, jnp.sum(part, axis=0, keepdims=True), out)
    vec_o[3:4, 0:rows] = row_of_sums(dq_o[...])
    vec_o[4:5, 0:rows] = row_of_sums(dv_o[...])


def sum_rows(*refs):
    refs[-1][...] = sum_of([ref[...] for ref in refs[:-1]])


def self_weights(items, x_ref, gain, shift, *refs):
    dqkv, o, g1 = (refs[k * items : (k + 1) * items] for k in range(3))
    vec, near, far, across, keep_o, send_o, whole = refs[3 * items :]
    rows = o[0].shape[0]
    span = range(items)
    normed = []
    for k in span:
        unit, _ = norm_parts(x_ref[k].astype(F32))
        normed.append((unit * line(gain) + line(shift)).astype(BF16))
    whole[0 : 3 * rows, :] = sum_of([nn(dqkv[k][...], normed[k]) for k in span])
    whole[3 * rows : 4 * rows, :] = sum_of([nn(o[k][...], g1[k][...]) for k in span])
    whole[4 * rows :, :] = jnp.zeros((whole.shape[0] - 4 * rows, whole.shape[1]), F32)
    summed = (vec[...] + near[...]) + (far[...] + across[...])
    pick = iota((8, whole.shape[1]), 0)
    whole[4 * rows : 4 * rows + 8, :] = jnp.where((pick == 5) | (pick == 6), summed, vec[...])
    scatter_blocks(whole, keep_o, send_o, X_FIRST)


def unpack(matrices, lines, steps, near, far, *rest):
    outs, whole = rest[:-1], rest[-1]
    gather_blocks(near, far, whole, steps)
    start = 0
    for out in outs[:matrices]:
        out[...] = whole[start : start + out.shape[0], :]
        start += out.shape[0]
    for k, out in enumerate(outs[matrices : matrices + lines]):
        out[...] = whole[start + k : start + k + 1, 0 : out.shape[0]].reshape(out.shape)
    for out in outs[matrices + lines :]:
        out[...] = whole[start : start + out.shape[0], :]


def finish_out(items, *refs):
    x2, pieces, (bias, out, whole) = refs[:items], refs[items : items + 2], refs[items + 2 :]
    for k in range(items):
        total = x2[k][...] + join_halves([p.at[k] for p in pieces], mp_side(), whole) + line(bias)
        out[k] = total.astype(BF16)


def finish_grad(items, *refs):
    dx1, pieces, (x_ref, gain, out, whole) = refs[:items], refs[items : items + 2], refs[items + 2 :]
    for k in range(items):
        grad_in = join_halves([p.at[k] for p in pieces], mp_side(), whole)
        grad, _, _ = norm_back(x_ref[k].astype(F32), line(gain), grad_in)
        out[k] = dx1[k][...] + grad


def finish_memory(kept, far, out):
    for k in range(kept.shape[0]):
        out[k] = kept[k].astype(F32) + far[k].astype(F32)


def both(left, right):
    return (left.astype(F32) + right.astype(F32)).astype(BF16)


def add_rows(left, right, out):
    out[...] = both(left[...], right[...])


def add_parts(left, *rest):
    parts, out = rest[:-1], rest[-1]
    start = 0
    for part in parts:
        spot = slice(start, start + part.shape[0])
        out[spot] = both(left[spot], part[...])
        start += part.shape[0]


def add_stack(count, *refs):
    out = refs[-1]
    each = (len(refs) - 1) // count
    for k in range(count):
        add_parts(*refs[k * each : (k + 1) * each], out.at[k])


def add_memory(count, *refs):
    left, right, (kept, sent) = refs[:count], refs[count : 2 * count], refs[2 * count :]
    for k in range(count):
        kept[k] = both(left[k][0], right[k][0])
        sent[k] = both(left[k][1], right[k][1])


def add_split(left, right, keep, send):
    half = keep.shape[0]
    keep[...] = both(left[0:half], right[0:half])
    send[...] = both(left[half:], right[half:])


def together(steps, *refs):
    given = sum(step[1] for step in steps)
    ins, outs = refs[:given], refs[given:]
    for body, takes, gives in steps:
        body(*ins[:takes], *outs[:gives])
        ins, outs = ins[takes:], outs[gives:]


def stack_pair(left, right, out):
    half = left.shape[0]
    out[0:half] = left[...]
    out[half:] = right[...]


SCALARS = pl.BlockSpec(memory_space=pltpu.SMEM)
LEFT = pl.BlockSpec(memory_space=pl.ANY)
AWAY = pl.BlockSpec(memory_space=pltpu.HBM)
NEAR = pl.BlockSpec(memory_space=pltpu.VMEM)
FAR = pl.BlockSpec(memory_space=pltpu.VMEM)


def chosen(array, item):
    rest = (0,) * (len(array.shape) - 1)
    return pl.BlockSpec((None,) + tuple(array.shape[1:]), lambda *_: (item,) + rest)


def shape(dims, dtype):
    return jax.ShapeDtypeStruct(dims, dtype)


def near_shape(dims, dtype=BF16):
    return pltpu.VMEM(dims, dtype)


def near_like(array, dims=None):
    return pltpu.VMEM(tuple(dims or array.shape), array.dtype)


class Order:
    def __init__(self):
        self.tick = None

    def later(self, value):
        return lax.optimization_barrier((value, self.tick))[0]

    def run(self, body, cost, operands, outs, scratch=(), specs=None, out_specs=None, aliases=None):
        specs = specs or {}
        placed, in_specs = [], []
        for k, array in enumerate(operands):
            spec = specs.get(k, SCALARS if array.dtype == jnp.int32 else NEAR)
            if spec is NEAR:
                array = pltpu.with_memory_space_constraint(array, pltpu.VMEM)
            elif spec is AWAY:
                array = pltpu.with_memory_space_constraint(array, pltpu.HBM)
            placed.append(array)
            in_specs.append(spec)
        count = len(placed)
        if self.tick is not None:
            placed.append(pltpu.with_memory_space_constraint(self.tick, pltpu.VMEM))
            in_specs.append(NEAR)
        given, made = len(placed), len(outs)

        def whole_body(*refs):
            tick = refs[given + made]
            tick[...] = jnp.zeros(tick.shape, tick.dtype)
            body(*refs[:count], *refs[given : given + made], *refs[given + made + 1 :])

        inner = body
        while isinstance(inner, functools.partial):
            inner = inner.func
        results = pl.pallas_call(
            whole_body,
            name=inner.__name__,
            grid=(1,),
            in_specs=in_specs,
            out_specs=list(out_specs or [NEAR] * made) + [NEAR],
            out_shape=list(outs) + [near_shape((8, 128), F32)],
            scratch_shapes=list(scratch),
            input_output_aliases=aliases or {},
            cost_estimate=pl.CostEstimate(flops=int(cost * COST), transcendentals=0, bytes_accessed=1),
            compiler_params=pltpu.CompilerParams(vmem_limit_bytes=VMEM_BYTES),
        )(*placed)
        self.tick = results[-1]
        return results[:-1]


def run_together(order, jobs):
    steps = [(body, len(operands), len(outs)) for body, operands, outs, _ in jobs]
    results = order.run(
        functools.partial(together, steps), 1, [a for job in jobs for a in job[1]], [o for job in jobs for o in job[2]]
    )
    for _, _, outs, then in jobs:
        then(*results[: len(outs)])
        results = results[len(outs) :]


def swap(value, axis, size, bit):
    return lax.ppermute(value, axis, [(k, k ^ bit) for k in range(size)])


class MpSum:
    def __init__(self, order, size, keep, *sends):
        self.order, self.size, self.keep = order, size, keep
        self.near = [swap(send, "mp", size, 1) for send in sends]

    def add(self):
        own = self.order.run(add_parts, 0.5, (self.keep, *self.near), (near_like(self.keep),))[0]
        self.spread(own)

    def spread(self, own):
        self.own = own
        self.far = swap(own, "mp", self.size, 2)

    def meet(self):
        run_together(self.order, [self.meet_job()])

    def meet_job(self):
        return add_rows, (self.own, self.far), (near_like(self.own),), self.share

    def share(self, total):
        self.pieces = total, swap(total, "mp", self.size, 1)


class PairSum(MpSum):
    def __init__(self, order, size, keeps, sends):
        self.order, self.size, self.keeps = order, size, keeps
        self.near = [swap(send, "mp", size, 1) for send in sends]

    def job(self):
        count = len(self.keeps)
        stack = near_like(self.keeps[0], (count,) + self.keeps[0].shape)
        parts = [part for pair in zip(self.keeps, self.near) for part in pair]
        return functools.partial(add_stack, count), parts, (stack,), self.spread


class DpSum:
    def __init__(self, order, size, steps, keep, send):
        self.order, self.size, self.steps = order, size, steps
        self.keep, self.near = keep, self.swap(send, 0)
        self.stage = 0

    def swap(self, value, step):
        return swap(value, "dp", self.size, self.steps[step])

    def step(self):
        run_together(self.order, [self.job()])

    def job(self):
        dims, stage = self.keep.shape, self.stage
        self.stage += 1
        both_parts = (self.keep, self.near)
        if stage < 2:
            out = near_like(self.keep, (dims[0] // 2,) + dims[1:])

            def then(keep, send):
                self.keep, self.near = keep, self.swap(send, stage + 1)

            return add_split, both_parts, (out, out), then
        if stage == 2:

            def then(total):
                bit = 8
                while bit < self.size:
                    other = swap(total, "dp", self.size, bit)
                    total = self.order.run(add_rows, 0.5, (total, other), (near_like(total),))[0]
                    bit *= 2
                self.keep, self.near = total, self.swap(total, 2)

            return add_rows, both_parts, (near_like(self.keep),), then
        out = near_like(self.keep, (dims[0] * 2,) + dims[1:])

        def then(total):
            self.keep, self.near = total, self.swap(total, 4 - stage)

        return stack_pair, both_parts, (out,), then

    def unpack(self, matrices, lines, *more):
        rows = 8 * self.keep.shape[1]
        specs = [pl.BlockSpec(o.shape, lambda *_: (0, 0)) for o in matrices]
        specs += [pl.BlockSpec(o.shape, lambda *_: (0,)) for o in lines] + [NEAR] * len(more)
        return self.order.run(
            functools.partial(unpack, len(matrices), len(lines), self.steps), 3, (self.keep, self.near),
            tuple(matrices) + tuple(lines) + more, (pltpu.VMEM((rows, matrices[0].shape[1]), F32),), None, specs,
        )


def shards(sizes, *arguments):
    (
        hidden, encoder, lengths, tasks, frames, out_grad,
        gain_self, shift_self, query_self, qbias_self, key_self, value_self, vbias_self, output_self, obias_self,
        gain_cross, shift_cross, query_cross, qbias_cross, key_cross, value_cross, vbias_cross, output_cross, obias_cross,
        gain_feed, shift_feed, expand_weight, expand_bias, contract_weight, contract_bias,
    ) = arguments
    n_mp, n_dp = sizes["mp"], sizes["dp"]
    items, length, width = hidden.shape
    memory_len = encoder.shape[1]
    rows = query_self.shape[1]
    heads = rows // HEAD
    units = expand_weight.shape[1]
    wide = -(-memory_len // 512) * 512
    chunk = 512
    half = length // 2
    wq1, wk1, wv1 = query_self.T, key_self.T, value_self.T
    wq2, wk2, wv2 = query_cross.T, key_cross.T, value_cross.T

    low_rows = near_shape((rows, length))
    mem_rows = near_shape((rows, wide))
    half_outs = (near_shape((half, width)), near_shape((half // 2, width)), near_shape((half - half // 2, width)))
    state = near_shape((length, width), F32)
    low_state = near_shape((length, width))
    unit_state = near_shape((length, units))
    vec_out = near_shape((8, width), F32)
    lse_out = near_shape((8, length), F32)
    aug_out = near_shape((heads, AUG, length))
    aug_mem = near_shape((heads, AUG, wide))
    mem_half = near_shape((2, rows, memory_len))
    pair_outs = (near_shape((half, width)), near_shape((half, width)))
    whole = pltpu.VMEM((length, width), F32)
    aug = pltpu.VMEM((AUG, length), BF16)
    row_scratch = pltpu.VMEM((rows, length), BF16)
    span = range(items)
    bind = functools.partial
    order = Order()

    def mp_sum(*parts):
        return MpSum(order, n_mp, *parts)

    def pack_outs(count):
        return (near_shape((4, count // 8, width)),) * 2, (pltpu.VMEM((count, width), F32),)

    def keys(i):
        return order.run(
            bind(cross_keys, i), 3, (frames, encoder, wk2, wv2, vbias_cross),
            (aug_mem, aug_mem), (), {1: chosen(encoder, i)},
        )

    self_out, self_sum, cross_kv = [], [], []
    loads = (
        hidden, gain_self, shift_self, wq1, qbias_self, wk1, wv1, vbias_self, output_self,
        wk2, wv2, vbias_cross, obias_self, gain_cross, shift_cross, wq2, qbias_cross, output_cross,
        out_grad, obias_cross, gain_feed, shift_feed, expand_weight, expand_bias, contract_weight, contract_bias,
    )
    self_outs = (low_rows, aug_out, aug_out, low_rows, lse_out, *half_outs)
    for i in span:
        if i == 0:
            out = order.run(
                bind(first_forward, i, 9, len(loads)), 4, (lengths, *loads),
                self_outs + tuple(near_like(a) for a in loads), (aug, pltpu.SemaphoreType.DMA((len(loads),))),
                {k + 1: AWAY for k in range(len(loads))},
            )
            near = out[8:]
            hidden, gain_self, shift_self, wq1, qbias_self, wk1, wv1, vbias_self, output_self = near[:9]
            wk2, wv2, vbias_cross, obias_self, gain_cross, shift_cross, wq2, qbias_cross, output_cross = near[9:18]
            out_grad, obias_cross, gain_feed, shift_feed, expand_weight, expand_bias, contract_weight, contract_bias = near[18:]
        else:
            operands = (lengths, hidden, gain_self, shift_self, wq1, qbias_self, wk1, wv1, vbias_self, output_self)
            out = order.run(bind(self_forward, i), 4, operands, self_outs, (aug,))
        self_out.append(out)
        self_sum.append(mp_sum(*out[5:8]))
    for i in span:
        self_sum[i].add()
        cross_kv.append(keys(i))

    cross_out, cross_sum = [], []
    for i in span:
        self_sum[i].meet()
        out = order.run(
            bind(cross_forward, i, wide), 6,
            (hidden, *self_sum[i].pieces, obias_self, gain_cross, shift_cross, wq2, qbias_cross, output_cross, *cross_kv[i]),
            (state, low_state, low_rows, low_rows, lse_out, *half_outs), (whole, aug),
        )
        cross_out.append(out)
        cross_sum.append(mp_sum(*out[5:8]))
        cross_sum[i].add()

    feed_out, feed_sum = [], []
    for i in span:
        cross_sum[i].meet()
        out = order.run(
            bind(feed, i), 4,
            (lengths, tasks, cross_out[i][0], *cross_sum[i].pieces, out_grad, obias_cross, gain_feed, shift_feed, expand_weight, expand_bias, contract_weight),
            (state, low_state, unit_state, unit_state, low_state, vec_out, *half_outs), (whole,),
        )
        feed_out.append(out)
        feed_sum.append(mp_sum(*out[6:9]))
        feed_sum[i].add()
    back_out, back_sum = [], []
    for i in span:
        _, _, q2, o2, lse2 = cross_out[i][:5]
        if i == 0:
            outs, scratch = pack_outs(width + units + 64)
            operands = [out[k] for k in (1, 3, 2, 4, 5) for out in feed_out]
            feed_dp = DpSum(order, n_dp, X_FIRST, *order.run(bind(feed_weights, items), 2, operands, outs, scratch))
        feed_sum[i].meet()
        out = order.run(
            bind(cross_backward, i, chunk), 9,
            (lengths, tasks, feed_out[i][0], *feed_sum[i].pieces, out_grad, gain_feed, output_cross, wq2, *cross_kv[i], q2, o2, lse2),
            (state, low_state, low_rows, mem_rows, mem_rows, vec_out, *half_outs), (whole, aug, aug, row_scratch),
        )
        back_out.append(out)
        back_sum.append(mp_sum(*out[6:9]))
        back_sum[i].add()

    self_back = []
    outs, scratch = pack_outs(4 * rows + 64)
    for i in span:
        q1, ka1, va1, o1, lse1 = self_out[i][:5]
        back_sum[i].meet()
        if i == 0:
            feed_dp.step()
        out = order.run(
            bind(self_backward, i), 5,
            (cross_out[i][0], *back_sum[i].pieces, back_out[i][0], hidden, gain_cross, output_self, wq1, wk1, wv1, ka1, va1, q1, o1, lse1),
            (state, low_state, near_shape((3 * rows, length)), vec_out, *pair_outs), (whole, aug, aug, row_scratch),
        )
        self_back.append(out)
        if i == 0:
            operands = [encoder] + [out[2] for out in back_out] + [out[1] for out in cross_out] + [out[3] for out in cross_out]
            operands += [out[1] for out in back_out] + [out[3] for out in back_out] + [out[4] for out in back_out]
            operands += [out[5] for out in back_out]
            made = order.run(
                bind(cross_weights, items), 3, operands, outs, scratch,
                {0: pl.BlockSpec(encoder.shape, lambda *_: (0, 0, 0))},
            )
            cross_dp = DpSum(order, n_dp, X_FIRST, *made)
    operands = [hidden, gain_self, shift_self] + [out[2] for out in self_back] + [out[3] for out in self_out]
    operands += [out[1] for out in self_back]
    grad_shape, block_shape = shape(hidden.shape, F32), shape(hidden.shape, BF16)
    mem_half, memory_out = near_shape((2, rows, memory_len)), near_shape((items, rows, memory_len))
    line_out, bias_out, matrix = shape((width,), F32), shape((rows,), F32), shape((rows, width), F32)
    lines = (line_out, line_out, line_out, bias_out, bias_out)
    whole_cube = [pl.BlockSpec(hidden.shape, lambda *_: (0, 0, 0))]
    got = {}

    def rows_self():
        vec = order.run(sum_rows, 0.3, [out[3] for out in self_back], (vec_out,))[0]
        got["V"] = [vec] + [swap(vec, "mp", n_mp, bit) for bit in (1, 2, 3)]

    def pack_self():
        made = order.run(bind(self_weights, items), 3, operands + got["V"], outs, scratch)
        got["S"] = DpSum(order, n_dp, X_FIRST, *made)

    def last_finish():
        got["hidden"] = order.run(
            bind(finish_grad, items), 4, [out[0] for out in self_back] + list(got["last"].pieces) + [hidden, gain_self],
            (grad_shape,), (whole,), None, whole_cube,
        )[0]

    def memory(i):
        part = order.run(memory_grad, 2, (wk2, wv2, back_out[i][3], back_out[i][4]), (mem_half, mem_half))
        got["m", i] = part

    def memory_swap():
        for i in span:
            keep, send = got["m", i]
            got["m", i] = keep, swap(order.later(send), "mp", n_mp, 1)

    def memory_finish():
        got["encoder"] = order.run(
            finish_memory, 2, got["far"], (shape((items, rows, memory_len), F32),), (), None,
            [pl.BlockSpec((items, rows, memory_len), lambda *_: (0, 0, 0))],
        )[0].transpose(0, 2, 1)

    def block_part(i):
        keep, send = order.run(feed_out_part, 1, (feed_out[i][2], contract_weight), pair_outs)
        got["b", i] = keep, send

    def block_finish():
        got["out"] = order.run(
            bind(finish_out, items), 3, [out[0] for out in feed_out] + list(got["block"].pieces) + [contract_bias],
            (block_shape,), (whole,), None, whole_cube,
        )[0]

    def unpack_feed():
        got["f"] = feed_dp.unpack(
            (shape((width, width), F32), shape((units, width), F32)), (line_out, shape((units,), F32))
        )

    def unpack_cross():
        got["x"] = cross_dp.unpack((matrix,) * 4, lines)

    def unpack_self():
        got["s"] = got["S"].unpack((matrix,) * 4, lines + (line_out, line_out))

    def job(which):
        if which in "FXS":
            return {"F": feed_dp, "X": cross_dp, "S": got.get("S")}[which].job()
        if which == "l":
            got["last"] = PairSum(order, n_mp, [out[4] for out in self_back], [order.later(out[5]) for out in self_back])
            return got["last"].job()
        if which == "b":
            return got["block"].job()
        if which == "m":
            return got["last"].meet_job()
        if which == "c":
            return got["block"].meet_job()
        parts = [got["m", i] for i in span]

        def then(kept, sent):
            got["far"] = kept, swap(sent, "mp", n_mp, 2)

        return bind(add_memory, items), [p[0] for p in parts] + [p[1] for p in parts], (memory_out, memory_out), then

    def block_swap():
        sends = [order.later(got["b", i][1]) for i in span]
        got["block"] = PairSum(order, n_mp, [got["b", i][0] for i in span], sends)

    acts = dict(
        M=memory_swap, N=block_swap, P=pack_self, V=rows_self, g=last_finish, A=lambda: [memory(i) for i in span], e=memory_finish,
        B=lambda: [block_part(i) for i in span], o=block_finish, u=unpack_feed, v=unpack_cross, w=unpack_self,
    )
    for word in ORDER:
        if word[0] in acts:
            for act in word:
                acts[act]()
        else:
            run_together(order, [job(which) for which in word])
    cross_grads, self_grads, feed_grads = got["x"], got["s"], got["f"]
    hidden_grad, encoder_grad, block_out = got["hidden"], got["encoder"], got["out"]
    return (
        block_out,
        hidden_grad,
        encoder_grad,
        self_grads[9],
        self_grads[10],
        self_grads[0].T,
        self_grads[7],
        self_grads[1].T,
        self_grads[2].T,
        self_grads[8],
        self_grads[3],
        self_grads[6],
        self_grads[4],
        self_grads[5],
        cross_grads[0].T,
        cross_grads[7],
        cross_grads[1].T,
        cross_grads[2].T,
        cross_grads[8],
        cross_grads[3],
        cross_grads[6],
        cross_grads[4],
        cross_grads[5],
        feed_grads[0],
        feed_grads[3],
        feed_grads[1],
        feed_grads[2],
    )


def solution(mesh):
    column, row, flat = P(None, "mp"), P("mp", None), P("mp")
    cube = P("dp", None, None)
    attention = (P(), P(), column, flat, column, column, flat, row, P())
    grads = (P(), P(), column, flat, column, column, flat, row, P())
    return jax.shard_map(
        functools.partial(shards, dict(mesh.shape)),
        mesh=mesh,
        in_specs=(cube, cube, P("dp"), P("dp"), P("dp"), cube)
        + attention
        + attention
        + (P(), P(), column, flat, row, P()),
        out_specs=(cube, cube, P("dp", None, "mp")) + grads + grads + (P(), P(), column, flat, row, P()),
        check_vma=False,
    )
```
